32 devices in a mesh: seq: 8 (over y, x, core), ctx: 4 (over z).
Axes of the slice: x: 2, y: 2, z: 4, core: 2. Of those that a mesh axis runs over, the one named last changes fastest.
Arguments:
- tokens: bfloat16 [4096, 4096], P(('seq', 'ctx')), may hold values from -30 to 30
- modality: int32 [4096], P(('seq', 'ctx')), may hold values from 0 to 1, as said below
- keep_mask: int32 [4096], P(('seq', 'ctx')), may hold values from 0 to 1, as said below
- positions: int32 [4096], P(('seq', 'ctx')), may hold values from 0 to 4095
- modal_table: float32 [2, 4096], replicated, may hold values from -3 to 3
- norm_gain: float32 [4096], replicated, may hold values from 0.1 to 1.9
- norm_bias: float32 [4096], replicated, may hold values from -3 to 3
- qkv_weight: bfloat16 [3, 4096, 4096], P(None, None, 'seq'), may hold values from -1 to 1
- out_weight: bfloat16 [4096, 4096], P('seq'), may hold values from -0.09375 to 0.09375
- mask_token: float32 [4096], replicated, may hold values from -4 to 4
Outputs:
- encoded: float32 [4096, 4096], P(('seq', 'ctx'))
The draws below stay inside these ranges and needn't reach their ends.
Inputs may be any that keep to these rules, and one draw needn't show every extreme that they name: `modality`: 0 marks a video token and 1 a taxel token; ids come in aligned runs of 16 tokens; five eighths of the tokens are video, and all tokens of at least one device are taxel. `keep_mask`: exactly 256 video tokens and 768 taxel tokens are kept, 1024 in all; on at least one device every token is kept.
All inputs are finite; a program needn't handle non-finite values.
Results may differ from the reference program's by a relative error of at most 0.0075.
Values may be sent and summed in bfloat16 or wider, within the bound.
A program may use at most 64 MiB of HBM per device.

```python
import math
import jax
import jax.numpy as jnp
from jax import lax

HEADS = 32
HEAD_DIM = 128
D = 4096
TOK_DEV = 128
TOKENS = 4096
VISIBLE = 1024


def clip_layout(key):
    base_key = jax.random.fold_in(key, 5)
    key_dense, key_blocks, key_keep = jax.random.split(base_key, 3)
    blocks = TOKENS // 16
    per_shard = TOK_DEV // 16
    dense = jax.random.randint(key_dense, (), 0, TOKENS // TOK_DEV)
    block_index = jnp.arange(blocks, dtype=jnp.int32)
    in_dense = block_index // per_shard == dense
    order = jax.random.permutation(key_blocks, blocks).astype(jnp.int32)
    block_score = jnp.where(in_dense, -1 - block_index, order)
    block_rank = jnp.argsort(jnp.argsort(-block_score))
    video_block = block_rank < 5 * blocks // 8
    modality = jnp.repeat(jnp.where(video_block, 0, 1).astype(jnp.int32), 16)
    token_index = jnp.arange(TOKENS, dtype=jnp.int32)
    token_order = jax.random.permutation(key_keep, TOKENS).astype(jnp.int32)
    dense_token = token_index // TOK_DEV == dense
    token_score = jnp.where(dense_token, -1 - token_index, token_order)
    composite = modality * (2 * TOKENS) + token_score
    token_rank = jnp.argsort(jnp.argsort(composite))
    video_total = 5 * TOKENS // 8
    chosen = (token_rank < TOKENS // 16) | (token_rank >= video_total) & (token_rank < video_total + 3 * TOKENS // 16)
    return (modality, chosen.astype(jnp.int32))


def draw_modality(key, part):
    return clip_layout(key)[0]


def draw_keep_mask(key, part):
    return clip_layout(key)[1]


def draw_tokens(key, part):
    key_base, key_rows, key_cols = jax.random.split(jax.random.fold_in(key, 11), 3)
    row_scale = jnp.exp(jax.random.uniform(key_rows, (TOKENS, 1), jnp.float32, math.log(0.25), math.log(2.5)))
    col_scale = jnp.exp(jax.random.uniform(key_cols, (1, D), jnp.float32, math.log(0.3), math.log(3.0)))
    values = jnp.clip(jax.random.normal(key_base, (TOKENS, D), jnp.float32), -4.0, 4.0) * row_scale * col_scale
    return values.astype(jnp.bfloat16)


def draw_qkv_weight(key, part):
    key_base = jax.random.fold_in(jax.random.fold_in(key, 23), 0)
    lift = jnp.array([1.3, 1.3, 1.0], jnp.float32).reshape(3, 1, 1)
    values = jnp.clip(jax.random.normal(key_base, (3, D, D), jnp.float32), -4.0, 4.0) * D ** (-0.5) * lift
    return values.astype(jnp.bfloat16)


def with_ends(entries, rng, least, top_value):
    extent = entries.shape
    index_at = [jax.random.randint(jax.random.fold_in(rng, axis), (), 0, extent[axis]) for axis in range(len(extent))]
    entries = entries.at[tuple(index_at)].set(least)
    longest = extent.index(max(extent))
    index_at[longest] = (index_at[longest] + 1) % extent[longest]
    return entries.at[tuple(index_at)].set(top_value)


def level_of(key, shape, cuts, least, largest):
    level, own = 1.0, jax.random.fold_in(key, 6)
    for axis_at, blocks in cuts:
        heights = jnp.exp(jax.random.uniform(jax.random.fold_in(own, axis_at), (blocks,), jnp.float32, least / len(cuts), largest / len(cuts)))
        level = level * jnp.repeat(heights, shape[axis_at] // blocks).reshape([-1 if axis == axis_at else 1 for axis in range(len(shape))])
    return level


def normal_values(rng, dims, scale, most, cuts=(), held_as=jnp.bfloat16):
    factor_of = level_of(rng, dims, cuts, -0.22, 0.18) if cuts else 1.0
    result = jax.random.normal(rng, dims, jnp.float32) * scale * factor_of
    return jnp.minimum(jnp.maximum(result, -most), most).astype(held_as)


def setup_inputs(seed: int = 0) -> dict:
    seeds = jax.random.split(jax.random.key(seed), 11)
    tokens = draw_tokens(jax.random.fold_in(seeds[10], 71), 0)
    modality = draw_modality(jax.random.fold_in(seeds[10], 71), 0)
    keep_mask = draw_keep_mask(jax.random.fold_in(seeds[10], 71), 0)
    positions = with_ends(jax.random.randint(seeds[3], (TOKENS,), 0, TOKENS), jax.random.fold_in(seeds[3], 1), 0, TOKENS - 1).astype(jnp.int32)
    modal_table = normal_values(seeds[4], (2, D), 0.5, 3.0, (), jnp.float32)
    norm_gain = jnp.clip(1.0 + 0.18 * jax.random.normal(seeds[5], (D,), jnp.float32), 0.1, 1.9)
    norm_bias = normal_values(seeds[6], (D,), 0.5, 3.0, (), jnp.float32)
    qkv_weight = draw_qkv_weight(jax.random.fold_in(seeds[10], 71), 0)
    out_weight = normal_values(seeds[8], (D, D), D ** -0.5, 0.09375, ((0, 8),))
    mask_token = normal_values(seeds[9], (D,), 1.0, 4.0, (), jnp.float32)
    return {"tokens": tokens, "modality": modality, "keep_mask": keep_mask, "positions": positions, "modal_table": modal_table, "norm_gain": norm_gain, "norm_bias": norm_bias, "qkv_weight": qkv_weight, "out_weight": out_weight, "mask_token": mask_token}


EPSILON = 1e-06

def position_table(positions, feature_width):
    half_width = feature_width // 2
    frequency = jnp.exp(-math.log(10000.0) * jnp.arange(half_width, dtype=jnp.float32) / half_width)
    angles = positions.astype(jnp.float32)[:, None] * frequency[None, :]
    return jnp.concatenate([jnp.sin(angles), jnp.cos(angles)], axis=1)

def embed(tokens, modality, positions, modal_table):
    table_rows = jnp.where(modality[:, None] == 1, modal_table[1][None, :], modal_table[0][None, :])
    summed = tokens.astype(jnp.float32) + position_table(positions, tokens.shape[1]) + table_rows
    return summed.astype(jnp.bfloat16)

def layer_norm(embedded, norm_gain, norm_bias):
    values = embedded.astype(jnp.float32)
    row_mean = lax.optimization_barrier(jnp.mean(values, axis=1, keepdims=True))
    centered = values - row_mean
    row_var = lax.optimization_barrier(jnp.mean(centered * centered, axis=1, keepdims=True))
    return (centered * lax.rsqrt(row_var + EPSILON) * norm_gain + norm_bias).astype(jnp.bfloat16)

def reference(tokens, modality, keep_mask, positions, modal_table, norm_gain, norm_bias, qkv_weight, out_weight, mask_token):
    embedded = embed(tokens, modality, positions, modal_table)
    visible = jnp.nonzero(keep_mask == 1, size=VISIBLE, fill_value=0)[0].astype(jnp.int32)
    balanced = embedded[visible]
    normed = layer_norm(balanced, norm_gain, norm_bias)
    triple = jnp.einsum('rd,tdc->trc', normed.astype(jnp.float32), qkv_weight.astype(jnp.float32), precision=lax.Precision.HIGHEST).astype(jnp.bfloat16)
    queries = triple[0].reshape(VISIBLE, HEADS, HEAD_DIM).transpose(1, 0, 2)
    key_rows = triple[1].reshape(VISIBLE, HEADS, HEAD_DIM).transpose(1, 0, 2)
    values = triple[2].reshape(VISIBLE, HEADS, HEAD_DIM).transpose(1, 0, 2)
    score_scale = 1.0 / math.sqrt(HEAD_DIM)

    def one_head(parts):
        query_head, key_head, value_head = parts
        scores = jnp.dot(query_head, key_head.T, preferred_element_type=jnp.float32) * score_scale
        row_top = lax.optimization_barrier(jnp.max(scores, axis=1, keepdims=True))
        expanded = jnp.exp(scores - row_top)
        denominator = lax.optimization_barrier(jnp.sum(expanded, axis=1, keepdims=True))
        weights = expanded.astype(jnp.bfloat16)
        summed = jnp.dot(weights, value_head, preferred_element_type=jnp.float32)
        return (summed / denominator).astype(jnp.bfloat16)
    attended = lax.map(one_head, (queries, key_rows, values))
    attended = attended.transpose(1, 0, 2).reshape(VISIBLE, D)
    projected = jnp.dot(attended, out_weight, preferred_element_type=jnp.float32)
    finished = balanced.astype(jnp.float32) + projected
    filler = jnp.broadcast_to(mask_token[None, :], (TOKENS, D)).astype(jnp.float32)
    return filler.at[visible].set(finished)
```

```python
import math

import jax
import jax.numpy as jnp
from jax import lax
from jax.experimental import pallas as pl
from jax.experimental.pallas import tpu as pltpu
from jax.sharding import PartitionSpec as P

HEAD_DIM = 128


EPSILON = 1e-06
MESH = pl.DeviceIdType.MESH


def position_table(positions, feature_width):
    half_width = feature_width // 2
    frequency = jnp.exp(-math.log(10000.0) * jnp.arange(half_width, dtype=jnp.float32) / half_width)
    angles = positions.astype(jnp.float32)[:, None] * frequency[None, :]
    return jnp.concatenate([jnp.sin(angles), jnp.cos(angles)], axis=1)


def embed(tokens, modality, positions, modal_table):
    table_rows = jnp.where(modality[:, None] == 1, modal_table[1][None, :], modal_table[0][None, :])
    summed = tokens.astype(jnp.float32) + position_table(positions, tokens.shape[1]) + table_rows
    return summed.astype(jnp.bfloat16)


def layer_norm(embedded, norm_gain, norm_bias):
    values = embedded.astype(jnp.float32)
    row_mean = jnp.mean(values, axis=1, keepdims=True)
    centered = values - row_mean
    row_var = jnp.mean(centered * centered, axis=1, keepdims=True)
    return (centered * lax.rsqrt(row_var + EPSILON) * norm_gain + norm_bias).astype(jnp.bfloat16)


def everyone():
    seq_count, ctx_count = lax.axis_size("seq"), lax.axis_size("ctx")

    def place():
        return lax.axis_index("seq") * ctx_count + lax.axis_index("ctx")

    return seq_count * ctx_count, place, lambda j: {"seq": j // ctx_count, "ctx": lax.rem(j, ctx_count)}


def along(axis):
    return lax.axis_size(axis), lambda: lax.axis_index(axis), lambda j: {axis: j}


def exchange(x, group, source, target, out_shape, collective_id):
    count, place, device_of = group

    def kernel(x_ref, out_ref, send_sem, recv_sem, own_sem):
        me = place()
        barrier = pltpu.get_barrier_semaphore()

        def greet(step, carry):
            peer = lax.rem(me + step, count)
            pl.semaphore_signal(barrier, inc=1, device_id=device_of(peer), device_id_type=MESH)
            return carry

        def push(step):
            peer = lax.rem(me + step, count)
            return pltpu.make_async_remote_copy(
                src_ref=source(x_ref, peer),
                dst_ref=target(out_ref, me),
                send_sem=send_sem.at[step],
                recv_sem=recv_sem.at[step],
                device_id=device_of(peer),
                device_id_type=MESH,
            )

        def start(step, carry):
            push(step).start()
            return carry

        def finish(step, carry):
            push(step).wait()
            return carry

        lax.fori_loop(1, count, greet, 0)
        own = pltpu.make_async_copy(source(x_ref, me), target(out_ref, me), own_sem)
        own.start()
        pl.semaphore_wait(barrier, count - 1)
        lax.fori_loop(1, count, start, 0)
        lax.fori_loop(1, count, finish, 0)
        own.wait()

    return pl.pallas_call(
        kernel,
        out_shape=jax.ShapeDtypeStruct(out_shape, x.dtype),
        in_specs=[pl.BlockSpec(memory_space=pltpu.VMEM)],
        out_specs=pl.BlockSpec(memory_space=pltpu.VMEM),
        scratch_shapes=[
            pltpu.SemaphoreType.DMA((count,)),
            pltpu.SemaphoreType.DMA((count,)),
            pltpu.SemaphoreType.DMA,
        ],
        compiler_params=pltpu.CompilerParams(collective_id=collective_id, has_side_effects=True),
    )(x)


CHUNKS = 4


def remote(src, dst, sems, at, device):
    send_sem, recv_sem = sems
    return pltpu.make_async_remote_copy(
        src_ref=src,
        dst_ref=dst,
        send_sem=send_sem.at[at],
        recv_sem=recv_sem.at[at],
        device_id=device,
        device_id_type=MESH,
    )


def aligned(start, size):
    return pl.ds(pl.multiple_of(start * size, size), size)


def greet_line_and_plane(seq_count, ctx_count):
    me, level = lax.axis_index("seq"), lax.axis_index("ctx")
    barrier = pltpu.get_barrier_semaphore()
    for step in range(1, seq_count):
        peer = {"seq": lax.rem(me + step, seq_count)}
        pl.semaphore_signal(barrier, inc=1, device_id=peer, device_id_type=MESH)
    for step in range(1, ctx_count):
        peer = {"ctx": lax.rem(level + step, ctx_count)}
        pl.semaphore_signal(barrier, inc=1, device_id=peer, device_id_type=MESH)
    pl.semaphore_wait(barrier, seq_count + ctx_count - 2)


def regrouping(capacity, outer, inner, slot_count):
    row = lax.broadcasted_iota(jnp.int32, (capacity, capacity), 0)
    column = lax.broadcasted_iota(jnp.int32, (capacity, capacity), 1)
    first = row // (inner * slot_count)
    second = row // slot_count % inner
    wanted = (second * outer + first) * slot_count + row % slot_count
    return (column == wanted).astype(jnp.bfloat16)


def moved(choice, rows):
    return jnp.dot(choice, rows, preferred_element_type=jnp.float32).astype(jnp.bfloat16)


def spread_rows(outgoing, choice, qkv_weight, slot_count, collective_id):
    capacity, width = outgoing.shape
    rows = choice.shape[0]
    half = rows // 2
    seq_count, ctx_count = lax.axis_size("seq"), lax.axis_size("ctx")
    line_rows, plane_rows = capacity // ctx_count, capacity // seq_count
    part_width = width // CHUNKS

    kinds, _, local_width = qkv_weight.shape

    def kernel(
        x_ref, choice_ref, w_hbm, triple_ref, mid, ordered, arrived, out_ref, w_ref, total,
        zs, zr, ps, pr, gs, gr, own_sem, own_sems, w_sems,
    ):
        me, level = lax.axis_index("seq"), lax.axis_index("ctx")
        sibling, left, down = flip(me, 1), flip(me, 2), flip(me, 4)
        across = flip(left, 4)
        all_rows, first, second = pl.ds(0, rows), pl.ds(0, half), pl.ds(half, half)
        along_line, over_plane, gathering = (zs, zr), (ps, pr), (gs, gr)

        def cols(k):
            return pl.ds(k * part_width, part_width)

        def line(k, step):
            peer = lax.rem(level + step, ctx_count)
            src = x_ref.at[aligned(peer, line_rows), cols(k)]
            dst = mid.at[aligned(level, line_rows), cols(k)]
            return remote(src, dst, along_line, (k, step), {"ctx": peer})

        def plane(k, step):
            peer = lax.rem(me + step, seq_count)
            src = ordered.at[aligned(peer, plane_rows), cols(k)]
            dst = arrived.at[aligned(me, plane_rows), cols(k)]
            return remote(src, dst, over_plane, (k, step), {"seq": peer})

        def plane_own(k):
            here = aligned(me, plane_rows)
            return pltpu.make_async_copy(ordered.at[here, cols(k)], arrived.at[here, cols(k)], own_sems.at[k])

        moves = (
            (me, all_rows, sibling),
            (me, all_rows, left),
            (me, all_rows, down),
            (left, first, down),
            (down, second, left),
            (left, all_rows, sibling),
            (down, all_rows, sibling),
            (across, first, sibling),
            (across, second, sibling),
        )

        def hand(k, at):
            origin, which, place = moves[at]
            ref = out_ref.at[origin, which, cols(k)]
            return remote(ref, ref, gathering, (k, at), {"seq": place})

        def fetch(k):
            return pltpu.make_async_copy(w_hbm.at[:, cols(k), :], w_ref.at[:, cols(k), :], w_sems.at[k])

        greet_line_and_plane(seq_count, ctx_count)
        for k in range(CHUNKS):
            for step in range(1, ctx_count):
                line(k, step).start()
        for k in range(CHUNKS):
            fetch(k).start()
        here = aligned(level, line_rows)
        own = pltpu.make_async_copy(x_ref.at[here], mid.at[here], own_sem)
        own.start()
        regroup = regrouping(capacity, seq_count, ctx_count, slot_count)
        own.wait()
        for turn in range(CHUNKS + 4):
            k = turn - 4
            if 0 <= k < CHUNKS:
                for at in (0, 5, 6, 7, 8):
                    hand(k, at).wait_recv()
                fetch(k).wait()
                gathered = out_ref[:, :, cols(k)].reshape(seq_count * rows, part_width)
                for kind in range(kinds):
                    term = jnp.dot(gathered, w_ref[kind, cols(k), :], preferred_element_type=jnp.float32)
                    if k == 0:
                        total[kind] = term
                    elif k < CHUNKS - 1:
                        total[kind] += term
                    else:
                        triple_ref[kind] = (total[kind] + term).astype(jnp.bfloat16)
            k = turn - 3
            if 0 <= k < CHUNKS:
                hand(k, 3).wait_recv()
                hand(k, 7).start()
                hand(k, 4).wait_recv()
                hand(k, 8).start()
            k = turn - 2
            if 0 <= k < CHUNKS:
                hand(k, 1).wait_recv()
                hand(k, 3).start()
                hand(k, 5).start()
                hand(k, 2).wait_recv()
                hand(k, 4).start()
                hand(k, 6).start()
            k = turn - 1
            if 0 <= k < CHUNKS:
                for step in range(1, seq_count):
                    plane(k, step).wait_recv()
                plane_own(k).wait()
                out_ref[me, :, cols(k)] = moved(choice_ref[...], arrived[:, cols(k)])
                for at in (1, 2, 0):
                    hand(k, at).start()
            k = turn
            if k < CHUNKS:
                for step in range(1, ctx_count):
                    line(k, step).wait_recv()
                ordered[:, cols(k)] = moved(regroup, mid[:, cols(k)])
                for step in range(1, seq_count):
                    plane(k, step).start()
                plane_own(k).start()
        for k in range(CHUNKS):
            for at in range(9):
                hand(k, at).wait_send()
            for step in range(1, seq_count):
                plane(k, step).wait_send()
            for step in range(1, ctx_count):
                line(k, step).wait_send()

    dma = pltpu.SemaphoreType.DMA
    return pl.pallas_call(
        kernel,
        out_shape=jax.ShapeDtypeStruct((kinds, seq_count * rows, local_width), jnp.bfloat16),
        in_specs=[pl.BlockSpec(memory_space=pltpu.VMEM)] * 2 + [pl.BlockSpec(memory_space=pl.ANY)],
        out_specs=pl.BlockSpec(memory_space=pltpu.VMEM),
        scratch_shapes=[pltpu.VMEM((capacity, width), jnp.bfloat16)] * 3
        + [
            pltpu.VMEM((seq_count, rows, width), jnp.bfloat16),
            pltpu.VMEM(qkv_weight.shape, jnp.bfloat16),
            pltpu.VMEM((kinds, seq_count * rows, local_width), jnp.float32),
        ]
        + [dma((CHUNKS, ctx_count))] * 2
        + [dma((CHUNKS, seq_count))] * 2
        + [dma((CHUNKS, 9))] * 2
        + [dma, dma((CHUNKS,)), dma((CHUNKS,))],
        compiler_params=pltpu.CompilerParams(collective_id=collective_id, has_side_effects=True),
    )(outgoing, choice, qkv_weight)


def flip(position, bit):
    return position + bit * (1 - 2 * lax.rem(position // bit, 2))


def return_rows(attended, out_weight, choice, slot_count, collective_id):
    width = out_weight.shape[1]
    capacity, rows = choice.shape
    half = rows // 2
    seq_count, ctx_count = lax.axis_size("seq"), lax.axis_size("ctx")
    line_rows, plane_rows = capacity // ctx_count, capacity // seq_count
    part_width = width // CHUNKS

    def kernel(
        x_ref, w_ref, choice_ref, out_ref, shares, near, sums, from_left, from_down, last, passed, total,
        sorted_rows, arrived, ordered, ss, sr, ps, pr, zs, zr, own_sems, line_sems,
    ):
        me, level = lax.axis_index("seq"), lax.axis_index("ctx")
        sibling, left, down = flip(me, 1), flip(me, 2), flip(me, 4)
        first, second = pl.ds(0, half), pl.ds(half, half)
        summing, over_plane, along_line = (ss, sr), (ps, pr), (zs, zr)

        def cols(k):
            return pl.ds(k * part_width, part_width)

        def at(place, which):
            place = flip(place, 2) if which % 2 else place
            return flip(place, 4) if which // 2 else place

        def over(k, q):
            src = shares.at[aligned(at(sibling, q), rows), cols(k)]
            return remote(src, near.at[q, :, cols(k)], summing, (k, q), {"seq": sibling})

        def far(k, which):
            if which == 0:
                return remote(sums.at[3, first, cols(k)], from_left.at[1, :, cols(k)], summing, (k, 4), {"seq": left})
            if which == 1:
                return remote(sums.at[3, second, cols(k)], from_down.at[1, :, cols(k)], summing, (k, 5), {"seq": down})
            if which == 2:
                return remote(sums.at[1, first, cols(k)], from_left.at[0, :, cols(k)], summing, (k, 6), {"seq": left})
            if which == 3:
                return remote(sums.at[2, second, cols(k)], from_down.at[0, :, cols(k)], summing, (k, 7), {"seq": down})
            if which == 4:
                return remote(passed.at[0, :, cols(k)], last.at[0, :, cols(k)], summing, (k, 8), {"seq": down})
            return remote(passed.at[1, :, cols(k)], last.at[1, :, cols(k)], summing, (k, 9), {"seq": left})

        def plane(k, step):
            peer = lax.rem(me + step, seq_count)
            src = sorted_rows.at[aligned(peer, plane_rows), cols(k)]
            dst = arrived.at[aligned(me, plane_rows), cols(k)]
            return remote(src, dst, over_plane, (k, step), {"seq": peer})

        def plane_own(k):
            here = aligned(me, plane_rows)
            return pltpu.make_async_copy(sorted_rows.at[here, cols(k)], arrived.at[here, cols(k)], own_sems.at[k])

        def line(k, step):
            peer = lax.rem(level + step, ctx_count)
            src = ordered.at[aligned(peer, line_rows), cols(k)]
            dst = out_ref.at[aligned(level, line_rows), cols(k)]
            return remote(src, dst, along_line, (k, step), {"ctx": peer})

        def line_own(k):
            here = aligned(level, line_rows)
            return pltpu.make_async_copy(ordered.at[here, cols(k)], out_ref.at[here, cols(k)], line_sems.at[k])

        def wide(value):
            return value.astype(jnp.float32)

        def narrow(value):
            return value.astype(jnp.bfloat16)

        greet_line_and_plane(seq_count, ctx_count)
        regroup = regrouping(capacity, ctx_count, seq_count, slot_count)
        order = (3, 1, 2, 0)
        for turn in range(CHUNKS + 4):
            k = turn - 4
            if 0 <= k < CHUNKS:
                for step in range(1, seq_count):
                    plane(k, step).wait_recv()
                plane_own(k).wait()
                ordered[:, cols(k)] = moved(regroup, arrived[:, cols(k)])
                for step in range(1, ctx_count):
                    line(k, step).start()
                line_own(k).start()
            k = turn - 3
            if 0 <= k < CHUNKS:
                c = cols(k)
                far(k, 2).wait_recv()
                far(k, 4).wait_recv()
                total[:half, c] = narrow(wide(sums[0, :half, c]) + wide(from_left[0, :, c]) + wide(last[0, :, c]))
                far(k, 3).wait_recv()
                far(k, 5).wait_recv()
                total[half:, c] = narrow(wide(sums[0, half:, c]) + wide(from_down[0, :, c]) + wide(last[1, :, c]))
                sorted_rows[:, c] = moved(choice_ref[...], total[:, c])
                for step in range(1, seq_count):
                    plane(k, step).start()
                plane_own(k).start()
            k = turn - 2
            if 0 <= k < CHUNKS:
                c = cols(k)
                far(k, 0).wait_recv()
                passed[0, :, c] = narrow(wide(sums[2, :half, c]) + wide(from_left[1, :, c]))
                far(k, 4).start()
                far(k, 1).wait_recv()
                passed[1, :, c] = narrow(wide(sums[1, half:, c]) + wide(from_down[1, :, c]))
                far(k, 5).start()
            k = turn - 1
            if 0 <= k < CHUNKS:
                c = cols(k)
                for q in order:
                    over(k, q).wait_recv()
                    mine = shares[aligned(at(me, q), rows), c]
                    sums[q, :, c] = narrow(wide(mine) + wide(near[q, :, c]))
                    if q == 3:
                        far(k, 0).start()
                        far(k, 1).start()
                    if q == 1:
                        far(k, 2).start()
                    if q == 2:
                        far(k, 3).start()
            k = turn
            if k < CHUNKS:
                shares[:, cols(k)] = moved(x_ref[...], w_ref[:, cols(k)])
                for q in order:
                    over(k, q).start()
        for k in range(CHUNKS):
            for step in range(1, ctx_count):
                line(k, step).wait()
            line_own(k).wait()
            for step in range(1, seq_count):
                plane(k, step).wait_send()
            for q in order:
                over(k, q).wait_send()
            for which in range(6):
                far(k, which).wait_send()

    dma = pltpu.SemaphoreType.DMA
    bf16 = jnp.bfloat16
    return pl.pallas_call(
        kernel,
        out_shape=jax.ShapeDtypeStruct((capacity, width), bf16),
        in_specs=[pl.BlockSpec(memory_space=pltpu.VMEM)] * 3,
        out_specs=pl.BlockSpec(memory_space=pltpu.VMEM),
        scratch_shapes=[pltpu.VMEM((seq_count * rows, width), bf16)]
        + [pltpu.VMEM((4, rows, width), bf16)] * 2
        + [pltpu.VMEM((2, half, width), bf16)] * 4
        + [pltpu.VMEM((rows, width), bf16)]
        + [pltpu.VMEM((capacity, width), bf16)] * 3
        + [dma((CHUNKS, 10))] * 2
        + [dma((CHUNKS, seq_count))] * 2
        + [dma((CHUNKS, ctx_count))] * 2
        + [dma((CHUNKS,))] * 2,
        compiler_params=pltpu.CompilerParams(collective_id=collective_id, has_side_effects=True),
    )(attended, out_weight, choice)


def part(ref, j):
    return ref.at[j]


def whole(ref, j):
    return ref


def attend(triple):
    _, heads, rows, _ = triple.shape
    block = min(rows, 256)
    score_scale = 1.0 / math.sqrt(HEAD_DIM)

    def kernel(q_ref, k_ref, v_ref, out_ref):
        scores = (
            lax.dot_general(
                q_ref[...], k_ref[...], (((1,), (1,)), ((), ())), preferred_element_type=jnp.float32
            )
            * score_scale
        )
        expanded = jnp.exp(scores - jnp.max(scores, axis=1, keepdims=True))
        total = jnp.sum(expanded, axis=1, keepdims=True)
        summed = jnp.dot(expanded.astype(jnp.bfloat16), v_ref[...], preferred_element_type=jnp.float32)
        out_ref[...] = (summed / total).astype(jnp.bfloat16)

    return pl.pallas_call(
        kernel,
        grid=(heads, rows // block),
        out_shape=jax.ShapeDtypeStruct((heads, rows, HEAD_DIM), jnp.bfloat16),
        in_specs=[
            pl.BlockSpec((None, None, block, HEAD_DIM), lambda h, i: (0, h, i, 0)),
            pl.BlockSpec((None, None, rows, HEAD_DIM), lambda h, i: (1, h, 0, 0)),
            pl.BlockSpec((None, None, rows, HEAD_DIM), lambda h, i: (2, h, 0, 0)),
        ],
        out_specs=pl.BlockSpec((None, block, HEAD_DIM), lambda h, i: (h, i, 0)),
    )(triple, triple, triple)


def attend_by_head(triple):
    _, group_rows, local_width = triple.shape
    ctx = along("ctx")
    count = ctx[0]
    width = local_width // count
    heads = width // HEAD_DIM
    gathered = exchange(
        triple,
        ctx,
        lambda ref, j: ref.at[:, :, pl.ds(pl.multiple_of(j * width, HEAD_DIM), width)],
        lambda ref, j: ref.at[:, pl.ds(pl.multiple_of(j * group_rows, group_rows), group_rows), :],
        (3, count * group_rows, width),
        3,
    )
    if heads == 1:
        split = gathered[:, None]
    else:
        split = jnp.transpose(
            gathered.reshape(3, count * group_rows, heads, HEAD_DIM), (0, 2, 1, 3)
        )
    done = attend(split)
    if heads == 1:
        done = done[0]
    else:
        done = jnp.transpose(done, (1, 0, 2)).reshape(count * group_rows, width)
    return exchange(
        done,
        ctx,
        lambda ref, j: ref.at[pl.ds(pl.multiple_of(j * group_rows, group_rows), group_rows), :],
        lambda ref, j: ref.at[:, pl.ds(pl.multiple_of(j * width, HEAD_DIM), width)],
        (group_rows, local_width),
        4,
    )


def attend_by_row(triple):
    queries, key_rows, values = (triple[0], triple[1], triple[2])
    group_rows, local_width = queries.shape
    heads_here = local_width // HEAD_DIM
    score_scale = 1.0 / math.sqrt(HEAD_DIM)
    both = lax.all_gather(jnp.stack([key_rows, values]), "ctx", axis=1, tiled=True)
    length = both.shape[1]
    query_heads = queries.reshape(group_rows, heads_here, HEAD_DIM)
    key_heads = both[0].reshape(length, heads_here, HEAD_DIM)
    value_heads = both[1].reshape(length, heads_here, HEAD_DIM)
    scores = (
        jnp.einsum("ghd,khd->hgk", query_heads, key_heads, preferred_element_type=jnp.float32)
        * score_scale
    )
    expanded = jnp.exp(scores - jnp.max(scores, axis=2, keepdims=True))
    total = jnp.sum(expanded, axis=2, keepdims=True)
    summed = jnp.einsum(
        "hgk,khd->hgd",
        expanded.astype(jnp.bfloat16),
        value_heads,
        preferred_element_type=jnp.float32,
    )
    attended = (summed / total).astype(jnp.bfloat16)
    return jnp.transpose(attended, (1, 0, 2)).reshape(group_rows, local_width)


def general(
    tokens,
    modality,
    keep_mask,
    positions,
    modal_table,
    norm_gain,
    norm_bias,
    qkv_weight,
    out_weight,
    mask_token,
):
    tok_rows, feature_width = tokens.shape
    seq_count = lax.axis_size("seq")
    ctx_count = lax.axis_size("ctx")
    devices = seq_count * ctx_count
    slot_count = (tok_rows + devices - 1) // devices
    capacity = devices * slot_count
    own_rows = tok_rows // 4
    my_index = lax.axis_index("seq") * ctx_count + lax.axis_index("ctx")
    visible = keep_mask == 1
    own_count = jnp.sum(keep_mask)
    counts = exchange(
        jnp.full((1, 128), own_count, jnp.int32), everyone(), whole, part, (devices, 1, 128), 0
    )[:, 0, 0]
    index = jnp.arange(devices, dtype=jnp.int32)
    starts = jnp.sum(jnp.where(index[None, :] < index[:, None], counts[None, :], 0), axis=1)
    my_start = jnp.sum(jnp.where(index < my_index, counts, 0))
    token_index = jnp.arange(tok_rows, dtype=jnp.int32)
    local_rank = (
        jnp.sum(jnp.where(token_index[None, :] <= token_index[:, None], keep_mask[None, :], 0), axis=1) - 1
    )
    global_rank = my_start + local_rank
    owner = global_rank % devices
    piped = seq_count == 8 and slot_count * ctx_count % 16 == 0
    if piped:
        owner = owner % ctx_count * seq_count + owner // ctx_count
    token_slot = jnp.where(visible, owner * slot_count + local_rank // devices, capacity)
    slot_index = jnp.arange(capacity, dtype=jnp.int32)
    slot_of_token = (token_slot[:, None] == slot_index[None, :]).astype(jnp.bfloat16)
    slot_place = slot_index % slot_count
    source_start = jnp.repeat(starts, slot_count)
    source_count = jnp.repeat(counts, slot_count)
    offset = (my_index - source_start) % devices + devices * slot_place
    usable = offset < source_count
    slot_row = jnp.where(usable, (source_start + offset) // devices, own_rows)
    row_of_slot = (
        slot_row[:, None] == jnp.arange(own_rows, dtype=jnp.int32)[None, :]
    ).astype(jnp.bfloat16)

    embedded = embed(tokens, modality, positions, modal_table)

    def pick(choice, rows, side):
        return lax.dot_general(
            choice, rows, (((side,), (0,)), ((), ())), preferred_element_type=jnp.float32
        )

    normed = layer_norm(embedded, norm_gain, norm_bias)
    outgoing = pick(slot_of_token, normed, 0).astype(jnp.bfloat16)
    slots = (devices, slot_count, feature_width)
    if piped:
        triple = spread_rows(outgoing, row_of_slot.T, qkv_weight, slot_count, 1)
    else:
        arriving = exchange(outgoing.reshape(slots), everyone(), part, part, slots, 1)
        own_normed = pick(row_of_slot, arriving.reshape(capacity, feature_width), 0).astype(jnp.bfloat16)
        group = exchange(own_normed, along("seq"), whole, part, (seq_count,) + own_normed.shape, 2)
        triple = jnp.einsum(
            "rd,tdc->trc",
            group.reshape(seq_count * own_rows, feature_width),
            qkv_weight,
            preferred_element_type=jnp.float32,
        ).astype(jnp.bfloat16)
    if triple.shape[2] % (ctx_count * HEAD_DIM) == 0:
        attended = attend_by_head(triple)
    else:
        attended = attend_by_row(triple)
    if piped:
        returned = return_rows(attended, out_weight, row_of_slot, slot_count, 5)
    else:
        shares = jnp.dot(attended, out_weight, preferred_element_type=jnp.float32).astype(jnp.bfloat16)
        shares = shares.reshape(seq_count, own_rows, feature_width)
        shares = exchange(shares, along("seq"), part, part, shares.shape, 5)
        projected = jnp.sum(shares.astype(jnp.float32), axis=0).astype(jnp.bfloat16)
        returning = pick(row_of_slot, projected, 1).astype(jnp.bfloat16)
        returned = exchange(returning.reshape(slots), everyone(), part, part, slots, 6)
        returned = returned.reshape(capacity, feature_width)
    restored = pick(slot_of_token, returned, 1)
    return jnp.where(visible[:, None], embedded.astype(jnp.float32) + restored, mask_token[None, :])


GROUP = 16
GROUPS = 3
BASE = GROUP * GROUPS
SHARED = 32
TAIL = 64
NEGATIVE = -1e30


def bf16(value):
    return value.astype(jnp.bfloat16)


def f32(value):
    return value.astype(jnp.float32)


def sine_and_cosine(angle):
    turns = jnp.floor(angle * (2.0 / math.pi) + 0.5)
    quarter = turns.astype(jnp.int32)
    r = ((angle - turns * 1.5703125) - turns * 4.837512969970703125e-4) - turns * 7.54978995489188216e-8
    square = r * r
    sine = r + r * square * (-1.6666654611e-1 + square * (8.3321608736e-3 - square * 1.9515295891e-4))
    cosine = (
        1.0
        - 0.5 * square
        + square * square * (4.166664568298827e-2 + square * (-1.388731625493765e-3 + square * 2.443315711809948e-5))
    )
    odd = (quarter & 1) == 1
    first = jnp.where(odd, cosine, sine)
    second = jnp.where(odd, sine, cosine)
    first = jnp.where((quarter & 2) == 2, -first, first)
    second = jnp.where(((quarter + 1) & 2) == 2, -second, second)
    return first, second


def as_column(row, size):
    across = lax.broadcasted_iota(jnp.int32, (size, size), 1)
    down = lax.broadcasted_iota(jnp.int32, (size, size), 0)
    return jnp.sum(jnp.where(across == down, row, 0.0), axis=1, keepdims=True)


def ranks_of(keep_row, size):
    across = lax.broadcasted_iota(jnp.int32, (size, size), 1)
    down = lax.broadcasted_iota(jnp.int32, (size, size), 0)
    column = as_column(keep_row, size)
    return jnp.sum(jnp.where(down < across, column, 0.0), axis=0, keepdims=True)


class Layout:
    def __init__(self, counts, place, level, seq_count, ctx_count):
        lanes = counts.shape[1:]
        tail_of = jnp.clip(counts - 2.0 * GROUP, 0.0, 1.0 * GROUP)
        over = jnp.maximum(counts - BASE, 0.0)
        index = lax.broadcasted_iota(jnp.int32, counts.shape, 0)
        self.over_start = jnp.sum(jnp.where(index < place, over, 0.0), axis=0)
        total = jnp.sum(over, axis=0)
        tails, free, starts = [], [], []
        running = jnp.zeros(lanes, jnp.float32)
        fits = jnp.ones(lanes, jnp.float32)
        for z in range(ctx_count):
            tail = jnp.sum(tail_of.reshape((seq_count, ctx_count) + lanes)[:, z], axis=0)
            room = jnp.clip(TAIL - tail, 0.0, 1.0 * SHARED)
            tails.append(tail)
            free.append(room)
            starts.append(running)
            running = running + room
            fits = jnp.where(tail > TAIL, 0.0, fits)
        self.fits = jnp.where(total > running, 0.0, fits)
        self.tails, self.free, self.starts = tails, free, starts
        self.used = [jnp.clip(total - starts[z], 0.0, free[z]) for z in range(ctx_count)]
        by_plane = counts.reshape((seq_count, ctx_count) + lanes)
        seat = lax.broadcasted_iota(jnp.int32, by_plane.shape, 0)
        lane = lax.broadcasted_iota(jnp.int32, by_plane.shape, 3)
        self.lane_counts = jnp.sum(jnp.where(lane // GROUP == seat, by_plane, 0.0), axis=0)
        tail_by_plane = tail_of.reshape(by_plane.shape)
        self.lane_tail_start = jnp.sum(jnp.where(seat < lane // GROUP, tail_by_plane, 0.0), axis=0)

    def of_level(self, values, level):
        out = values[0]
        for z in range(1, len(values)):
            out = jnp.where(level == z, values[z], out)
        return out

    def shared_slots(self, keep_row, rank_row):
        ordinal = self.over_start[0:1] + rank_row - BASE
        slot = jnp.full(ordinal.shape, -1.0, jnp.float32)
        for z in range(len(self.free)):
            here = (ordinal >= self.starts[z][0:1]) & (ordinal < self.starts[z][0:1] + self.free[z][0:1])
            slot = jnp.where(here, ordinal - self.starts[z][0:1] + SHARED * z, slot)
        return jnp.where((keep_row > 0.0) & (rank_row >= BASE), slot, -1.0)

    def tail_choice(self, level):
        counts = self.of_level([self.lane_counts[z] for z in range(len(self.free))], level)[0:1]
        start = self.of_level([self.lane_tail_start[z] for z in range(len(self.free))], level)[0:1]
        tail = self.of_level(self.tails, level)[0:1]
        used = self.of_level(self.used, level)[0:1]
        size = (TAIL, counts.shape[1])
        target = f32(lax.broadcasted_iota(jnp.int32, size, 0))
        lane = lax.broadcasted_iota(jnp.int32, size, 1)
        within = f32(lane % GROUP)
        valid = counts - 2 * GROUP > within
        grouped = bf16(jnp.where(valid & (start + within == target), 1.0, 0.0))
        where = f32(lane)
        shared = bf16(jnp.where((where < used) & (tail + where == target), 1.0, 0.0))
        return grouped, shared[:, :SHARED]

    def key_bias(self):
        width = self.lane_counts.shape[2]
        within = f32(lax.broadcasted_iota(jnp.int32, (1, width), 1) % GROUP)
        parts = []
        for group in range(GROUPS - 1):
            for z in range(len(self.free)):
                parts.append(jnp.where(self.lane_counts[z][0:1] > within + group * GROUP, 0.0, NEGATIVE))
        slot = f32(lax.broadcasted_iota(jnp.int32, (1, width), 1))
        for z in range(0, len(self.free), 2):
            low = self.tails[z][0:1] + self.used[z][0:1]
            high = self.tails[z + 1][0:1] + self.used[z + 1][0:1]
            limit = jnp.where(slot < TAIL, low, high + TAIL)
            parts.append(jnp.where(slot < limit, 0.0, NEGATIVE))
        return jnp.concatenate(parts, axis=1)


class Plane:
    def __init__(self):
        self.me = lax.axis_index("seq")
        self.level = lax.axis_index("ctx")
        self.sibling, self.left, self.down = flip(self.me, 1), flip(self.me, 2), flip(self.me, 4)
        self.across = flip(self.left, 4)

    def order(self, seat):
        core, x, y = lax.rem(seat, 2), lax.rem(seat // 2, 2), seat // 4
        return core * 4 + y * 2 + x


class Gather:
    def __init__(self, plane, halves, sems, at):
        self.plane, self.halves, self.sems, self.at = plane, halves, sems, at

    def moves(self):
        p = self.plane
        out = []
        for origin, half, place in (
            (p.me, None, p.left),
            (p.me, None, p.down),
            (p.me, None, p.sibling),
            (p.left, 0, p.down),
            (p.down, 1, p.left),
            (p.left, None, p.sibling),
            (p.down, None, p.sibling),
            (p.across, 0, p.sibling),
            (p.across, 1, p.sibling),
        ):
            out.append((self.halves(origin, half), place))
        return out

    def copy(self, move):
        ref, place = self.moves()[move]
        return remote(ref, ref, self.sems, (self.at, move), {"seq": place})

    def begin(self):
        for move in (0, 1, 2):
            self.copy(move).start()

    def forward(self):
        self.copy(0).wait_recv()
        self.copy(3).start()
        self.copy(5).start()
        self.copy(1).wait_recv()
        self.copy(4).start()
        self.copy(6).start()

    def finish(self):
        self.copy(3).wait_recv()
        self.copy(7).start()
        self.copy(4).wait_recv()
        self.copy(8).start()

    def arrive(self):
        for move in (2, 5, 6, 7, 8):
            self.copy(move).wait_recv()

    def drain(self):
        for move in range(9):
            self.copy(move).wait_send()


class BlockSum:
    def __init__(self, plane, source, first, second, third, result, sems):
        self.plane, self.sems = plane, sems
        self.source, self.first, self.second, self.third, self.result = source, first, second, third, result

    def block(self, seat, half):
        return 2 * (lax.rem(seat // 2, 2) + 2 * (seat // 4)) + half

    def copies(self):
        p = self.plane
        core = lax.rem(p.me, 2)
        out = [(self.source.at[pl.ds(8 * (1 - core), 8)], self.first, p.sibling)]
        mine = 8 * core
        out.append((self.source.at[mine + self.block(p.across, 0)], self.second.at[0], p.left))
        out.append((self.source.at[mine + self.block(p.left, 0)], self.second.at[1], p.left))
        out.append((self.source.at[mine + self.block(p.across, 1)], self.second.at[2], p.down))
        out.append((self.source.at[mine + self.block(p.down, 1)], self.second.at[3], p.down))
        out.append((self.source.at[mine + self.block(p.down, 0)], self.third.at[0], p.down))
        out.append((self.source.at[mine + self.block(p.left, 1)], self.third.at[1], p.left))
        return out

    def copy(self, at):
        src, dst, place = self.copies()[at]
        return remote(src, dst, self.sems, (at,), {"seq": place})

    def level_one(self):
        self.copy(0).start()

    def level_two(self):
        core = lax.rem(self.plane.me, 2)
        self.copy(0).wait_recv()
        for block in range(8):
            at = 8 * core + block
            self.source[at] = self.source[at] + self.first[block]
        for at in (1, 2, 3, 4):
            self.copy(at).start()

    def level_three(self):
        p = self.plane
        mine = 8 * lax.rem(p.me, 2)
        self.copy(1).wait_recv()
        at = mine + self.block(p.down, 0)
        self.source[at] = self.source[at] + self.second[0]
        self.copy(5).start()
        self.copy(3).wait_recv()
        at = mine + self.block(p.left, 1)
        self.source[at] = self.source[at] + self.second[2]
        self.copy(6).start()

    def total(self):
        p = self.plane
        mine = 8 * lax.rem(p.me, 2)
        self.copy(2).wait_recv()
        self.copy(5).wait_recv()
        first = self.source[mine + self.block(p.me, 0)]
        self.result[0] = first + self.second[1] + self.third[0]
        self.copy(4).wait_recv()
        self.copy(6).wait_recv()
        second = self.source[mine + self.block(p.me, 1)]
        self.result[1] = second + self.second[3] + self.third[1]

    def drain(self):
        for at in range(7):
            self.copy(at).wait_send()


def counts_of(ref, seq_count, ctx_count):
    return f32(ref[...].reshape((seq_count * ctx_count,) + ref.shape[2:]))


def gather_and_project(tokens, modality, keep, positions, frequency, modal_table, gain, bias, qkv_weight, collective_id):
    seq_count, ctx_count = lax.axis_size("seq"), lax.axis_size("ctx")
    tok_rows, width = tokens.shape
    kinds, _, local_width = qkv_weight.shape
    head_width = local_width // ctx_count
    blocks = 16
    block_width = width // blocks
    plane_rows = seq_count * GROUP
    slots = ctx_count * (2 * plane_rows + TAIL)
    half_width = width // 2

    def kernel(
        tok_ref, mod_ref, keep_ref, pos_ref, freq_ref, table_ref, gain_ref, bias_ref, w_hbm,
        out_ref, emb_ref, cnt_ref, fits_ref,
        w_ref, normed, gathered, spare, shared_in, first, second, third, summed, crossed, shared, staged,
        w_sems, cs, cr, gs, gr, bs, br, xs, xr, ds, dr, own_sems,
    ):
        plane = Plane()
        me, level = plane.me, plane.level

        def fetch(kind):
            return pltpu.make_async_copy(w_hbm.at[kind], w_ref.at[kind], w_sems.at[kind])

        def count_line(step):
            peer = lax.rem(level + step, ctx_count)
            ref = cnt_ref.at[me, level]
            return remote(ref, ref, (cs, cr), (step - 1,), {"ctx": peer})

        def count_plane(step):
            peer = lax.rem(me + step, seq_count)
            ref = cnt_ref.at[me]
            return remote(ref, ref, (cs, cr), (ctx_count - 2 + step,), {"seq": peer})

        def piece(group):
            def halves(origin, half):
                ref = gathered.at[group, origin]
                if half is None:
                    return ref
                return ref.at[:, pl.ds(half * half_width, half_width)]

            return halves

        def shared_piece(origin, half):
            start = 2 * plane.order(origin)
            if half is None:
                return shared.at[pl.ds(start, 2)]
            return shared.at[start + half]

        groups = [Gather(plane, piece(g), (gs, gr), g) for g in range(GROUPS)]
        spread = Gather(plane, shared_piece, (gs, gr), GROUPS)
        sums = BlockSum(plane, shared_in, first, second, third, summed, (bs, br))

        def cross(step):
            peer = lax.rem(level + step, ctx_count)
            src = summed.at[:, aligned(peer, SHARED), :]
            return remote(src, crossed.at[step - 1], (xs, xr), (step - 1,), {"ctx": peer})

        def deal(group, kind, step):
            peer = lax.rem(level + step, ctx_count)
            rows = plane_rows if group < 2 else TAIL
            start = group * ctx_count * plane_rows + level * rows
            dst = out_ref.at[kind, pl.ds(pl.multiple_of(start, GROUP), rows)]
            src = staged.at[group * kinds + kind, peer, pl.ds(0, rows)]
            at = (group * kinds + kind) * (ctx_count - 1) + step - 1
            return remote(src, dst, (ds, dr), (at,), {"ctx": peer})

        def keep_own(group, kind):
            rows = plane_rows if group < 2 else TAIL
            start = group * ctx_count * plane_rows + level * rows
            dst = out_ref.at[kind, pl.ds(pl.multiple_of(start, GROUP), rows)]
            src = staged.at[group * kinds + kind, level, pl.ds(0, rows)]
            return pltpu.make_async_copy(src, dst, own_sems.at[group * kinds + kind])

        keep_row = f32(keep_ref[...])
        own_count = jnp.sum(keep_row, axis=1, keepdims=True).astype(jnp.int32)
        cnt_ref[me, level] = jnp.broadcast_to(own_count, cnt_ref.shape[2:])
        for step in range(1, seq_count):
            peer = {"seq": lax.rem(me + step, seq_count)}
            pl.semaphore_signal(pltpu.get_barrier_semaphore(), inc=1, device_id=peer, device_id_type=MESH)
        for step in range(1, ctx_count):
            peer = {"ctx": lax.rem(level + step, ctx_count)}
            pl.semaphore_signal(pltpu.get_barrier_semaphore(), inc=1, device_id=peer, device_id_type=MESH)
        for kind in range(kinds):
            fetch(kind).start()
        pl.semaphore_wait(pltpu.get_barrier_semaphore(), seq_count + ctx_count - 2)
        for step in range(1, ctx_count):
            count_line(step).start()

        rank_row = ranks_of(keep_row, tok_rows)
        place_column = as_column(f32(pos_ref[...]), tok_rows)
        taxel = as_column(f32(mod_ref[...]), tok_rows) > 0.5

        def embed_block(at, total):
            here = aligned(at, block_width)
            waves = sine_and_cosine(place_column * freq_ref[:, here])
            for side in range(2):
                start = side * half_width + at * block_width
                cols = pl.ds(pl.multiple_of(start, block_width), block_width)
                row = jnp.where(taxel, table_ref[1:2, cols], table_ref[0:1, cols])
                rounded = bf16(f32(tok_ref[:, cols]) + waves[side] + row)
                emb_ref[:, cols] = rounded
                values = f32(rounded)
                for lane in range(0, block_width, 128):
                    total = total + values[:, lane : lane + 128]
            return total

        nothing = jnp.zeros((tok_rows, 128), jnp.float32)
        total = lax.fori_loop(0, blocks // 2, embed_block, nothing)
        mean = jnp.sum(total, axis=1, keepdims=True) * (1.0 / width)
        for step in range(1, ctx_count):
            count_line(step).wait_recv()
        for step in range(1, seq_count):
            count_plane(step).start()

        def var_block(at, total):
            centered = f32(emb_ref[:, aligned(at, block_width)]) - mean
            centered = centered * centered
            for lane in range(0, block_width, 128):
                total = total + centered[:, lane : lane + 128]
            return total

        total = lax.fori_loop(0, blocks, var_block, nothing)
        scale = lax.rsqrt(jnp.sum(total, axis=1, keepdims=True) * (1.0 / width) + EPSILON)

        slot = f32(lax.broadcasted_iota(jnp.int32, (BASE, tok_rows), 0))
        base_choice = bf16(jnp.where((keep_row > 0.0) & (rank_row == slot), 1.0, 0.0))

        def norm_block(at, carry):
            cols = aligned(at, block_width)
            values = (f32(emb_ref[:, cols]) - mean) * scale * gain_ref[:, cols] + bias_ref[:, cols]
            rows = bf16(values)
            normed[:, cols] = rows
            chosen = moved(base_choice, rows)
            for group in range(GROUPS):
                gathered[group, me, :, cols] = chosen[group * GROUP : (group + 1) * GROUP]
            return carry

        lax.fori_loop(0, blocks, norm_block, 0)
        groups[0].begin()
        for step in range(1, seq_count):
            count_plane(step).wait_recv()
        layout = Layout(counts_of(cnt_ref, seq_count, ctx_count), me * ctx_count + level, level, seq_count, ctx_count)
        fits_ref[...] = layout.fits
        slot = f32(lax.broadcasted_iota(jnp.int32, (ctx_count * SHARED, tok_rows), 0))
        shared_choice = bf16(jnp.where(layout.shared_slots(keep_row, rank_row) == slot, 1.0, 0.0))
        for block in range(blocks):
            shared_in[block] = moved(shared_choice, normed[:, block * block_width : (block + 1) * block_width])
        sums.level_one()
        sums.level_two()
        groups[0].forward()
        sums.level_three()
        groups[0].finish()
        groups[1].begin()
        sums.total()
        for step in range(1, ctx_count):
            cross(step).start()
        groups[0].arrive()

        def project(group, kind, extra=None):
            rows = gathered[group].reshape(plane_rows, width)
            return bf16(jnp.dot(rows, w_ref[kind], preferred_element_type=jnp.float32))

        def stage(group, kind, values):
            for peer in range(ctx_count):
                staged[group * kinds + kind, peer, : values.shape[0]] = values[
                    :, peer * head_width : (peer + 1) * head_width
                ]
            for step in (2, 3, 1):
                deal(group, kind, step).start()
            keep_own(group, kind).start()

        fetch(0).wait()
        stage(0, 0, project(0, 0))
        groups[1].forward()
        fetch(1).wait()
        stage(0, 1, project(0, 1))
        for step in range(1, ctx_count):
            cross(step).wait_recv()
        own = summed[:, aligned(level, SHARED), :]
        start = 2 * plane.order(me)
        shared[pl.ds(start, 2)] = own + crossed[0] + crossed[1] + crossed[2]
        groups[1].finish()
        groups[2].begin()
        spread.begin()
        fetch(2).wait()
        stage(0, 2, project(0, 2))
        groups[1].arrive()
        stage(1, 0, project(1, 0))
        groups[2].forward()
        spread.forward()
        stage(1, 1, project(1, 1))
        groups[2].finish()
        spread.finish()
        stage(1, 2, project(1, 2))
        grouped_choice, shared_choice = layout.tail_choice(level)
        groups[2].arrive()
        spread.arrive()
        tail_rows = gathered[2].reshape(plane_rows, width)
        for kind in range(kinds):
            total = jnp.zeros((plane_rows + SHARED, local_width), jnp.float32)
            for block in range(blocks):
                cols = slice(block * block_width, (block + 1) * block_width)
                rows = jnp.concatenate([tail_rows[:, cols], shared[block]], axis=0)
                total = total + jnp.dot(rows, w_ref[kind, cols, :], preferred_element_type=jnp.float32)
            rows = bf16(total)
            packed = jnp.dot(grouped_choice, rows[:plane_rows], preferred_element_type=jnp.float32)
            packed = packed + jnp.dot(shared_choice, rows[plane_rows:], preferred_element_type=jnp.float32)
            stage(2, kind, bf16(packed))
        for group in range(GROUPS):
            for kind in range(kinds):
                keep_own(group, kind).wait()
                for step in range(1, ctx_count):
                    deal(group, kind, step).wait()
        for step in range(1, ctx_count):
            count_line(step).wait_send()
            cross(step).wait_send()
        for step in range(1, seq_count):
            count_plane(step).wait_send()
        for gather in groups + [spread]:
            gather.drain()
        sums.drain()

    dma = pltpu.SemaphoreType.DMA
    b16 = jnp.bfloat16
    deals = GROUPS * kinds * (ctx_count - 1)
    shared_rows = ctx_count * SHARED
    vmem = pl.BlockSpec(memory_space=pltpu.VMEM)
    return pl.pallas_call(
        kernel,
        out_shape=[
            jax.ShapeDtypeStruct((kinds, slots, head_width), b16),
            jax.ShapeDtypeStruct((tok_rows, width), b16),
            jax.ShapeDtypeStruct((seq_count, ctx_count, 8, 128), jnp.int32),
            jax.ShapeDtypeStruct((8, 128), jnp.float32),
        ],
        in_specs=[vmem] * 8 + [pl.BlockSpec(memory_space=pl.ANY)],
        out_specs=[vmem] * 4,
        scratch_shapes=[
            pltpu.VMEM(qkv_weight.shape, b16),
            pltpu.VMEM((tok_rows, width), b16),
            pltpu.VMEM((GROUPS, seq_count, GROUP, width), b16),
            pltpu.VMEM((8, 128), b16),
            pltpu.VMEM((blocks, shared_rows, block_width), b16),
            pltpu.VMEM((8, shared_rows, block_width), b16),
            pltpu.VMEM((4, shared_rows, block_width), b16),
            pltpu.VMEM((2, shared_rows, block_width), b16),
            pltpu.VMEM((2, shared_rows, block_width), b16),
            pltpu.VMEM((ctx_count - 1, 2, SHARED, block_width), b16),
            pltpu.VMEM((blocks, SHARED, block_width), b16),
            pltpu.VMEM((GROUPS * kinds, ctx_count, plane_rows, head_width), b16),
            dma((kinds,)),
        ]
        + [dma((seq_count + ctx_count - 2,))] * 2
        + [dma((GROUPS + 1, 9))] * 2
        + [dma((7,))] * 2
        + [dma((ctx_count - 1,))] * 2
        + [dma((deals,))] * 2
        + [dma((GROUPS * kinds,))],
        compiler_params=pltpu.CompilerParams(
            collective_id=collective_id, has_side_effects=True, vmem_limit_bytes=56 * 2**20
        ),
    )(tokens, modality, keep, positions, frequency, modal_table, gain, bias, qkv_weight)


def attend_and_return(triple, counts, keep, out_weight, collective_id):
    seq_count, ctx_count = lax.axis_size("seq"), lax.axis_size("ctx")
    kinds, slots, head_width = triple.shape
    local_width, width = out_weight.shape
    tok_rows = keep.shape[1]
    blocks = 16
    block_width = width // blocks
    plane_rows = seq_count * GROUP
    half_width = width // 2
    shared_rows = ctx_count * SHARED
    score_scale = 1.0 / math.sqrt(HEAD_DIM)

    def kernel(
        qkv_ref, cnt_ref, keep_ref, w_hbm, out_ref,
        w_ref, attended, inward, shares, near, sums, from_left, from_down, last, passed, returned,
        shared_in, first, second, third, final,
        w_sem, fs, fr, own_sems, ss, sr, bs, br, xs, xr, gs, gr,
    ):
        plane = Plane()
        me, level = plane.me, plane.level
        sibling, left, down = plane.sibling, plane.left, plane.down
        summing = (ss, sr)
        fetch = pltpu.make_async_copy(w_hbm, w_ref, w_sem)
        fetch.start()

        def at(place, which):
            place = flip(place, 2) if which % 2 else place
            return flip(place, 4) if which // 2 else place

        low, high = pl.ds(0, half_width), pl.ds(half_width, half_width)

        def over(g, q):
            return remote(shares.at[g, at(sibling, q)], near.at[g, q], summing, (g, q), {"seq": sibling})

        def far(g, which):
            src, dst, place = (
                (sums.at[g, 3, :, low], from_left.at[g, 1], left),
                (sums.at[g, 3, :, high], from_down.at[g, 1], down),
                (sums.at[g, 1, :, low], from_left.at[g, 0], left),
                (sums.at[g, 2, :, high], from_down.at[g, 0], down),
                (passed.at[g, 0], last.at[g, 0], down),
                (passed.at[g, 1], last.at[g, 1], left),
            )[which]
            return remote(src, dst, summing, (g, 4 + which), {"seq": place})

        def rows_of(group):
            return plane_rows if group < 2 else TAIL

        def slot_start(group, z):
            return pl.multiple_of(group * ctx_count * plane_rows + z * rows_of(group), GROUP)

        def back(group, step):
            peer = lax.rem(level + step, ctx_count)
            src = attended.at[pl.ds(slot_start(group, peer), rows_of(group))]
            dst = inward.at[group, pl.ds(0, rows_of(group)), aligned(level, head_width)]
            return remote(src, dst, (fs, fr), (group * (ctx_count - 1) + step - 1,), {"ctx": peer})

        def back_own(group):
            src = attended.at[pl.ds(slot_start(group, level), rows_of(group))]
            dst = inward.at[group, pl.ds(0, rows_of(group)), aligned(level, head_width)]
            return pltpu.make_async_copy(src, dst, own_sems.at[group])

        def shared_piece(origin, half):
            start = 2 * plane.order(origin)
            if half is None:
                return final.at[pl.ds(start, 2)]
            return final.at[start + half]

        spread = Gather(plane, shared_piece, (gs, gr), 0)
        start = 2 * plane.order(me)

        def result_slot():
            return final.at[pl.ds(start, 2), aligned(level, SHARED), :]

        def cross(step):
            peer = lax.rem(level + step, ctx_count)
            ref = result_slot()
            return remote(ref, ref, (xs, xr), (step - 1,), {"ctx": peer})

        class Result:
            def __setitem__(self, half, value):
                final[start + half, aligned(level, SHARED), :] = value

        block_sum = BlockSum(plane, shared_in, first, second, third, Result(), (bs, br))

        greet_line_and_plane(seq_count, ctx_count)
        layout = Layout(counts_of(cnt_ref, seq_count, ctx_count), me * ctx_count + level, level, seq_count, ctx_count)
        key_bias = layout.key_bias()
        keep_row = f32(keep_ref[...])
        rank_row = ranks_of(keep_row, tok_rows)

        def attend(begin, rows):
            queries = qkv_ref[0, pl.ds(begin, rows)]
            scores = lax.dot_general(
                queries, qkv_ref[1], (((1,), (1,)), ((), ())), preferred_element_type=jnp.float32
            )
            scores = scores * score_scale + key_bias
            expanded = jnp.exp(scores - jnp.max(scores, axis=1, keepdims=True))
            total = jnp.sum(expanded, axis=1, keepdims=True)
            summed = jnp.dot(bf16(expanded), qkv_ref[2], preferred_element_type=jnp.float32)
            attended[pl.ds(begin, rows)] = bf16(summed / total)

        def send_back(group):
            for step in (2, 3, 1):
                back(group, step).start()
            back_own(group).start()

        def collect(group):
            back_own(group).wait()
            for step in range(1, ctx_count):
                back(group, step).wait_recv()

        def begin_sum(g):
            for q in (3, 1, 2, 0):
                over(g, q).start()

        def chip_sum(g):
            for q in (3, 1, 2, 0):
                over(g, q).wait_recv()
                sums[g, q] = bf16(f32(shares[g, at(me, q)]) + f32(near[g, q]))
                if q == 3:
                    far(g, 0).start()
                    far(g, 1).start()
                if q == 1:
                    far(g, 2).start()
                if q == 2:
                    far(g, 3).start()

        def pass_sum(g):
            far(g, 0).wait_recv()
            passed[g, 0] = bf16(f32(sums[g, 2, :, :half_width]) + f32(from_left[g, 1]))
            far(g, 4).start()
            far(g, 1).wait_recv()
            passed[g, 1] = bf16(f32(sums[g, 1, :, half_width:]) + f32(from_down[g, 1]))
            far(g, 5).start()

        def end_sum(g):
            rows = pl.ds(g * GROUP, GROUP)
            far(g, 2).wait_recv()
            far(g, 4).wait_recv()
            returned[rows, :half_width] = bf16(
                f32(sums[g, 0, :, :half_width]) + f32(from_left[g, 0]) + f32(last[g, 0])
            )
            far(g, 3).wait_recv()
            far(g, 5).wait_recv()
            returned[rows, half_width:] = bf16(
                f32(sums[g, 0, :, half_width:]) + f32(from_down[g, 0]) + f32(last[g, 1])
            )

        tail_start = 2 * ctx_count * plane_rows
        attend(tail_start, ctx_count * TAIL)
        send_back(2)
        span = ctx_count * plane_rows // 2
        attend(0, span)
        attend(span, span)
        send_back(0)
        fetch.wait()
        grouped_choice, shared_choice = layout.tail_choice(level)
        collect(2)
        packed = inward[2, :TAIL]
        unpack = (((0,), (0,)), ((), ()))
        grouped = bf16(lax.dot_general(grouped_choice, packed, unpack, preferred_element_type=jnp.float32))
        extra = bf16(lax.dot_general(shared_choice, packed, unpack, preferred_element_type=jnp.float32))
        rows = jnp.concatenate([grouped, extra], axis=0)
        for block in range(blocks):
            cols = slice(block * block_width, (block + 1) * block_width)
            values = bf16(jnp.dot(rows, w_ref[:, cols], preferred_element_type=jnp.float32))
            shares[2, :, :, cols] = values[:plane_rows].reshape(seq_count, GROUP, block_width)
            shared_in[block] = values[plane_rows:]
        block_sum.level_one()
        begin_sum(2)
        block_sum.level_two()
        attend(2 * span, span)
        block_sum.level_three()
        chip_sum(2)
        attend(3 * span, span)
        send_back(1)
        block_sum.total()
        for step in range(1, ctx_count):
            cross(step).start()

        def project(g):
            for block in range(blocks):
                cols = slice(block * block_width, (block + 1) * block_width)
                values = moved(inward[g], w_ref[:, cols])
                shares[g, :, :, cols] = values.reshape(seq_count, GROUP, block_width)

        collect(0)
        project(0)
        begin_sum(0)
        pass_sum(2)
        for step in range(1, ctx_count):
            cross(step).wait_recv()
        spread.begin()
        chip_sum(0)
        collect(1)
        project(1)
        begin_sum(1)
        spread.forward()
        pass_sum(0)
        chip_sum(1)
        end_sum(2)
        spread.finish()
        end_sum(0)
        pass_sum(1)
        spread.arrive()
        slot = f32(lax.broadcasted_iota(jnp.int32, (shared_rows, tok_rows), 0))
        from_shared = bf16(jnp.where(layout.shared_slots(keep_row, rank_row) == slot, 1.0, 0.0))
        slot = f32(lax.broadcasted_iota(jnp.int32, (BASE, tok_rows), 0))
        from_base = bf16(jnp.where((keep_row > 0.0) & (rank_row == slot), 1.0, 0.0))
        end_sum(1)
        for block in range(blocks):
            cols = slice(block * block_width, (block + 1) * block_width)
            placed = lax.dot_general(from_shared, final[block], unpack, preferred_element_type=jnp.float32)
            placed = placed + lax.dot_general(
                from_base, returned[:, cols], unpack, preferred_element_type=jnp.float32
            )
            out_ref[:, cols] = bf16(placed)
        for g in range(GROUPS):
            for q in range(4):
                over(g, q).wait_send()
            for which in range(6):
                far(g, which).wait_send()
            for step in range(1, ctx_count):
                back(g, step).wait_send()
        block_sum.drain()
        spread.drain()
        for step in range(1, ctx_count):
            cross(step).wait_send()

    dma = pltpu.SemaphoreType.DMA
    b16 = jnp.bfloat16
    vmem = pl.BlockSpec(memory_space=pltpu.VMEM)
    return pl.pallas_call(
        kernel,
        out_shape=jax.ShapeDtypeStruct((tok_rows, width), b16),
        in_specs=[vmem] * 3 + [pl.BlockSpec(memory_space=pl.ANY)],
        out_specs=vmem,
        scratch_shapes=[
            pltpu.VMEM(out_weight.shape, b16),
            pltpu.VMEM((slots, head_width), b16),
            pltpu.VMEM((GROUPS, plane_rows, local_width), b16),
            pltpu.VMEM((GROUPS, seq_count, GROUP, width), b16),
            pltpu.VMEM((GROUPS, 4, GROUP, width), b16),
            pltpu.VMEM((GROUPS, 4, GROUP, width), b16),
        ]
        + [pltpu.VMEM((GROUPS, 2, GROUP, half_width), b16)] * 4
        + [
            pltpu.VMEM((BASE, width), b16),
            pltpu.VMEM((blocks, SHARED, block_width), b16),
            pltpu.VMEM((8, SHARED, block_width), b16),
            pltpu.VMEM((4, SHARED, block_width), b16),
            pltpu.VMEM((2, SHARED, block_width), b16),
            pltpu.VMEM((blocks, shared_rows, block_width), b16),
            dma,
        ]
        + [dma((GROUPS * (ctx_count - 1),))] * 2
        + [dma((GROUPS,))]
        + [dma((GROUPS, 10))] * 2
        + [dma((7,))] * 2
        + [dma((ctx_count - 1,))] * 2
        + [dma((1, 9))] * 2,
        compiler_params=pltpu.CompilerParams(
            collective_id=collective_id, has_side_effects=True, vmem_limit_bytes=56 * 2**20
        ),
    )(triple, counts, keep, out_weight)


def local(
    tokens,
    modality,
    keep_mask,
    positions,
    modal_table,
    norm_gain,
    norm_bias,
    qkv_weight,
    out_weight,
    mask_token,
):
    arguments = (
        tokens, modality, keep_mask, positions, modal_table, norm_gain, norm_bias, qkv_weight, out_weight, mask_token,
    )
    seq_count, ctx_count = lax.axis_size("seq"), lax.axis_size("ctx")
    tok_rows, width = tokens.shape
    local_width = qkv_weight.shape[2]
    shaped = seq_count == 8 and ctx_count == 4 and tok_rows == 128 and width % 4096 == 0
    if not (shaped and local_width == ctx_count * HEAD_DIM):
        return general(*arguments)
    half_width = width // 2
    frequency = jnp.exp(-math.log(10000.0) * jnp.arange(half_width, dtype=jnp.float32) / half_width)
    triple, embedded, counts, fits = gather_and_project(
        tokens, modality[None], keep_mask[None], positions[None], frequency[None], modal_table,
        norm_gain[None], norm_bias[None], qkv_weight, 11,
    )
    placed = attend_and_return(triple, counts, keep_mask[None], out_weight, 12)

    def finish(*given):
        return jnp.where((keep_mask == 1)[:, None], f32(embedded) + f32(placed), mask_token[None, :])

    return lax.cond(fits[0, 0] > 0.5, finish, general, *arguments)


def solution(mesh):
    in_specs = (
        P(("seq", "ctx"), None),
        P(("seq", "ctx")),
        P(("seq", "ctx")),
        P(("seq", "ctx")),
        P(),
        P(),
        P(),
        P(None, None, "seq"),
        P("seq", None),
        P(),
    )
    out_specs = P(("seq", "ctx"), None)
    return jax.shard_map(local, mesh=mesh, in_specs=in_specs, out_specs=out_specs, check_vma=False)
```

```python
import math

import jax
import jax.numpy as jnp
import numpy as np
from jax import lax
from jax.experimental import pallas as pl
from jax.experimental.pallas import tpu as pltpu
from jax.sharding import PartitionSpec as P

HEAD_DIM = 128


EPSILON = 1e-06
MESH = pl.DeviceIdType.MESH


def position_table(positions, feature_width):
    half_width = feature_width // 2
    frequency = jnp.exp(-math.log(10000.0) * jnp.arange(half_width, dtype=jnp.float32) / half_width)
    angles = positions.astype(jnp.float32)[:, None] * frequency[None, :]
    return jnp.concatenate([jnp.sin(angles), jnp.cos(angles)], axis=1)


def embed(tokens, modality, positions, modal_table):
    table_rows = jnp.where(modality[:, None] == 1, modal_table[1][None, :], modal_table[0][None, :])
    summed = tokens.astype(jnp.float32) + position_table(positions, tokens.shape[1]) + table_rows
    return summed.astype(jnp.bfloat16)


def layer_norm(embedded, norm_gain, norm_bias):
    values = embedded.astype(jnp.float32)
    row_mean = jnp.mean(values, axis=1, keepdims=True)
    centered = values - row_mean
    row_var = jnp.mean(centered * centered, axis=1, keepdims=True)
    return (centered * lax.rsqrt(row_var + EPSILON) * norm_gain + norm_bias).astype(jnp.bfloat16)


def everyone():
    seq_count, ctx_count = lax.axis_size("seq"), lax.axis_size("ctx")

    def place():
        return lax.axis_index("seq") * ctx_count + lax.axis_index("ctx")

    return seq_count * ctx_count, place, lambda j: {"seq": j // ctx_count, "ctx": lax.rem(j, ctx_count)}


def along(axis):
    return lax.axis_size(axis), lambda: lax.axis_index(axis), lambda j: {axis: j}


def exchange(x, group, source, target, out_shape, collective_id):
    count, place, device_of = group

    def kernel(x_ref, out_ref, send_sem, recv_sem, own_sem):
        me = place()
        barrier = pltpu.get_barrier_semaphore()

        def greet(step, carry):
            peer = lax.rem(me + step, count)
            pl.semaphore_signal(barrier, inc=1, device_id=device_of(peer), device_id_type=MESH)
            return carry

        def push(step):
            peer = lax.rem(me + step, count)
            return pltpu.make_async_remote_copy(
                src_ref=source(x_ref, peer),
                dst_ref=target(out_ref, me),
                send_sem=send_sem.at[step],
                recv_sem=recv_sem.at[step],
                device_id=device_of(peer),
                device_id_type=MESH,
            )

        def start(step, carry):
            push(step).start()
            return carry

        def finish(step, carry):
            push(step).wait()
            return carry

        lax.fori_loop(1, count, greet, 0)
        own = pltpu.make_async_copy(source(x_ref, me), target(out_ref, me), own_sem)
        own.start()
        pl.semaphore_wait(barrier, count - 1)
        lax.fori_loop(1, count, start, 0)
        lax.fori_loop(1, count, finish, 0)
        own.wait()

    return pl.pallas_call(
        kernel,
        out_shape=jax.ShapeDtypeStruct(out_shape, x.dtype),
        in_specs=[pl.BlockSpec(memory_space=pltpu.VMEM)],
        out_specs=pl.BlockSpec(memory_space=pltpu.VMEM),
        scratch_shapes=[
            pltpu.SemaphoreType.DMA((count,)),
            pltpu.SemaphoreType.DMA((count,)),
            pltpu.SemaphoreType.DMA,
        ],
        compiler_params=pltpu.CompilerParams(collective_id=collective_id, has_side_effects=True),
    )(x)


CHUNKS = 4


def remote(src, dst, sems, at, device):
    send_sem, recv_sem = sems
    return pltpu.make_async_remote_copy(
        src_ref=src,
        dst_ref=dst,
        send_sem=send_sem.at[at],
        recv_sem=recv_sem.at[at],
        device_id=device,
        device_id_type=MESH,
    )


def aligned(start, size):
    return pl.ds(pl.multiple_of(start * size, size), size)


def greet_line_and_plane(seq_count, ctx_count):
    me, level = lax.axis_index("seq"), lax.axis_index("ctx")
    barrier = pltpu.get_barrier_semaphore()
    for step in range(1, seq_count):
        peer = {"seq": lax.rem(me + step, seq_count)}
        pl.semaphore_signal(barrier, inc=1, device_id=peer, device_id_type=MESH)
    for step in range(1, ctx_count):
        peer = {"ctx": lax.rem(level + step, ctx_count)}
        pl.semaphore_signal(barrier, inc=1, device_id=peer, device_id_type=MESH)
    pl.semaphore_wait(barrier, seq_count + ctx_count - 2)


def regrouping(capacity, outer, inner, slot_count):
    row = lax.broadcasted_iota(jnp.int32, (capacity, capacity), 0)
    column = lax.broadcasted_iota(jnp.int32, (capacity, capacity), 1)
    first = row // (inner * slot_count)
    second = row // slot_count % inner
    wanted = (second * outer + first) * slot_count + row % slot_count
    return (column == wanted).astype(jnp.bfloat16)


def moved(choice, rows):
    return jnp.dot(choice, rows, preferred_element_type=jnp.float32).astype(jnp.bfloat16)


def spread_rows(outgoing, choice, qkv_weight, slot_count, collective_id):
    capacity, width = outgoing.shape
    rows = choice.shape[0]
    half = rows // 2
    seq_count, ctx_count = lax.axis_size("seq"), lax.axis_size("ctx")
    line_rows, plane_rows = capacity // ctx_count, capacity // seq_count
    part_width = width // CHUNKS

    kinds, _, local_width = qkv_weight.shape

    def kernel(
        x_ref, choice_ref, w_hbm, triple_ref, mid, ordered, arrived, out_ref, w_ref, total,
        zs, zr, ps, pr, gs, gr, own_sem, own_sems, w_sems,
    ):
        me, level = lax.axis_index("seq"), lax.axis_index("ctx")
        sibling, left, down = flip(me, 1), flip(me, 2), flip(me, 4)
        across = flip(left, 4)
        all_rows, first, second = pl.ds(0, rows), pl.ds(0, half), pl.ds(half, half)
        along_line, over_plane, gathering = (zs, zr), (ps, pr), (gs, gr)

        def cols(k):
            return pl.ds(k * part_width, part_width)

        def line(k, step):
            peer = lax.rem(level + step, ctx_count)
            src = x_ref.at[aligned(peer, line_rows), cols(k)]
            dst = mid.at[aligned(level, line_rows), cols(k)]
            return remote(src, dst, along_line, (k, step), {"ctx": peer})

        def plane(k, step):
            peer = lax.rem(me + step, seq_count)
            src = ordered.at[aligned(peer, plane_rows), cols(k)]
            dst = arrived.at[aligned(me, plane_rows), cols(k)]
            return remote(src, dst, over_plane, (k, step), {"seq": peer})

        def plane_own(k):
            here = aligned(me, plane_rows)
            return pltpu.make_async_copy(ordered.at[here, cols(k)], arrived.at[here, cols(k)], own_sems.at[k])

        moves = (
            (me, all_rows, sibling),
            (me, all_rows, left),
            (me, all_rows, down),
            (left, first, down),
            (down, second, left),
            (left, all_rows, sibling),
            (down, all_rows, sibling),
            (across, first, sibling),
            (across, second, sibling),
        )

        def hand(k, at):
            origin, which, place = moves[at]
            ref = out_ref.at[origin, which, cols(k)]
            return remote(ref, ref, gathering, (k, at), {"seq": place})

        def fetch(k):
            return pltpu.make_async_copy(w_hbm.at[:, cols(k), :], w_ref.at[:, cols(k), :], w_sems.at[k])

        greet_line_and_plane(seq_count, ctx_count)
        for k in range(CHUNKS):
            for step in range(1, ctx_count):
                line(k, step).start()
        for k in range(CHUNKS):
            fetch(k).start()
        here = aligned(level, line_rows)
        own = pltpu.make_async_copy(x_ref.at[here], mid.at[here], own_sem)
        own.start()
        regroup = regrouping(capacity, seq_count, ctx_count, slot_count)
        own.wait()
        for turn in range(CHUNKS + 4):
            k = turn - 4
            if 0 <= k < CHUNKS:
                for at in (0, 5, 6, 7, 8):
                    hand(k, at).wait_recv()
                fetch(k).wait()
                gathered = out_ref[:, :, cols(k)].reshape(seq_count * rows, part_width)
                for kind in range(kinds):
                    term = jnp.dot(gathered, w_ref[kind, cols(k), :], preferred_element_type=jnp.float32)
                    if k == 0:
                        total[kind] = term
                    elif k < CHUNKS - 1:
                        total[kind] += term
                    else:
                        triple_ref[kind] = (total[kind] + term).astype(jnp.bfloat16)
            k = turn - 3
            if 0 <= k < CHUNKS:
                hand(k, 3).wait_recv()
                hand(k, 7).start()
                hand(k, 4).wait_recv()
                hand(k, 8).start()
            k = turn - 2
            if 0 <= k < CHUNKS:
                hand(k, 1).wait_recv()
                hand(k, 3).start()
                hand(k, 5).start()
                hand(k, 2).wait_recv()
                hand(k, 4).start()
                hand(k, 6).start()
            k = turn - 1
            if 0 <= k < CHUNKS:
                for step in range(1, seq_count):
                    plane(k, step).wait_recv()
                plane_own(k).wait()
                out_ref[me, :, cols(k)] = moved(choice_ref[...], arrived[:, cols(k)])
                for at in (1, 2, 0):
                    hand(k, at).start()
            k = turn
            if k < CHUNKS:
                for step in range(1, ctx_count):
                    line(k, step).wait_recv()
                ordered[:, cols(k)] = moved(regroup, mid[:, cols(k)])
                for step in range(1, seq_count):
                    plane(k, step).start()
                plane_own(k).start()
        for k in range(CHUNKS):
            for at in range(9):
                hand(k, at).wait_send()
            for step in range(1, seq_count):
                plane(k, step).wait_send()
            for step in range(1, ctx_count):
                line(k, step).wait_send()

    dma = pltpu.SemaphoreType.DMA
    return pl.pallas_call(
        kernel,
        out_shape=jax.ShapeDtypeStruct((kinds, seq_count * rows, local_width), jnp.bfloat16),
        in_specs=[pl.BlockSpec(memory_space=pltpu.VMEM)] * 2 + [pl.BlockSpec(memory_space=pl.ANY)],
        out_specs=pl.BlockSpec(memory_space=pltpu.VMEM),
        scratch_shapes=[pltpu.VMEM((capacity, width), jnp.bfloat16)] * 3
        + [
            pltpu.VMEM((seq_count, rows, width), jnp.bfloat16),
            pltpu.VMEM(qkv_weight.shape, jnp.bfloat16),
            pltpu.VMEM((kinds, seq_count * rows, local_width), jnp.float32),
        ]
        + [dma((CHUNKS, ctx_count))] * 2
        + [dma((CHUNKS, seq_count))] * 2
        + [dma((CHUNKS, 9))] * 2
        + [dma, dma((CHUNKS,)), dma((CHUNKS,))],
        compiler_params=pltpu.CompilerParams(collective_id=collective_id, has_side_effects=True),
    )(outgoing, choice, qkv_weight)


def flip(position, bit):
    return position + bit * (1 - 2 * lax.rem(position // bit, 2))


def return_rows(attended, out_weight, choice, slot_count, collective_id):
    width = out_weight.shape[1]
    capacity, rows = choice.shape
    half = rows // 2
    seq_count, ctx_count = lax.axis_size("seq"), lax.axis_size("ctx")
    line_rows, plane_rows = capacity // ctx_count, capacity // seq_count
    part_width = width // CHUNKS

    def kernel(
        x_ref, w_ref, choice_ref, out_ref, shares, near, sums, from_left, from_down, last, passed, total,
        sorted_rows, arrived, ordered, ss, sr, ps, pr, zs, zr, own_sems, line_sems,
    ):
        me, level = lax.axis_index("seq"), lax.axis_index("ctx")
        sibling, left, down = flip(me, 1), flip(me, 2), flip(me, 4)
        first, second = pl.ds(0, half), pl.ds(half, half)
        summing, over_plane, along_line = (ss, sr), (ps, pr), (zs, zr)

        def cols(k):
            return pl.ds(k * part_width, part_width)

        def at(place, which):
            place = flip(place, 2) if which % 2 else place
            return flip(place, 4) if which // 2 else place

        def over(k, q):
            src = shares.at[aligned(at(sibling, q), rows), cols(k)]
            return remote(src, near.at[q, :, cols(k)], summing, (k, q), {"seq": sibling})

        def far(k, which):
            if which == 0:
                return remote(sums.at[3, first, cols(k)], from_left.at[1, :, cols(k)], summing, (k, 4), {"seq": left})
            if which == 1:
                return remote(sums.at[3, second, cols(k)], from_down.at[1, :, cols(k)], summing, (k, 5), {"seq": down})
            if which == 2:
                return remote(sums.at[1, first, cols(k)], from_left.at[0, :, cols(k)], summing, (k, 6), {"seq": left})
            if which == 3:
                return remote(sums.at[2, second, cols(k)], from_down.at[0, :, cols(k)], summing, (k, 7), {"seq": down})
            if which == 4:
                return remote(passed.at[0, :, cols(k)], last.at[0, :, cols(k)], summing, (k, 8), {"seq": down})
            return remote(passed.at[1, :, cols(k)], last.at[1, :, cols(k)], summing, (k, 9), {"seq": left})

        def plane(k, step):
            peer = lax.rem(me + step, seq_count)
            src = sorted_rows.at[aligned(peer, plane_rows), cols(k)]
            dst = arrived.at[aligned(me, plane_rows), cols(k)]
            return remote(src, dst, over_plane, (k, step), {"seq": peer})

        def plane_own(k):
            here = aligned(me, plane_rows)
            return pltpu.make_async_copy(sorted_rows.at[here, cols(k)], arrived.at[here, cols(k)], own_sems.at[k])

        def line(k, step):
            peer = lax.rem(level + step, ctx_count)
            src = ordered.at[aligned(peer, line_rows), cols(k)]
            dst = out_ref.at[aligned(level, line_rows), cols(k)]
            return remote(src, dst, along_line, (k, step), {"ctx": peer})

        def line_own(k):
            here = aligned(level, line_rows)
            return pltpu.make_async_copy(ordered.at[here, cols(k)], out_ref.at[here, cols(k)], line_sems.at[k])

        def wide(value):
            return value.astype(jnp.float32)

        def narrow(value):
            return value.astype(jnp.bfloat16)

        greet_line_and_plane(seq_count, ctx_count)
        regroup = regrouping(capacity, ctx_count, seq_count, slot_count)
        order = (3, 1, 2, 0)
        for turn in range(CHUNKS + 4):
            k = turn - 4
            if 0 <= k < CHUNKS:
                for step in range(1, seq_count):
                    plane(k, step).wait_recv()
                plane_own(k).wait()
                ordered[:, cols(k)] = moved(regroup, arrived[:, cols(k)])
                for step in range(1, ctx_count):
                    line(k, step).start()
                line_own(k).start()
            k = turn - 3
            if 0 <= k < CHUNKS:
                c = cols(k)
                far(k, 2).wait_recv()
                far(k, 4).wait_recv()
                total[:half, c] = narrow(wide(sums[0, :half, c]) + wide(from_left[0, :, c]) + wide(last[0, :, c]))
                far(k, 3).wait_recv()
                far(k, 5).wait_recv()
                total[half:, c] = narrow(wide(sums[0, half:, c]) + wide(from_down[0, :, c]) + wide(last[1, :, c]))
                sorted_rows[:, c] = moved(choice_ref[...], total[:, c])
                for step in range(1, seq_count):
                    plane(k, step).start()
                plane_own(k).start()
            k = turn - 2
            if 0 <= k < CHUNKS:
                c = cols(k)
                far(k, 0).wait_recv()
                passed[0, :, c] = narrow(wide(sums[2, :half, c]) + wide(from_left[1, :, c]))
                far(k, 4).start()
                far(k, 1).wait_recv()
                passed[1, :, c] = narrow(wide(sums[1, half:, c]) + wide(from_down[1, :, c]))
                far(k, 5).start()
            k = turn - 1
            if 0 <= k < CHUNKS:
                c = cols(k)
                for q in order:
                    over(k, q).wait_recv()
                    mine = shares[aligned(at(me, q), rows), c]
                    sums[q, :, c] = narrow(wide(mine) + wide(near[q, :, c]))
                    if q == 3:
                        far(k, 0).start()
                        far(k, 1).start()
                    if q == 1:
                        far(k, 2).start()
                    if q == 2:
                        far(k, 3).start()
            k = turn
            if k < CHUNKS:
                shares[:, cols(k)] = moved(x_ref[...], w_ref[:, cols(k)])
                for q in order:
                    over(k, q).start()
        for k in range(CHUNKS):
            for step in range(1, ctx_count):
                line(k, step).wait()
            line_own(k).wait()
            for step in range(1, seq_count):
                plane(k, step).wait_send()
            for q in order:
                over(k, q).wait_send()
            for which in range(6):
                far(k, which).wait_send()

    dma = pltpu.SemaphoreType.DMA
    bf16 = jnp.bfloat16
    return pl.pallas_call(
        kernel,
        out_shape=jax.ShapeDtypeStruct((capacity, width), bf16),
        in_specs=[pl.BlockSpec(memory_space=pltpu.VMEM)] * 3,
        out_specs=pl.BlockSpec(memory_space=pltpu.VMEM),
        scratch_shapes=[pltpu.VMEM((seq_count * rows, width), bf16)]
        + [pltpu.VMEM((4, rows, width), bf16)] * 2
        + [pltpu.VMEM((2, half, width), bf16)] * 4
        + [pltpu.VMEM((rows, width), bf16)]
        + [pltpu.VMEM((capacity, width), bf16)] * 3
        + [dma((CHUNKS, 10))] * 2
        + [dma((CHUNKS, seq_count))] * 2
        + [dma((CHUNKS, ctx_count))] * 2
        + [dma((CHUNKS,))] * 2,
        compiler_params=pltpu.CompilerParams(collective_id=collective_id, has_side_effects=True),
    )(attended, out_weight, choice)


def part(ref, j):
    return ref.at[j]


def whole(ref, j):
    return ref


def attend(triple):
    _, heads, rows, _ = triple.shape
    block = min(rows, 256)
    score_scale = 1.0 / math.sqrt(HEAD_DIM)

    def kernel(q_ref, k_ref, v_ref, out_ref):
        scores = (
            lax.dot_general(
                q_ref[...], k_ref[...], (((1,), (1,)), ((), ())), preferred_element_type=jnp.float32
            )
            * score_scale
        )
        expanded = jnp.exp(scores - jnp.max(scores, axis=1, keepdims=True))
        total = jnp.sum(expanded, axis=1, keepdims=True)
        summed = jnp.dot(expanded.astype(jnp.bfloat16), v_ref[...], preferred_element_type=jnp.float32)
        out_ref[...] = (summed / total).astype(jnp.bfloat16)

    return pl.pallas_call(
        kernel,
        grid=(heads, rows // block),
        out_shape=jax.ShapeDtypeStruct((heads, rows, HEAD_DIM), jnp.bfloat16),
        in_specs=[
            pl.BlockSpec((None, None, block, HEAD_DIM), lambda h, i: (0, h, i, 0)),
            pl.BlockSpec((None, None, rows, HEAD_DIM), lambda h, i: (1, h, 0, 0)),
            pl.BlockSpec((None, None, rows, HEAD_DIM), lambda h, i: (2, h, 0, 0)),
        ],
        out_specs=pl.BlockSpec((None, block, HEAD_DIM), lambda h, i: (h, i, 0)),
    )(triple, triple, triple)


def attend_by_head(triple):
    _, group_rows, local_width = triple.shape
    ctx = along("ctx")
    count = ctx[0]
    width = local_width // count
    heads = width // HEAD_DIM
    gathered = exchange(
        triple,
        ctx,
        lambda ref, j: ref.at[:, :, pl.ds(pl.multiple_of(j * width, HEAD_DIM), width)],
        lambda ref, j: ref.at[:, pl.ds(pl.multiple_of(j * group_rows, group_rows), group_rows), :],
        (3, count * group_rows, width),
        3,
    )
    if heads == 1:
        split = gathered[:, None]
    else:
        split = jnp.transpose(
            gathered.reshape(3, count * group_rows, heads, HEAD_DIM), (0, 2, 1, 3)
        )
    done = attend(split)
    if heads == 1:
        done = done[0]
    else:
        done = jnp.transpose(done, (1, 0, 2)).reshape(count * group_rows, width)
    return exchange(
        done,
        ctx,
        lambda ref, j: ref.at[pl.ds(pl.multiple_of(j * group_rows, group_rows), group_rows), :],
        lambda ref, j: ref.at[:, pl.ds(pl.multiple_of(j * width, HEAD_DIM), width)],
        (group_rows, local_width),
        4,
    )


def attend_by_row(triple):
    queries, key_rows, values = (triple[0], triple[1], triple[2])
    group_rows, local_width = queries.shape
    heads_here = local_width // HEAD_DIM
    score_scale = 1.0 / math.sqrt(HEAD_DIM)
    both = lax.all_gather(jnp.stack([key_rows, values]), "ctx", axis=1, tiled=True)
    length = both.shape[1]
    query_heads = queries.reshape(group_rows, heads_here, HEAD_DIM)
    key_heads = both[0].reshape(length, heads_here, HEAD_DIM)
    value_heads = both[1].reshape(length, heads_here, HEAD_DIM)
    scores = (
        jnp.einsum("ghd,khd->hgk", query_heads, key_heads, preferred_element_type=jnp.float32)
        * score_scale
    )
    expanded = jnp.exp(scores - jnp.max(scores, axis=2, keepdims=True))
    total = jnp.sum(expanded, axis=2, keepdims=True)
    summed = jnp.einsum(
        "hgk,khd->hgd",
        expanded.astype(jnp.bfloat16),
        value_heads,
        preferred_element_type=jnp.float32,
    )
    attended = (summed / total).astype(jnp.bfloat16)
    return jnp.transpose(attended, (1, 0, 2)).reshape(group_rows, local_width)


def general(
    tokens,
    modality,
    keep_mask,
    positions,
    modal_table,
    norm_gain,
    norm_bias,
    qkv_weight,
    out_weight,
    mask_token,
):
    tok_rows, feature_width = tokens.shape
    seq_count = lax.axis_size("seq")
    ctx_count = lax.axis_size("ctx")
    devices = seq_count * ctx_count
    slot_count = (tok_rows + devices - 1) // devices
    capacity = devices * slot_count
    own_rows = tok_rows // 4
    my_index = lax.axis_index("seq") * ctx_count + lax.axis_index("ctx")
    visible = keep_mask == 1
    own_count = jnp.sum(keep_mask)
    counts = exchange(
        jnp.full((1, 128), own_count, jnp.int32), everyone(), whole, part, (devices, 1, 128), 0
    )[:, 0, 0]
    index = jnp.arange(devices, dtype=jnp.int32)
    starts = jnp.sum(jnp.where(index[None, :] < index[:, None], counts[None, :], 0), axis=1)
    my_start = jnp.sum(jnp.where(index < my_index, counts, 0))
    token_index = jnp.arange(tok_rows, dtype=jnp.int32)
    local_rank = (
        jnp.sum(jnp.where(token_index[None, :] <= token_index[:, None], keep_mask[None, :], 0), axis=1) - 1
    )
    global_rank = my_start + local_rank
    owner = global_rank % devices
    piped = seq_count == 8 and slot_count * ctx_count % 16 == 0
    if piped:
        owner = owner % ctx_count * seq_count + owner // ctx_count
    token_slot = jnp.where(visible, owner * slot_count + local_rank // devices, capacity)
    slot_index = jnp.arange(capacity, dtype=jnp.int32)
    slot_of_token = (token_slot[:, None] == slot_index[None, :]).astype(jnp.bfloat16)
    slot_place = slot_index % slot_count
    source_start = jnp.repeat(starts, slot_count)
    source_count = jnp.repeat(counts, slot_count)
    offset = (my_index - source_start) % devices + devices * slot_place
    usable = offset < source_count
    slot_row = jnp.where(usable, (source_start + offset) // devices, own_rows)
    row_of_slot = (
        slot_row[:, None] == jnp.arange(own_rows, dtype=jnp.int32)[None, :]
    ).astype(jnp.bfloat16)

    embedded = embed(tokens, modality, positions, modal_table)

    def pick(choice, rows, side):
        return lax.dot_general(
            choice, rows, (((side,), (0,)), ((), ())), preferred_element_type=jnp.float32
        )

    normed = layer_norm(embedded, norm_gain, norm_bias)
    outgoing = pick(slot_of_token, normed, 0).astype(jnp.bfloat16)
    slots = (devices, slot_count, feature_width)
    if piped:
        triple = spread_rows(outgoing, row_of_slot.T, qkv_weight, slot_count, 1)
    else:
        arriving = exchange(outgoing.reshape(slots), everyone(), part, part, slots, 1)
        own_normed = pick(row_of_slot, arriving.reshape(capacity, feature_width), 0).astype(jnp.bfloat16)
        group = exchange(own_normed, along("seq"), whole, part, (seq_count,) + own_normed.shape, 2)
        triple = jnp.einsum(
            "rd,tdc->trc",
            group.reshape(seq_count * own_rows, feature_width),
            qkv_weight,
            preferred_element_type=jnp.float32,
        ).astype(jnp.bfloat16)
    if triple.shape[2] % (ctx_count * HEAD_DIM) == 0:
        attended = attend_by_head(triple)
    else:
        attended = attend_by_row(triple)
    if piped:
        returned = return_rows(attended, out_weight, row_of_slot, slot_count, 5)
    else:
        shares = jnp.dot(attended, out_weight, preferred_element_type=jnp.float32).astype(jnp.bfloat16)
        shares = shares.reshape(seq_count, own_rows, feature_width)
        shares = exchange(shares, along("seq"), part, part, shares.shape, 5)
        projected = jnp.sum(shares.astype(jnp.float32), axis=0).astype(jnp.bfloat16)
        returning = pick(row_of_slot, projected, 1).astype(jnp.bfloat16)
        returned = exchange(returning.reshape(slots), everyone(), part, part, slots, 6)
        returned = returned.reshape(capacity, feature_width)
    restored = pick(slot_of_token, returned, 1)
    return [bf16(restored), embedded]


GROUP = 16
GROUPS = 2
BASE = GROUP * GROUPS
SHARED = 32
TAIL = 64
NEGATIVE = -1e30


def bf16(value):
    return value.astype(jnp.bfloat16)


def f32(value):
    return value.astype(jnp.float32)


def sine_and_cosine(angle):
    turns = jnp.floor(angle * (2.0 / math.pi) + 0.5)
    quarter = turns.astype(jnp.int32)
    r = ((angle - turns * 1.5703125) - turns * 4.837512969970703125e-4) - turns * 7.54978995489188216e-8
    square = r * r
    sine = r + r * square * (-1.6666654611e-1 + square * (8.3321608736e-3 - square * 1.9515295891e-4))
    cosine = (
        1.0
        - 0.5 * square
        + square * square * (4.166664568298827e-2 + square * (-1.388731625493765e-3 + square * 2.443315711809948e-5))
    )
    odd = (quarter & 1) == 1
    first = jnp.where(odd, cosine, sine)
    second = jnp.where(odd, sine, cosine)
    first = jnp.where((quarter & 2) == 2, -first, first)
    second = jnp.where(((quarter + 1) & 2) == 2, -second, second)
    return first, second


def as_column(row, size):
    across = lax.broadcasted_iota(jnp.int32, (size, size), 1)
    down = lax.broadcasted_iota(jnp.int32, (size, size), 0)
    return jnp.sum(jnp.where(across == down, row, 0.0), axis=1, keepdims=True)


def ranks_of(keep_row, size):
    across = lax.broadcasted_iota(jnp.int32, (size, size), 1)
    down = lax.broadcasted_iota(jnp.int32, (size, size), 0)
    column = as_column(keep_row, size)
    return jnp.sum(jnp.where(down < across, column, 0.0), axis=0, keepdims=True)


class Layout:
    def __init__(self, counts, place, level, seq_count, ctx_count):
        lanes = counts.shape[1:]
        cores = (seq_count // 2, 2, ctx_count) + lanes
        extra = jnp.maximum(counts - BASE, 0.0).reshape(cores)
        first = jnp.minimum(extra[:, 0], 1.0 * GROUP)
        second = jnp.minimum(extra[:, 1], GROUP - first)
        of_chip = first + second
        tail_of = jnp.stack([first, second], axis=1).reshape(counts.shape)
        over = extra.reshape(counts.shape) - tail_of
        index = lax.broadcasted_iota(jnp.int32, counts.shape, 0)
        self.over_start = jnp.sum(jnp.where(index < place, over, 0.0), axis=0)
        self.own_tail = jnp.sum(jnp.where(index == place, tail_of, 0.0), axis=0)
        before = jnp.sum(jnp.where(index == place - ctx_count, tail_of, 0.0), axis=0)
        self.own_start = jnp.where(lax.rem(place // ctx_count, 2) == 1, before, 0.0)
        total = jnp.sum(over, axis=0)
        tails, free, starts = [], [], []
        running = jnp.zeros(lanes, jnp.float32)
        for z in range(ctx_count):
            tail = jnp.sum(of_chip[:, z], axis=0)
            room = jnp.clip(TAIL - tail, 0.0, 1.0 * SHARED)
            tails.append(tail)
            free.append(room)
            starts.append(running)
            running = running + room
        self.fits = jnp.where(total > running, 0.0, 1.0)
        self.tails, self.free, self.starts = tails, free, starts
        self.used = [jnp.clip(total - starts[z], 0.0, free[z]) for z in range(ctx_count)]
        by_plane = counts.reshape((seq_count, ctx_count) + lanes)
        seat = lax.broadcasted_iota(jnp.int32, by_plane.shape, 0)
        lane = lax.broadcasted_iota(jnp.int32, by_plane.shape, 3)
        self.lane_counts = jnp.sum(jnp.where(lane // GROUP == seat, by_plane, 0.0), axis=0)
        seat = lax.broadcasted_iota(jnp.int32, of_chip.shape, 0)
        lane = lax.broadcasted_iota(jnp.int32, of_chip.shape, 3)
        self.lane_tails = jnp.sum(jnp.where(lane // GROUP == seat, of_chip, 0.0), axis=0)
        self.lane_tail_start = jnp.sum(jnp.where(seat < lane // GROUP, of_chip, 0.0), axis=0)

    def of_level(self, values, level):
        out = values[0]
        for z in range(1, len(values)):
            out = jnp.where(level == z, values[z], out)
        return out

    def shared_slots(self, keep_row, rank_row):
        beyond = rank_row - BASE - self.own_tail[0:1]
        ordinal = self.over_start[0:1] + beyond
        slot = jnp.full(ordinal.shape, -1.0, jnp.float32)
        for z in range(len(self.free)):
            here = (ordinal >= self.starts[z][0:1]) & (ordinal < self.starts[z][0:1] + self.free[z][0:1])
            slot = jnp.where(here, ordinal - self.starts[z][0:1] + SHARED * z, slot)
        return jnp.where((keep_row > 0.0) & (beyond >= 0.0), slot, -1.0)

    def tail_slots(self, keep_row, rank_row):
        ordinal = rank_row - BASE
        valid = (keep_row > 0.0) & (ordinal >= 0.0) & (ordinal < self.own_tail[0:1])
        return jnp.where(valid, ordinal + self.own_start[0:1], -1.0)

    def tail_choice(self, level):
        counts = self.of_level([self.lane_tails[z] for z in range(len(self.free))], level)[0:1]
        start = self.of_level([self.lane_tail_start[z] for z in range(len(self.free))], level)[0:1]
        tail = self.of_level(self.tails, level)[0:1]
        used = self.of_level(self.used, level)[0:1]
        size = (TAIL, counts.shape[1])
        target = f32(lax.broadcasted_iota(jnp.int32, size, 0))
        lane = lax.broadcasted_iota(jnp.int32, size, 1)
        within = f32(lane % GROUP)
        valid = counts > within
        grouped = bf16(jnp.where(valid & (start + within == target), 1.0, 0.0))
        where = f32(lane)
        shared = bf16(jnp.where((where < used) & (tail + where == target), 1.0, 0.0))
        return grouped, shared[:, :SHARED]

    def key_bias(self):
        width = self.lane_counts.shape[2]
        within = f32(lax.broadcasted_iota(jnp.int32, (1, width), 1) % GROUP)
        parts = []
        for group in range(GROUPS):
            for z in range(len(self.free)):
                parts.append(jnp.where(self.lane_counts[z][0:1] > within + group * GROUP, 0.0, NEGATIVE))
        slot = f32(lax.broadcasted_iota(jnp.int32, (1, width), 1))
        for z in range(0, len(self.free), 2):
            low = self.tails[z][0:1] + self.used[z][0:1]
            high = self.tails[z + 1][0:1] + self.used[z + 1][0:1]
            limit = jnp.where(slot < TAIL, low, high + TAIL)
            parts.append(jnp.where(slot < limit, 0.0, NEGATIVE))
        return jnp.concatenate(parts, axis=1)


class Plane:
    def __init__(self):
        self.me = lax.axis_index("seq")
        self.level = lax.axis_index("ctx")
        self.sibling, self.left, self.down = flip(self.me, 1), flip(self.me, 2), flip(self.me, 4)
        self.across = flip(self.left, 4)

    def order(self, seat):
        core, x, y = lax.rem(seat, 2), lax.rem(seat // 2, 2), seat // 4
        return core * 4 + y * 2 + x


class Gather:
    def __init__(self, plane, halves, sems, at):
        self.plane, self.halves, self.sems, self.at = plane, halves, sems, at

    def moves(self):
        p = self.plane
        out = []
        for origin, half, place in (
            (p.me, None, p.left),
            (p.me, None, p.down),
            (p.me, None, p.sibling),
            (p.left, 0, p.down),
            (p.down, 1, p.left),
            (p.left, None, p.sibling),
            (p.down, None, p.sibling),
            (p.across, 0, p.sibling),
            (p.across, 1, p.sibling),
        ):
            out.append((self.halves(origin, half), place))
        return out

    def copy(self, move):
        ref, place = self.moves()[move]
        return remote(ref, ref, self.sems, (self.at, move), {"seq": place})

    def begin(self):
        for move in (0, 1, 2):
            self.copy(move).start()

    def forward(self):
        self.copy(0).wait_recv()
        self.copy(3).start()
        self.copy(5).start()
        self.copy(1).wait_recv()
        self.copy(4).start()
        self.copy(6).start()

    def finish(self):
        self.copy(3).wait_recv()
        self.copy(7).start()
        self.copy(4).wait_recv()
        self.copy(8).start()

    def arrive(self):
        for move in (2, 5, 6, 7, 8):
            self.copy(move).wait_recv()

    def drain(self):
        for move in range(9):
            self.copy(move).wait_send()


class BlockSum:
    def __init__(self, plane, source, first, second, third, result, sems):
        self.plane, self.sems = plane, sems
        self.source, self.first, self.second, self.third, self.result = source, first, second, third, result

    def block(self, seat, half):
        return 2 * (lax.rem(seat // 2, 2) + 2 * (seat // 4)) + half

    def copies(self):
        p = self.plane
        core = lax.rem(p.me, 2)
        out = [(self.source.at[pl.ds(8 * (1 - core), 8)], self.first, p.sibling)]
        mine = 8 * core
        out.append((self.source.at[mine + self.block(p.across, 0)], self.second.at[0], p.left))
        out.append((self.source.at[mine + self.block(p.left, 0)], self.second.at[1], p.left))
        out.append((self.source.at[mine + self.block(p.across, 1)], self.second.at[2], p.down))
        out.append((self.source.at[mine + self.block(p.down, 1)], self.second.at[3], p.down))
        out.append((self.source.at[mine + self.block(p.down, 0)], self.third.at[0], p.down))
        out.append((self.source.at[mine + self.block(p.left, 1)], self.third.at[1], p.left))
        return out

    def copy(self, at):
        src, dst, place = self.copies()[at]
        return remote(src, dst, self.sems, (at,), {"seq": place})

    def level_one(self):
        self.copy(0).start()

    def level_two(self):
        core = lax.rem(self.plane.me, 2)
        self.copy(0).wait_recv()
        for block in range(8):
            at = 8 * core + block
            self.source[at] = self.source[at] + self.first[block]
        for at in (1, 2, 3, 4):
            self.copy(at).start()

    def level_three(self):
        p = self.plane
        mine = 8 * lax.rem(p.me, 2)
        self.copy(1).wait_recv()
        at = mine + self.block(p.down, 0)
        self.source[at] = self.source[at] + self.second[0]
        self.copy(5).start()
        self.copy(3).wait_recv()
        at = mine + self.block(p.left, 1)
        self.source[at] = self.source[at] + self.second[2]
        self.copy(6).start()

    def total(self):
        p = self.plane
        mine = 8 * lax.rem(p.me, 2)
        self.copy(2).wait_recv()
        self.copy(5).wait_recv()
        first = self.source[mine + self.block(p.me, 0)]
        self.result[0] = first + self.second[1] + self.third[0]
        self.copy(4).wait_recv()
        self.copy(6).wait_recv()
        second = self.source[mine + self.block(p.me, 1)]
        self.result[1] = second + self.second[3] + self.third[1]

    def drain(self):
        for at in range(7):
            self.copy(at).wait_send()


class RowSum:
    def __init__(self, plane, given, mine, near, sums, from_left, from_down, last, passed, store, sems, at):
        self.plane, self.given, self.mine, self.near, self.sums = plane, given, mine, near, sums
        self.from_left, self.from_down, self.last, self.passed = from_left, from_down, last, passed
        self.store, self.sems, self.at = store, sems, at
        self.half = passed.shape[-1]

    def over(self, q):
        return remote(self.given(q), self.near.at[q], self.sems, (self.at, q), {"seq": self.plane.sibling})

    def far(self, which):
        low, high = pl.ds(0, self.half), pl.ds(self.half, self.half)
        left, down = self.plane.left, self.plane.down
        src, dst, to = (
            (self.sums.at[3, :, low], self.from_left.at[1], left),
            (self.sums.at[3, :, high], self.from_down.at[1], down),
            (self.sums.at[1, :, low], self.from_left.at[0], left),
            (self.sums.at[2, :, high], self.from_down.at[0], down),
            (self.passed.at[0], self.last.at[0], down),
            (self.passed.at[1], self.last.at[1], left),
        )[which]
        return remote(src, dst, self.sems, (self.at, 4 + which), {"seq": to})

    def begin(self):
        for q in (3, 1, 2, 0):
            self.over(q).start()

    def chip(self):
        for q in (3, 1, 2, 0):
            self.over(q).wait_recv()
            self.sums[q] = bf16(f32(self.mine(q)) + f32(self.near[q]))
            if q == 3:
                self.far(0).start()
                self.far(1).start()
            if q == 1:
                self.far(2).start()
            if q == 2:
                self.far(3).start()

    def relay(self):
        self.far(0).wait_recv()
        self.passed[0] = bf16(f32(self.sums[2, :, : self.half]) + f32(self.from_left[1]))
        self.far(4).start()
        self.far(1).wait_recv()
        self.passed[1] = bf16(f32(self.sums[1, :, self.half :]) + f32(self.from_down[1]))
        self.far(5).start()

    def end(self):
        self.far(2).wait_recv()
        self.far(4).wait_recv()
        self.store(0, bf16(f32(self.sums[0, :, : self.half]) + f32(self.from_left[0]) + f32(self.last[0])))
        self.far(3).wait_recv()
        self.far(5).wait_recv()
        self.store(1, bf16(f32(self.sums[0, :, self.half :]) + f32(self.from_down[0]) + f32(self.last[1])))

    def drain(self):
        for q in range(4):
            self.over(q).wait_send()
        for which in range(6):
            self.far(which).wait_send()


def counts_of(ref, seq_count, ctx_count):
    return f32(ref[...].reshape((seq_count * ctx_count,) + ref.shape[2:]))


def embedded_rows(tokens, waves, taxel, table):
    return bf16(tokens + waves + jnp.where(taxel, table[1:2], table[0:1]))


def encode(tokens, modality, keep, positions, frequency, modal_table, gain, bias, qkv_weight, out_weight, collective_id):
    seq_count, ctx_count = lax.axis_size("seq"), lax.axis_size("ctx")
    tok_rows, width = tokens.shape
    kinds, _, local_width = qkv_weight.shape
    head_width = local_width // ctx_count
    blocks = 16
    block_width = width // blocks
    plane_rows = seq_count * GROUP
    slots = ctx_count * (2 * plane_rows + TAIL)
    half_width = width // 2
    shared_rows = ctx_count * SHARED
    score_scale = 1.0 / math.sqrt(HEAD_DIM)
    early = 4
    early_width = width // early

    quarter = width // 4
    chips = seq_count // 2
    sets = GROUPS + 1

    def kernel(
        mod_ref, keep_ref, pos_ref, freq_ref, table_ref, gain_ref, bias_ref, tok_hbm, w_hbm, proj_hbm,
        out_hbm, emb_hbm, fits_ref,
        tok_ref, w_ref, proj_ref, emb_ref, cnt_ref, normed, opening, gathered, tail_own, tail_in, tail,
        shared_in, first, second, third, summed, crossed, shared, staged, qk_ref, v_ref, peak, running,
        attended, inward, shares, near, sums, from_left, from_down, last, passed, returned,
        tail_shares, tail_near, tail_sums, tail_left, tail_down, tail_last, tail_passed,
        ret_in, ret_first, ret_second, ret_third, final, out_ref,
        w_sems, cs, cr, gs, gr, bs, br, xs, xr, ds, dr,
        fs, fr, back_sems, ss, sr, rs, rr, ys, yr, ts, tr, out_sems,
    ):
        plane = Plane()
        me, level = plane.me, plane.level
        sibling, left, down = plane.sibling, plane.left, plane.down
        unpack = (((0,), (0,)), ((), ()))

        def fetch(kind):
            return pltpu.make_async_copy(w_hbm.at[kind], w_ref.at[kind], w_sems.at[kind])

        save_embedded = pltpu.make_async_copy(emb_ref, emb_hbm, w_sems.at[kinds + 2])
        fetch_tokens = pltpu.make_async_copy(tok_hbm, tok_ref, w_sems.at[kinds])
        fetch_projection = pltpu.make_async_copy(proj_hbm, proj_ref, w_sems.at[kinds + 1])

        def count_line(step):
            peer = lax.rem(level + step, ctx_count)
            ref = cnt_ref.at[me, level]
            return remote(ref, ref, (cs, cr), (step - 1,), {"ctx": peer})

        def count_plane(step):
            peer = lax.rem(me + step, seq_count)
            ref = cnt_ref.at[me]
            return remote(ref, ref, (cs, cr), (ctx_count - 2 + step,), {"seq": peer})

        def piece(group):
            def halves(origin, half):
                ref = gathered.at[group, origin]
                if half is None:
                    return ref
                return ref.at[:, pl.ds(half * half_width, half_width)]

            return halves

        def blocks_of(ref):
            def halves(origin, half):
                start = 2 * plane.order(origin)
                if half is None:
                    return ref.at[pl.ds(start, 2)]
                return ref.at[start + half]

            return halves

        def tail_piece(origin, half):
            start = lax.rem(origin, 2) * half_width + (half or 0) * quarter
            cols = pl.ds(pl.multiple_of(start, quarter), half_width if half is None else quarter)
            return tail.at[origin // 2, :, cols]

        groups = [Gather(plane, piece(g), (gs, gr), g) for g in range(GROUPS)]
        groups.append(Gather(plane, tail_piece, (gs, gr), GROUPS))
        spread = Gather(plane, blocks_of(shared), (gs, gr), GROUPS + 1)
        back_spread = Gather(plane, blocks_of(final), (gs, gr), GROUPS + 2)
        core = lax.rem(me, 2)
        my_half, other_half = aligned(core, half_width), aligned(1 - core, half_width)
        tail_swap = remote(tail_own.at[:, other_half], tail_in, (ts, tr), (0,), {"seq": sibling})
        tail_rows = pl.ds(BASE, GROUP)
        tail_result = returned.at[tail_rows, my_half]
        tail_back = remote(tail_result, tail_result, (ts, tr), (1,), {"seq": sibling})
        reduce_in = BlockSum(plane, shared_in, first, second, third, summed, (bs, br))

        def cross(step):
            peer = lax.rem(level + step, ctx_count)
            src = summed.at[:, aligned(peer, SHARED), :]
            return remote(src, crossed.at[step - 1], (xs, xr), (step - 1,), {"ctx": peer})

        def rows_of(group):
            return plane_rows if group < 2 else TAIL

        def slot_start(group, z):
            return pl.multiple_of(group * ctx_count * plane_rows + z * rows_of(group), GROUP)

        def dealt(kind, start, rows):
            here = pl.ds(pl.multiple_of(start, GROUP), rows)
            if kind == 2:
                return v_ref.at[here, pl.ds(0, head_width)]
            return qk_ref.at[kind, here]

        def deal(group, kind, step):
            peer = lax.rem(level + step, ctx_count)
            src = staged.at[group * kinds + kind, peer, pl.ds(0, rows_of(group))]
            at = (group * kinds + kind) * (ctx_count - 1) + step - 1
            return remote(src, dealt(kind, slot_start(group, level), rows_of(group)), (ds, dr), (at,), {"ctx": peer})

        def place(which_seat, which):
            seat = flip(which_seat, 2) if which % 2 else which_seat
            return flip(seat, 4) if which // 2 else seat

        def row_sum(g):
            def store(side, value):
                returned[g * GROUP : (g + 1) * GROUP, side * half_width : (side + 1) * half_width] = value

            return RowSum(
                plane, lambda q: shares.at[g, place(sibling, q)], lambda q: shares[g, place(me, q)], near.at[g],
                sums.at[g], from_left.at[g], from_down.at[g], last.at[g], passed.at[g], store, (ss, sr), g,
            )

        def store_tail(side, value):
            start = pl.multiple_of(core * half_width + side * quarter, quarter)
            returned[tail_rows, pl.ds(start, quarter)] = value

        row_sums = [row_sum(g) for g in range(GROUPS)]
        row_sums.append(
            RowSum(
                plane, lambda q: tail_shares.at[place(me, q) // 2, :, other_half],
                lambda q: tail_shares[place(me, q) // 2, :, my_half], tail_near,
                tail_sums, tail_left, tail_down, tail_last, tail_passed, store_tail, (ss, sr), GROUPS,
            )
        )

        def back(group, step):
            peer = lax.rem(level + step, ctx_count)
            src = attended.at[pl.ds(slot_start(group, peer), rows_of(group))]
            dst = inward.at[group, pl.ds(0, rows_of(group)), aligned(level, head_width)]
            return remote(src, dst, (fs, fr), (group * (ctx_count - 1) + step - 1,), {"ctx": peer})

        def back_own(group):
            src = attended.at[pl.ds(slot_start(group, level), rows_of(group))]
            dst = inward.at[group, pl.ds(0, rows_of(group)), aligned(level, head_width)]
            return pltpu.make_async_copy(src, dst, back_sems.at[group])

        own_start = 2 * plane.order(me)

        def cross_back(step):
            peer = lax.rem(level + step, ctx_count)
            ref = final.at[pl.ds(own_start, 2), aligned(level, SHARED), :]
            return remote(ref, ref, (ys, yr), (step - 1,), {"ctx": peer})

        class Result:
            def __setitem__(self, half, value):
                final[own_start + half, aligned(level, SHARED), :] = value

        reduce_back = BlockSum(plane, ret_in, ret_first, ret_second, ret_third, Result(), (rs, rr))

        fetch_tokens.start()
        barrier = pltpu.get_barrier_semaphore()
        for step in range(1, seq_count):
            peer = {"seq": lax.rem(me + step, seq_count)}
            pl.semaphore_signal(barrier, inc=1, device_id=peer, device_id_type=MESH)
        for step in range(1, ctx_count):
            peer = {"ctx": lax.rem(level + step, ctx_count)}
            pl.semaphore_signal(barrier, inc=1, device_id=peer, device_id_type=MESH)
        keep_row = f32(keep_ref[...])
        place_row, taxel_row = f32(pos_ref[...]), f32(mod_ref[...])
        own_count = jnp.sum(keep_row, axis=1, keepdims=True).astype(jnp.int32)
        cnt_ref[me, level] = jnp.broadcast_to(own_count, cnt_ref.shape[2:])
        rank_row = ranks_of(keep_row, tok_rows)
        slot = f32(lax.broadcasted_iota(jnp.int32, (BASE, tok_rows), 0))
        base_pick = jnp.where((keep_row > 0.0) & (rank_row == slot), 1.0, 0.0)
        base_choice = bf16(base_pick)

        opening_pick = base_pick[:GROUP]
        opening_place = jnp.sum(opening_pick * place_row, axis=1, keepdims=True)
        opening_taxel = jnp.sum(opening_pick * taxel_row, axis=1, keepdims=True) > 0.5
        total = jnp.zeros((GROUP, 1), jnp.float32)
        fetch_tokens.wait()
        for part in range(early // 2):
            waves = sine_and_cosine(opening_place * freq_ref[:, part * early_width : (part + 1) * early_width])
            for side in range(2):
                start = side * half_width + part * early_width
                cols = slice(start, start + early_width)
                rows = jnp.dot(base_choice[:GROUP], tok_ref[:, cols], preferred_element_type=jnp.float32)
                rounded = embedded_rows(rows, waves[side], opening_taxel, table_ref[:, cols])
                opening[:, cols] = rounded
                total = total + jnp.sum(f32(rounded), axis=1, keepdims=True)
        mean = total * (1.0 / width)
        total = jnp.zeros((GROUP, 1), jnp.float32)
        for part in range(early):
            centered = f32(opening[:, part * early_width : (part + 1) * early_width]) - mean
            total = total + jnp.sum(centered * centered, axis=1, keepdims=True)
        scale = lax.rsqrt(total * (1.0 / width) + EPSILON)
        for part in range(early):
            cols = slice(part * early_width, (part + 1) * early_width)
            gathered[0, me, :, cols] = bf16((f32(opening[:, cols]) - mean) * scale * gain_ref[:, cols] + bias_ref[:, cols])
        pl.semaphore_wait(barrier, seq_count + ctx_count - 2)
        groups[0].begin()
        for step in range(1, ctx_count):
            count_line(step).start()

        def project(rows, kind):
            return bf16(jnp.dot(rows, w_ref[kind], preferred_element_type=jnp.float32))

        def send(group, kind, values):
            rows = rows_of(group)
            for z in range(ctx_count):
                staged[group * kinds + kind, z, :rows] = values[:, z * head_width : (z + 1) * head_width]
            dealt(kind, slot_start(group, level), rows)[...] = staged[group * kinds + kind, level, :rows]
            for step in (2, 3, 1):
                deal(group, kind, step).start()

        for kind in (1, 2, 0):
            fetch(kind).start()
        fetch_projection.start()
        v_ref[:, head_width:] = jnp.ones((slots, head_width), jnp.bfloat16)

        place_column = as_column(place_row, tok_rows)
        taxel = as_column(taxel_row, tok_rows) > 0.5

        def embed_block(at, total):
            waves = sine_and_cosine(place_column * freq_ref[:, aligned(at, block_width)])
            for side in range(2):
                start = side * half_width + at * block_width
                cols = pl.ds(pl.multiple_of(start, block_width), block_width)
                rounded = embedded_rows(f32(tok_ref[:, cols]), waves[side], taxel, table_ref[:, cols])
                emb_ref[:, cols] = rounded
                values = f32(rounded)
                for lane in range(0, block_width, 128):
                    total = total + values[:, lane : lane + 128]
            return total

        nothing = jnp.zeros((tok_rows, 128), jnp.float32)
        total = lax.fori_loop(0, blocks // 2, embed_block, nothing)
        mean = jnp.sum(total, axis=1, keepdims=True) * (1.0 / width)
        for step in range(1, ctx_count):
            count_line(step).wait_recv()
        for step in range(1, seq_count):
            count_plane(step).start()
        groups[0].forward()

        def var_block(at, total):
            centered = f32(emb_ref[:, aligned(at, block_width)]) - mean
            centered = centered * centered
            for lane in range(0, block_width, 128):
                total = total + centered[:, lane : lane + 128]
            return total

        total = lax.fori_loop(0, blocks, var_block, nothing)
        scale = lax.rsqrt(jnp.sum(total, axis=1, keepdims=True) * (1.0 / width) + EPSILON)

        def norm_block(at, carry):
            cols = aligned(at, block_width)
            values = (f32(emb_ref[:, cols]) - mean) * scale * gain_ref[:, cols] + bias_ref[:, cols]
            rows = bf16(values)
            normed[:, cols] = rows
            gathered[1, me, :, cols] = moved(base_choice[GROUP:], rows)
            return carry

        lax.fori_loop(0, blocks, norm_block, 0)
        groups[1].begin()
        groups[0].finish()
        save_embedded.start()
        for step in range(1, seq_count):
            count_plane(step).wait_recv()
        layout = Layout(counts_of(cnt_ref, seq_count, ctx_count), me * ctx_count + level, level, seq_count, ctx_count)
        fits_ref[0] = jnp.max(layout.fits).astype(jnp.int32)
        slot = f32(lax.broadcasted_iota(jnp.int32, (shared_rows, tok_rows), 0))
        shared_choice = bf16(jnp.where(layout.shared_slots(keep_row, rank_row) == slot, 1.0, 0.0))
        slot = f32(lax.broadcasted_iota(jnp.int32, (GROUP, tok_rows), 0))
        tail_choice = bf16(jnp.where(layout.tail_slots(keep_row, rank_row) == slot, 1.0, 0.0))
        both_choice = jnp.concatenate([shared_choice, tail_choice], axis=0)
        for block in range(blocks):
            cols = slice(block * block_width, (block + 1) * block_width)
            rows = moved(both_choice, normed[:, cols])
            shared_in[block] = rows[:shared_rows]
            tail_own[:, cols] = rows[shared_rows:]
        reduce_in.level_one()
        tail_swap.start()
        groups[0].arrive()

        opening_rows = gathered[0].reshape(plane_rows, width)
        fetch(1).wait()
        send(0, 1, project(opening_rows, 1))
        reduce_in.level_two()
        groups[1].forward()
        fetch(2).wait()
        send(0, 2, project(opening_rows, 2))
        fetch(0).wait()
        send(0, 0, project(opening_rows, 0))
        tail_swap.wait_recv()
        tail[me // 2, :, my_half] = tail_own[:, my_half] + tail_in[...]
        groups[1].finish()
        reduce_in.level_three()
        groups[2].begin()
        groups[1].arrive()
        group_rows = gathered[1].reshape(plane_rows, width)
        key_rows = project(group_rows, 1)
        reduce_in.total()
        for step in range(1, ctx_count):
            cross(step).start()
        send(1, 1, key_rows)
        groups[2].forward()
        send(1, 2, project(group_rows, 2))
        groups[2].finish()
        for step in range(1, ctx_count):
            cross(step).wait_recv()
        own = summed[:, aligned(level, SHARED), :]
        shared[pl.ds(own_start, 2)] = own + crossed[0] + crossed[1] + crossed[2]
        spread.begin()
        send(1, 0, project(group_rows, 0))
        grouped_choice, shared_choice = layout.tail_choice(level)
        key_bias = layout.key_bias()
        spread.forward()
        groups[2].arrive()
        spread.finish()
        spread.arrive()
        tail_count = chips * GROUP
        held_tail = tail[...].reshape(tail_count, width)
        for kind in (1, 2, 0):
            total = jnp.zeros((tail_count + SHARED, local_width), jnp.float32)
            for block in range(blocks):
                cols = slice(block * block_width, (block + 1) * block_width)
                rows = jnp.concatenate([held_tail[:, cols], shared[block]], axis=0)
                total = total + jnp.dot(rows, w_ref[kind, cols, :], preferred_element_type=jnp.float32)
            rows = bf16(total)
            packed = jnp.dot(grouped_choice[:, :tail_count], rows[:tail_count], preferred_element_type=jnp.float32)
            packed = packed + jnp.dot(shared_choice, rows[tail_count:], preferred_element_type=jnp.float32)
            send(2, kind, bf16(packed))

        def dealt_in(group, kind):
            for step in range(1, ctx_count):
                deal(group, kind, step).wait_recv()

        first_keys = GROUPS * ctx_count * plane_rows
        factor = score_scale * math.log2(math.e)

        def scores_of(begin, rows, low, high):
            scores = lax.dot_general(
                qk_ref[0, pl.ds(begin, rows)], qk_ref[1, low:high], (((1,), (1,)), ((), ())),
                preferred_element_type=jnp.float32,
            )
            return scores * factor + key_bias[:, low:high]

        def weigh(scores, top, low, high):
            weights = bf16(jnp.exp2(scores - top))
            return jnp.dot(weights, v_ref[low:high], preferred_element_type=jnp.float32)

        def finish_rows(begin, rows, both):
            attended[pl.ds(begin, rows)] = bf16(both[:, :head_width] / both[:, head_width:])

        def attend_early(begin, rows):
            scores = scores_of(begin, rows, 0, first_keys)
            top = jnp.max(scores, axis=1, keepdims=True)
            peak[pl.ds(begin, rows)] = jnp.broadcast_to(top, (rows, 128))
            running[pl.ds(begin, rows)] = weigh(scores, top, 0, first_keys)

        def attend_late(begin, rows):
            scores = scores_of(begin, rows, first_keys, slots)
            before = peak[pl.ds(begin, rows)][:, :1]
            top = jnp.maximum(before, jnp.max(scores, axis=1, keepdims=True))
            both = running[pl.ds(begin, rows)] * jnp.exp2(before - top)
            finish_rows(begin, rows, both + weigh(scores, top, first_keys, slots))

        def attend_whole(begin, rows):
            scores = scores_of(begin, rows, 0, slots)
            finish_rows(begin, rows, weigh(scores, jnp.max(scores, axis=1, keepdims=True), 0, slots))

        def send_back(group):
            for step in (2, 3, 1):
                back(group, step).start()
            back_own(group).start()

        def collect(group):
            back_own(group).wait()
            for step in range(1, ctx_count):
                back(group, step).wait_recv()

        span = ctx_count * plane_rows // 2
        for group in range(GROUPS):
            dealt_in(group, 1)
            dealt_in(group, 2)
        for group in range(GROUPS):
            dealt_in(group, 0)
            attend_early(2 * group * span, span)
            attend_early((2 * group + 1) * span, span)
        for kind in range(kinds):
            dealt_in(GROUPS, kind)
        attend_whole(first_keys, ctx_count * TAIL)
        send_back(2)
        for group in range(GROUPS):
            attend_late(2 * group * span, span)
            attend_late((2 * group + 1) * span, span)
            send_back(group)
        fetch_projection.wait()
        collect(2)
        packed = inward[2, :TAIL]
        grouped = bf16(lax.dot_general(grouped_choice, packed, unpack, preferred_element_type=jnp.float32))
        extra = bf16(lax.dot_general(shared_choice, packed, unpack, preferred_element_type=jnp.float32))
        rows = jnp.concatenate([grouped[:tail_count], extra], axis=0)
        for block in range(blocks):
            cols = slice(block * block_width, (block + 1) * block_width)
            values = bf16(jnp.dot(rows, proj_ref[:, cols], preferred_element_type=jnp.float32))
            tail_shares[:, :, cols] = values[:tail_count].reshape(chips, GROUP, block_width)
            ret_in[block] = values[tail_count:]
        reduce_back.level_one()
        row_sums[2].begin()
        reduce_back.level_two()
        row_sums[2].chip()

        def project_back(g):
            for block in range(blocks):
                cols = slice(block * block_width, (block + 1) * block_width)
                values = moved(inward[g], proj_ref[:, cols])
                shares[g, :, :, cols] = values.reshape(seq_count, GROUP, block_width)

        collect(0)
        project_back(0)
        row_sums[0].begin()
        reduce_back.level_three()
        row_sums[2].relay()
        row_sums[0].chip()
        reduce_back.total()
        for step in range(1, ctx_count):
            cross_back(step).start()
        collect(1)
        project_back(1)
        row_sums[1].begin()
        row_sums[2].end()
        tail_back.start()
        row_sums[0].relay()
        row_sums[1].chip()
        for step in range(1, ctx_count):
            cross_back(step).wait_recv()
        back_spread.begin()
        row_sums[0].end()
        row_sums[1].relay()
        back_spread.forward()
        back_spread.finish()
        slot = f32(lax.broadcasted_iota(jnp.int32, (shared_rows, tok_rows), 0))
        from_shared = bf16(jnp.where(layout.shared_slots(keep_row, rank_row) == slot, 1.0, 0.0))
        from_rows = jnp.concatenate([base_choice, tail_choice], axis=0)
        tail_back.wait_recv()
        back_spread.arrive()
        row_sums[1].end()

        def deliver(part):
            cols = pl.ds(part * early_width, early_width)
            return pltpu.make_async_copy(out_ref.at[:, cols], out_hbm.at[:, cols], out_sems.at[part])

        for block in range(blocks):
            cols = slice(block * block_width, (block + 1) * block_width)
            placed = lax.dot_general(from_shared, final[block], unpack, preferred_element_type=jnp.float32)
            placed = placed + lax.dot_general(
                from_rows, returned[:, cols], unpack, preferred_element_type=jnp.float32
            )
            out_ref[:, cols] = bf16(placed)
            if (block + 1) % (blocks // early) == 0:
                deliver(block // (blocks // early)).start()
        save_embedded.wait()
        for part in range(early):
            deliver(part).wait()
        for g in range(sets):
            for kind in range(kinds):
                for step in range(1, ctx_count):
                    deal(g, kind, step).wait_send()
            row_sums[g].drain()
            for step in range(1, ctx_count):
                back(g, step).wait_send()
        tail_swap.wait_send()
        tail_back.wait_send()
        for step in range(1, ctx_count):
            count_line(step).wait_send()
            cross(step).wait_send()
            cross_back(step).wait_send()
        for step in range(1, seq_count):
            count_plane(step).wait_send()
        for gather in groups + [spread, back_spread]:
            gather.drain()
        reduce_in.drain()
        reduce_back.drain()

    dma = pltpu.SemaphoreType.DMA
    b16 = jnp.bfloat16
    vmem = pl.BlockSpec(memory_space=pltpu.VMEM)
    anywhere = pl.BlockSpec(memory_space=pl.ANY)

    def held(*shape):
        return pltpu.VMEM(shape, b16)

    def pair(*shape):
        return [dma(shape)] * 2

    return pl.pallas_call(
        kernel,
        out_shape=[jax.ShapeDtypeStruct((tok_rows, width), b16)] * 2 + [jax.ShapeDtypeStruct((1,), jnp.int32)],
        in_specs=[vmem] * 7 + [anywhere] * 3,
        out_specs=[anywhere, anywhere, pl.BlockSpec(memory_space=pltpu.SMEM)],
        scratch_shapes=[
            held(tok_rows, width),
            held(*qkv_weight.shape),
            held(*out_weight.shape),
            held(tok_rows, width),
            pltpu.VMEM((seq_count, ctx_count, 8, 128), jnp.int32),
            held(tok_rows, width),
            held(GROUP, width),
            held(GROUPS, seq_count, GROUP, width),
            held(GROUP, width),
            held(GROUP, half_width),
            held(chips, GROUP, width),
            held(blocks, shared_rows, block_width),
            held(8, shared_rows, block_width),
            held(4, shared_rows, block_width),
            held(2, shared_rows, block_width),
            held(2, shared_rows, block_width),
            held(ctx_count - 1, 2, SHARED, block_width),
            held(blocks, SHARED, block_width),
            held(sets * kinds, ctx_count, plane_rows, head_width),
            held(2, slots, head_width),
            held(slots, 2 * head_width),
            pltpu.VMEM((GROUPS * ctx_count * plane_rows, 128), jnp.float32),
            pltpu.VMEM((GROUPS * ctx_count * plane_rows, 2 * head_width), jnp.float32),
            held(slots, head_width),
            held(sets, plane_rows, local_width),
            held(GROUPS, seq_count, GROUP, width),
            held(GROUPS, 4, GROUP, width),
            held(GROUPS, 4, GROUP, width),
        ]
        + [held(GROUPS, 2, GROUP, half_width)] * 4
        + [
            held(BASE + GROUP, width),
            held(chips, GROUP, width),
            held(4, GROUP, half_width),
            held(4, GROUP, half_width),
        ]
        + [held(2, GROUP, quarter)] * 4
        + [
            held(blocks, SHARED, block_width),
            held(8, SHARED, block_width),
            held(4, SHARED, block_width),
            held(2, SHARED, block_width),
            held(blocks, shared_rows, block_width),
            held(tok_rows, width),
        ]
        + [dma((kinds + 3,))]
        + pair(seq_count + ctx_count - 2)
        + pair(sets + 2, 9)
        + pair(7)
        + pair(ctx_count - 1)
        + pair(sets * kinds * (ctx_count - 1))
        + pair(sets * (ctx_count - 1))
        + [dma((sets,))]
        + pair(sets, 10)
        + pair(7)
        + pair(ctx_count - 1)
        + pair(2)
        + [dma((early,))],
        compiler_params=pltpu.CompilerParams(
            collective_id=collective_id, has_side_effects=True, vmem_limit_bytes=60 * 2**20
        ),
    )(modality, keep, positions, frequency, modal_table, gain, bias, tokens, qkv_weight, out_weight)


def local(
    tokens,
    modality,
    keep_mask,
    positions,
    modal_table,
    norm_gain,
    norm_bias,
    qkv_weight,
    out_weight,
    mask_token,
):
    arguments = (
        tokens, modality, keep_mask, positions, modal_table, norm_gain, norm_bias, qkv_weight, out_weight, mask_token,
    )
    seq_count, ctx_count = lax.axis_size("seq"), lax.axis_size("ctx")
    tok_rows, width = tokens.shape
    local_width = qkv_weight.shape[2]
    shaped = seq_count == 8 and ctx_count == 4 and tok_rows == 128 and width % 4096 == 0
    shaped = shaped and local_width == ctx_count * HEAD_DIM
    if shaped:
        half_width = width // 2
        exponents = np.arange(half_width, dtype=np.float64) / half_width
        frequency = jnp.asarray(np.exp(-math.log(10000.0) * exponents).astype(np.float32))[None]
        *done, fits = encode(
            tokens, modality[None], keep_mask[None], positions[None], frequency, modal_table,
            norm_gain[None], norm_bias[None], qkv_weight, out_weight, 11,
        )
        restored, embedded = lax.cond(fits[0] == 1, lambda done, *given: done, lambda done, *given: general(*given), done, *arguments)
        restored, embedded = lax.optimization_barrier((restored, embedded))
    else:
        restored, embedded = general(*arguments)
    return jnp.where((keep_mask == 1)[:, None], f32(embedded) + f32(restored), mask_token[None, :])


def solution(mesh):
    in_specs = (
        P(("seq", "ctx"), None),
        P(("seq", "ctx")),
        P(("seq", "ctx")),
        P(("seq", "ctx")),
        P(),
        P(),
        P(),
        P(None, None, "seq"),
        P("seq", None),
        P(),
    )
    out_specs = P(("seq", "ctx"), None)
    return jax.shard_map(local, mesh=mesh, in_specs=in_specs, out_specs=out_specs, check_vma=False)
```

```python
import math

import jax
import jax.numpy as jnp
import numpy as np
from jax import lax
from jax.experimental import pallas as pl
from jax.experimental.pallas import tpu as pltpu
from jax.sharding import PartitionSpec as P

HEAD_DIM = 128


EPSILON = 1e-06
MESH = pl.DeviceIdType.MESH


def position_table(positions, feature_width):
    half_width = feature_width // 2
    frequency = jnp.exp(-math.log(10000.0) * jnp.arange(half_width, dtype=jnp.float32) / half_width)
    angles = positions.astype(jnp.float32)[:, None] * frequency[None, :]
    return jnp.concatenate([jnp.sin(angles), jnp.cos(angles)], axis=1)


def embed(tokens, modality, positions, modal_table):
    table_rows = jnp.where(modality[:, None] == 1, modal_table[1][None, :], modal_table[0][None, :])
    summed = tokens.astype(jnp.float32) + position_table(positions, tokens.shape[1]) + table_rows
    return summed.astype(jnp.bfloat16)


def layer_norm(embedded, norm_gain, norm_bias):
    values = embedded.astype(jnp.float32)
    row_mean = jnp.mean(values, axis=1, keepdims=True)
    centered = values - row_mean
    row_var = jnp.mean(centered * centered, axis=1, keepdims=True)
    return (centered * lax.rsqrt(row_var + EPSILON) * norm_gain + norm_bias).astype(jnp.bfloat16)


def everyone():
    seq_count, ctx_count = lax.axis_size("seq"), lax.axis_size("ctx")

    def place():
        return lax.axis_index("seq") * ctx_count + lax.axis_index("ctx")

    return seq_count * ctx_count, place, lambda j: {"seq": j // ctx_count, "ctx": lax.rem(j, ctx_count)}


def along(axis):
    return lax.axis_size(axis), lambda: lax.axis_index(axis), lambda j: {axis: j}


def exchange(x, group, source, target, out_shape, collective_id):
    count, place, device_of = group

    def kernel(x_ref, out_ref, send_sem, recv_sem, own_sem):
        me = place()
        barrier = pltpu.get_barrier_semaphore()

        def greet(step, carry):
            peer = lax.rem(me + step, count)
            pl.semaphore_signal(barrier, inc=1, device_id=device_of(peer), device_id_type=MESH)
            return carry

        def push(step):
            peer = lax.rem(me + step, count)
            return pltpu.make_async_remote_copy(
                src_ref=source(x_ref, peer),
                dst_ref=target(out_ref, me),
                send_sem=send_sem.at[step],
                recv_sem=recv_sem.at[step],
                device_id=device_of(peer),
                device_id_type=MESH,
            )

        def start(step, carry):
            push(step).start()
            return carry

        def finish(step, carry):
            push(step).wait()
            return carry

        lax.fori_loop(1, count, greet, 0)
        own = pltpu.make_async_copy(source(x_ref, me), target(out_ref, me), own_sem)
        own.start()
        pl.semaphore_wait(barrier, count - 1)
        lax.fori_loop(1, count, start, 0)
        lax.fori_loop(1, count, finish, 0)
        own.wait()

    return pl.pallas_call(
        kernel,
        out_shape=jax.ShapeDtypeStruct(out_shape, x.dtype),
        in_specs=[pl.BlockSpec(memory_space=pltpu.VMEM)],
        out_specs=pl.BlockSpec(memory_space=pltpu.VMEM),
        scratch_shapes=[
            pltpu.SemaphoreType.DMA((count,)),
            pltpu.SemaphoreType.DMA((count,)),
            pltpu.SemaphoreType.DMA,
        ],
        compiler_params=pltpu.CompilerParams(collective_id=collective_id, has_side_effects=True),
    )(x)


CHUNKS = 4


def remote(src, dst, sems, at, device):
    send_sem, recv_sem = sems
    return pltpu.make_async_remote_copy(
        src_ref=src,
        dst_ref=dst,
        send_sem=send_sem.at[at],
        recv_sem=recv_sem.at[at],
        device_id=device,
        device_id_type=MESH,
    )


def aligned(start, size):
    return pl.ds(pl.multiple_of(start * size, size), size)


def greet_line_and_plane(seq_count, ctx_count):
    me, level = lax.axis_index("seq"), lax.axis_index("ctx")
    barrier = pltpu.get_barrier_semaphore()
    for step in range(1, seq_count):
        peer = {"seq": lax.rem(me + step, seq_count)}
        pl.semaphore_signal(barrier, inc=1, device_id=peer, device_id_type=MESH)
    for step in range(1, ctx_count):
        peer = {"ctx": lax.rem(level + step, ctx_count)}
        pl.semaphore_signal(barrier, inc=1, device_id=peer, device_id_type=MESH)
    pl.semaphore_wait(barrier, seq_count + ctx_count - 2)


def regrouping(capacity, outer, inner, slot_count):
    row = lax.broadcasted_iota(jnp.int32, (capacity, capacity), 0)
    column = lax.broadcasted_iota(jnp.int32, (capacity, capacity), 1)
    first = row // (inner * slot_count)
    second = row // slot_count % inner
    wanted = (second * outer + first) * slot_count + row % slot_count
    return (column == wanted).astype(jnp.bfloat16)


def moved(choice, rows):
    return jnp.dot(choice, rows, preferred_element_type=jnp.float32).astype(jnp.bfloat16)


def spread_rows(outgoing, choice, qkv_weight, slot_count, collective_id):
    capacity, width = outgoing.shape
    rows = choice.shape[0]
    half = rows // 2
    seq_count, ctx_count = lax.axis_size("seq"), lax.axis_size("ctx")
    line_rows, plane_rows = capacity // ctx_count, capacity // seq_count
    part_width = width // CHUNKS

    kinds, _, local_width = qkv_weight.shape

    def kernel(
        x_ref, choice_ref, w_hbm, triple_ref, mid, ordered, arrived, out_ref, w_ref, total,
        zs, zr, ps, pr, gs, gr, own_sem, own_sems, w_sems,
    ):
        me, level = lax.axis_index("seq"), lax.axis_index("ctx")
        sibling, left, down = flip(me, 1), flip(me, 2), flip(me, 4)
        across = flip(left, 4)
        all_rows, first, second = pl.ds(0, rows), pl.ds(0, half), pl.ds(half, half)
        along_line, over_plane, gathering = (zs, zr), (ps, pr), (gs, gr)

        def cols(k):
            return pl.ds(k * part_width, part_width)

        def line(k, step):
            peer = lax.rem(level + step, ctx_count)
            src = x_ref.at[aligned(peer, line_rows), cols(k)]
            dst = mid.at[aligned(level, line_rows), cols(k)]
            return remote(src, dst, along_line, (k, step), {"ctx": peer})

        def plane(k, step):
            peer = lax.rem(me + step, seq_count)
            src = ordered.at[aligned(peer, plane_rows), cols(k)]
            dst = arrived.at[aligned(me, plane_rows), cols(k)]
            return remote(src, dst, over_plane, (k, step), {"seq": peer})

        def plane_own(k):
            here = aligned(me, plane_rows)
            return pltpu.make_async_copy(ordered.at[here, cols(k)], arrived.at[here, cols(k)], own_sems.at[k])

        moves = (
            (me, all_rows, sibling),
            (me, all_rows, left),
            (me, all_rows, down),
            (left, first, down),
            (down, second, left),
            (left, all_rows, sibling),
            (down, all_rows, sibling),
            (across, first, sibling),
            (across, second, sibling),
        )

        def hand(k, at):
            origin, which, place = moves[at]
            ref = out_ref.at[origin, which, cols(k)]
            return remote(ref, ref, gathering, (k, at), {"seq": place})

        def fetch(k):
            return pltpu.make_async_copy(w_hbm.at[:, cols(k), :], w_ref.at[:, cols(k), :], w_sems.at[k])

        greet_line_and_plane(seq_count, ctx_count)
        for k in range(CHUNKS):
            for step in range(1, ctx_count):
                line(k, step).start()
        for k in range(CHUNKS):
            fetch(k).start()
        here = aligned(level, line_rows)
        own = pltpu.make_async_copy(x_ref.at[here], mid.at[here], own_sem)
        own.start()
        regroup = regrouping(capacity, seq_count, ctx_count, slot_count)
        own.wait()
        for turn in range(CHUNKS + 4):
            k = turn - 4
            if 0 <= k < CHUNKS:
                for at in (0, 5, 6, 7, 8):
                    hand(k, at).wait_recv()
                fetch(k).wait()
                gathered = out_ref[:, :, cols(k)].reshape(seq_count * rows, part_width)
                for kind in range(kinds):
                    term = jnp.dot(gathered, w_ref[kind, cols(k), :], preferred_element_type=jnp.float32)
                    if k == 0:
                        total[kind] = term
                    elif k < CHUNKS - 1:
                        total[kind] += term
                    else:
                        triple_ref[kind] = (total[kind] + term).astype(jnp.bfloat16)
            k = turn - 3
            if 0 <= k < CHUNKS:
                hand(k, 3).wait_recv()
                hand(k, 7).start()
                hand(k, 4).wait_recv()
                hand(k, 8).start()
            k = turn - 2
            if 0 <= k < CHUNKS:
                hand(k, 1).wait_recv()
                hand(k, 3).start()
                hand(k, 5).start()
                hand(k, 2).wait_recv()
                hand(k, 4).start()
                hand(k, 6).start()
            k = turn - 1
            if 0 <= k < CHUNKS:
                for step in range(1, seq_count):
                    plane(k, step).wait_recv()
                plane_own(k).wait()
                out_ref[me, :, cols(k)] = moved(choice_ref[...], arrived[:, cols(k)])
                for at in (1, 2, 0):
                    hand(k, at).start()
            k = turn
            if k < CHUNKS:
                for step in range(1, ctx_count):
                    line(k, step).wait_recv()
                ordered[:, cols(k)] = moved(regroup, mid[:, cols(k)])
                for step in range(1, seq_count):
                    plane(k, step).start()
                plane_own(k).start()
        for k in range(CHUNKS):
            for at in range(9):
                hand(k, at).wait_send()
            for step in range(1, seq_count):
                plane(k, step).wait_send()
            for step in range(1, ctx_count):
                line(k, step).wait_send()

    dma = pltpu.SemaphoreType.DMA
    return pl.pallas_call(
        kernel,
        out_shape=jax.ShapeDtypeStruct((kinds, seq_count * rows, local_width), jnp.bfloat16),
        in_specs=[pl.BlockSpec(memory_space=pltpu.VMEM)] * 2 + [pl.BlockSpec(memory_space=pl.ANY)],
        out_specs=pl.BlockSpec(memory_space=pltpu.VMEM),
        scratch_shapes=[pltpu.VMEM((capacity, width), jnp.bfloat16)] * 3
        + [
            pltpu.VMEM((seq_count, rows, width), jnp.bfloat16),
            pltpu.VMEM(qkv_weight.shape, jnp.bfloat16),
            pltpu.VMEM((kinds, seq_count * rows, local_width), jnp.float32),
        ]
        + [dma((CHUNKS, ctx_count))] * 2
        + [dma((CHUNKS, seq_count))] * 2
        + [dma((CHUNKS, 9))] * 2
        + [dma, dma((CHUNKS,)), dma((CHUNKS,))],
        compiler_params=pltpu.CompilerParams(collective_id=collective_id, has_side_effects=True),
    )(outgoing, choice, qkv_weight)


def flip(position, bit):
    return position + bit * (1 - 2 * lax.rem(position // bit, 2))


def return_rows(attended, out_weight, choice, slot_count, collective_id):
    width = out_weight.shape[1]
    capacity, rows = choice.shape
    half = rows // 2
    seq_count, ctx_count = lax.axis_size("seq"), lax.axis_size("ctx")
    line_rows, plane_rows = capacity // ctx_count, capacity // seq_count
    part_width = width // CHUNKS

    def kernel(
        x_ref, w_ref, choice_ref, out_ref, shares, near, sums, from_left, from_down, last, passed, total,
        sorted_rows, arrived, ordered, ss, sr, ps, pr, zs, zr, own_sems, line_sems,
    ):
        me, level = lax.axis_index("seq"), lax.axis_index("ctx")
        sibling, left, down = flip(me, 1), flip(me, 2), flip(me, 4)
        first, second = pl.ds(0, half), pl.ds(half, half)
        summing, over_plane, along_line = (ss, sr), (ps, pr), (zs, zr)

        def cols(k):
            return pl.ds(k * part_width, part_width)

        def at(place, which):
            place = flip(place, 2) if which % 2 else place
            return flip(place, 4) if which // 2 else place

        def over(k, q):
            src = shares.at[aligned(at(sibling, q), rows), cols(k)]
            return remote(src, near.at[q, :, cols(k)], summing, (k, q), {"seq": sibling})

        def far(k, which):
            if which == 0:
                return remote(sums.at[3, first, cols(k)], from_left.at[1, :, cols(k)], summing, (k, 4), {"seq": left})
            if which == 1:
                return remote(sums.at[3, second, cols(k)], from_down.at[1, :, cols(k)], summing, (k, 5), {"seq": down})
            if which == 2:
                return remote(sums.at[1, first, cols(k)], from_left.at[0, :, cols(k)], summing, (k, 6), {"seq": left})
            if which == 3:
                return remote(sums.at[2, second, cols(k)], from_down.at[0, :, cols(k)], summing, (k, 7), {"seq": down})
            if which == 4:
                return remote(passed.at[0, :, cols(k)], last.at[0, :, cols(k)], summing, (k, 8), {"seq": down})
            return remote(passed.at[1, :, cols(k)], last.at[1, :, cols(k)], summing, (k, 9), {"seq": left})

        def plane(k, step):
            peer = lax.rem(me + step, seq_count)
            src = sorted_rows.at[aligned(peer, plane_rows), cols(k)]
            dst = arrived.at[aligned(me, plane_rows), cols(k)]
            return remote(src, dst, over_plane, (k, step), {"seq": peer})

        def plane_own(k):
            here = aligned(me, plane_rows)
            return pltpu.make_async_copy(sorted_rows.at[here, cols(k)], arrived.at[here, cols(k)], own_sems.at[k])

        def line(k, step):
            peer = lax.rem(level + step, ctx_count)
            src = ordered.at[aligned(peer, line_rows), cols(k)]
            dst = out_ref.at[aligned(level, line_rows), cols(k)]
            return remote(src, dst, along_line, (k, step), {"ctx": peer})

        def line_own(k):
            here = aligned(level, line_rows)
            return pltpu.make_async_copy(ordered.at[here, cols(k)], out_ref.at[here, cols(k)], line_sems.at[k])

        def wide(value):
            return value.astype(jnp.float32)

        def narrow(value):
            return value.astype(jnp.bfloat16)

        greet_line_and_plane(seq_count, ctx_count)
        regroup = regrouping(capacity, ctx_count, seq_count, slot_count)
        order = (3, 1, 2, 0)
        for turn in range(CHUNKS + 4):
            k = turn - 4
            if 0 <= k < CHUNKS:
                for step in range(1, seq_count):
                    plane(k, step).wait_recv()
                plane_own(k).wait()
                ordered[:, cols(k)] = moved(regroup, arrived[:, cols(k)])
                for step in range(1, ctx_count):
                    line(k, step).start()
                line_own(k).start()
            k = turn - 3
            if 0 <= k < CHUNKS:
                c = cols(k)
                far(k, 2).wait_recv()
                far(k, 4).wait_recv()
                total[:half, c] = narrow(wide(sums[0, :half, c]) + wide(from_left[0, :, c]) + wide(last[0, :, c]))
                far(k, 3).wait_recv()
                far(k, 5).wait_recv()
                total[half:, c] = narrow(wide(sums[0, half:, c]) + wide(from_down[0, :, c]) + wide(last[1, :, c]))
                sorted_rows[:, c] = moved(choice_ref[...], total[:, c])
                for step in range(1, seq_count):
                    plane(k, step).start()
                plane_own(k).start()
            k = turn - 2
            if 0 <= k < CHUNKS:
                c = cols(k)
                far(k, 0).wait_recv()
                passed[0, :, c] = narrow(wide(sums[2, :half, c]) + wide(from_left[1, :, c]))
                far(k, 4).start()
                far(k, 1).wait_recv()
                passed[1, :, c] = narrow(wide(sums[1, half:, c]) + wide(from_down[1, :, c]))
                far(k, 5).start()
            k = turn - 1
            if 0 <= k < CHUNKS:
                c = cols(k)
                for q in order:
                    over(k, q).wait_recv()
                    mine = shares[aligned(at(me, q), rows), c]
                    sums[q, :, c] = narrow(wide(mine) + wide(near[q, :, c]))
                    if q == 3:
                        far(k, 0).start()
                        far(k, 1).start()
                    if q == 1:
                        far(k, 2).start()
                    if q == 2:
                        far(k, 3).start()
            k = turn
            if k < CHUNKS:
                shares[:, cols(k)] = moved(x_ref[...], w_ref[:, cols(k)])
                for q in order:
                    over(k, q).start()
        for k in range(CHUNKS):
            for step in range(1, ctx_count):
                line(k, step).wait()
            line_own(k).wait()
            for step in range(1, seq_count):
                plane(k, step).wait_send()
            for q in order:
                over(k, q).wait_send()
            for which in range(6):
                far(k, which).wait_send()

    dma = pltpu.SemaphoreType.DMA
    bf16 = jnp.bfloat16
    return pl.pallas_call(
        kernel,
        out_shape=jax.ShapeDtypeStruct((capacity, width), bf16),
        in_specs=[pl.BlockSpec(memory_space=pltpu.VMEM)] * 3,
        out_specs=pl.BlockSpec(memory_space=pltpu.VMEM),
        scratch_shapes=[pltpu.VMEM((seq_count * rows, width), bf16)]
        + [pltpu.VMEM((4, rows, width), bf16)] * 2
        + [pltpu.VMEM((2, half, width), bf16)] * 4
        + [pltpu.VMEM((rows, width), bf16)]
        + [pltpu.VMEM((capacity, width), bf16)] * 3
        + [dma((CHUNKS, 10))] * 2
        + [dma((CHUNKS, seq_count))] * 2
        + [dma((CHUNKS, ctx_count))] * 2
        + [dma((CHUNKS,))] * 2,
        compiler_params=pltpu.CompilerParams(collective_id=collective_id, has_side_effects=True),
    )(attended, out_weight, choice)


def part(ref, j):
    return ref.at[j]


def whole(ref, j):
    return ref


def attend(triple):
    _, heads, rows, _ = triple.shape
    block = min(rows, 256)
    score_scale = 1.0 / math.sqrt(HEAD_DIM)

    def kernel(q_ref, k_ref, v_ref, out_ref):
        scores = (
            lax.dot_general(
                q_ref[...], k_ref[...], (((1,), (1,)), ((), ())), preferred_element_type=jnp.float32
            )
            * score_scale
        )
        expanded = jnp.exp(scores - jnp.max(scores, axis=1, keepdims=True))
        total = jnp.sum(expanded, axis=1, keepdims=True)
        summed = jnp.dot(expanded.astype(jnp.bfloat16), v_ref[...], preferred_element_type=jnp.float32)
        out_ref[...] = (summed / total).astype(jnp.bfloat16)

    return pl.pallas_call(
        kernel,
        grid=(heads, rows // block),
        out_shape=jax.ShapeDtypeStruct((heads, rows, HEAD_DIM), jnp.bfloat16),
        in_specs=[
            pl.BlockSpec((None, None, block, HEAD_DIM), lambda h, i: (0, h, i, 0)),
            pl.BlockSpec((None, None, rows, HEAD_DIM), lambda h, i: (1, h, 0, 0)),
            pl.BlockSpec((None, None, rows, HEAD_DIM), lambda h, i: (2, h, 0, 0)),
        ],
        out_specs=pl.BlockSpec((None, block, HEAD_DIM), lambda h, i: (h, i, 0)),
    )(triple, triple, triple)


def attend_by_head(triple):
    _, group_rows, local_width = triple.shape
    ctx = along("ctx")
    count = ctx[0]
    width = local_width // count
    heads = width // HEAD_DIM
    gathered = exchange(
        triple,
        ctx,
        lambda ref, j: ref.at[:, :, pl.ds(pl.multiple_of(j * width, HEAD_DIM), width)],
        lambda ref, j: ref.at[:, pl.ds(pl.multiple_of(j * group_rows, group_rows), group_rows), :],
        (3, count * group_rows, width),
        3,
    )
    if heads == 1:
        split = gathered[:, None]
    else:
        split = jnp.transpose(
            gathered.reshape(3, count * group_rows, heads, HEAD_DIM), (0, 2, 1, 3)
        )
    done = attend(split)
    if heads == 1:
        done = done[0]
    else:
        done = jnp.transpose(done, (1, 0, 2)).reshape(count * group_rows, width)
    return exchange(
        done,
        ctx,
        lambda ref, j: ref.at[pl.ds(pl.multiple_of(j * group_rows, group_rows), group_rows), :],
        lambda ref, j: ref.at[:, pl.ds(pl.multiple_of(j * width, HEAD_DIM), width)],
        (group_rows, local_width),
        4,
    )


def attend_by_row(triple):
    queries, key_rows, values = (triple[0], triple[1], triple[2])
    group_rows, local_width = queries.shape
    heads_here = local_width // HEAD_DIM
    score_scale = 1.0 / math.sqrt(HEAD_DIM)
    both = lax.all_gather(jnp.stack([key_rows, values]), "ctx", axis=1, tiled=True)
    length = both.shape[1]
    query_heads = queries.reshape(group_rows, heads_here, HEAD_DIM)
    key_heads = both[0].reshape(length, heads_here, HEAD_DIM)
    value_heads = both[1].reshape(length, heads_here, HEAD_DIM)
    scores = (
        jnp.einsum("ghd,khd->hgk", query_heads, key_heads, preferred_element_type=jnp.float32)
        * score_scale
    )
    expanded = jnp.exp(scores - jnp.max(scores, axis=2, keepdims=True))
    total = jnp.sum(expanded, axis=2, keepdims=True)
    summed = jnp.einsum(
        "hgk,khd->hgd",
        expanded.astype(jnp.bfloat16),
        value_heads,
        preferred_element_type=jnp.float32,
    )
    attended = (summed / total).astype(jnp.bfloat16)
    return jnp.transpose(attended, (1, 0, 2)).reshape(group_rows, local_width)


def general(
    tokens,
    modality,
    keep_mask,
    positions,
    modal_table,
    norm_gain,
    norm_bias,
    qkv_weight,
    out_weight,
    mask_token,
):
    tok_rows, feature_width = tokens.shape
    seq_count = lax.axis_size("seq")
    ctx_count = lax.axis_size("ctx")
    devices = seq_count * ctx_count
    slot_count = (tok_rows + devices - 1) // devices
    capacity = devices * slot_count
    own_rows = tok_rows // 4
    my_index = lax.axis_index("seq") * ctx_count + lax.axis_index("ctx")
    visible = keep_mask == 1
    own_count = jnp.sum(keep_mask)
    counts = exchange(
        jnp.full((1, 128), own_count, jnp.int32), everyone(), whole, part, (devices, 1, 128), 0
    )[:, 0, 0]
    index = jnp.arange(devices, dtype=jnp.int32)
    starts = jnp.sum(jnp.where(index[None, :] < index[:, None], counts[None, :], 0), axis=1)
    my_start = jnp.sum(jnp.where(index < my_index, counts, 0))
    token_index = jnp.arange(tok_rows, dtype=jnp.int32)
    local_rank = (
        jnp.sum(jnp.where(token_index[None, :] <= token_index[:, None], keep_mask[None, :], 0), axis=1) - 1
    )
    global_rank = my_start + local_rank
    owner = global_rank % devices
    piped = seq_count == 8 and slot_count * ctx_count % 16 == 0
    if piped:
        owner = owner % ctx_count * seq_count + owner // ctx_count
    token_slot = jnp.where(visible, owner * slot_count + local_rank // devices, capacity)
    slot_index = jnp.arange(capacity, dtype=jnp.int32)
    slot_of_token = (token_slot[:, None] == slot_index[None, :]).astype(jnp.bfloat16)
    slot_place = slot_index % slot_count
    source_start = jnp.repeat(starts, slot_count)
    source_count = jnp.repeat(counts, slot_count)
    offset = (my_index - source_start) % devices + devices * slot_place
    usable = offset < source_count
    slot_row = jnp.where(usable, (source_start + offset) // devices, own_rows)
    row_of_slot = (
        slot_row[:, None] == jnp.arange(own_rows, dtype=jnp.int32)[None, :]
    ).astype(jnp.bfloat16)

    embedded = embed(tokens, modality, positions, modal_table)

    def pick(choice, rows, side):
        return lax.dot_general(
            choice, rows, (((side,), (0,)), ((), ())), preferred_element_type=jnp.float32
        )

    normed = layer_norm(embedded, norm_gain, norm_bias)
    outgoing = pick(slot_of_token, normed, 0).astype(jnp.bfloat16)
    slots = (devices, slot_count, feature_width)
    if piped:
        triple = spread_rows(outgoing, row_of_slot.T, qkv_weight, slot_count, 1)
    else:
        arriving = exchange(outgoing.reshape(slots), everyone(), part, part, slots, 1)
        own_normed = pick(row_of_slot, arriving.reshape(capacity, feature_width), 0).astype(jnp.bfloat16)
        group = exchange(own_normed, along("seq"), whole, part, (seq_count,) + own_normed.shape, 2)
        triple = jnp.einsum(
            "rd,tdc->trc",
            group.reshape(seq_count * own_rows, feature_width),
            qkv_weight,
            preferred_element_type=jnp.float32,
        ).astype(jnp.bfloat16)
    if triple.shape[2] % (ctx_count * HEAD_DIM) == 0:
        attended = attend_by_head(triple)
    else:
        attended = attend_by_row(triple)
    if piped:
        returned = return_rows(attended, out_weight, row_of_slot, slot_count, 5)
    else:
        shares = jnp.dot(attended, out_weight, preferred_element_type=jnp.float32).astype(jnp.bfloat16)
        shares = shares.reshape(seq_count, own_rows, feature_width)
        shares = exchange(shares, along("seq"), part, part, shares.shape, 5)
        projected = jnp.sum(shares.astype(jnp.float32), axis=0).astype(jnp.bfloat16)
        returning = pick(row_of_slot, projected, 1).astype(jnp.bfloat16)
        returned = exchange(returning.reshape(slots), everyone(), part, part, slots, 6)
        returned = returned.reshape(capacity, feature_width)
    restored = pick(slot_of_token, returned, 1)
    return [bf16(restored), embedded]


GROUP = 16
GROUPS = 2
BASE = GROUP * GROUPS
SHARED = 32
TAIL = 64
NEGATIVE = -1e30


def bf16(value):
    return value.astype(jnp.bfloat16)


def f32(value):
    return value.astype(jnp.float32)


def sine_and_cosine(angle):
    turns = jnp.floor(angle * (2.0 / math.pi) + 0.5)
    quarter = turns.astype(jnp.int32)
    r = ((angle - turns * 1.5703125) - turns * 4.837512969970703125e-4) - turns * 7.54978995489188216e-8
    square = r * r
    sine = r + r * square * (-1.6666654611e-1 + square * (8.3321608736e-3 - square * 1.9515295891e-4))
    cosine = (
        1.0
        - 0.5 * square
        + square * square * (4.166664568298827e-2 + square * (-1.388731625493765e-3 + square * 2.443315711809948e-5))
    )
    odd = (quarter & 1) == 1
    first = jnp.where(odd, cosine, sine)
    second = jnp.where(odd, sine, cosine)
    first = jnp.where((quarter & 2) == 2, -first, first)
    second = jnp.where(((quarter + 1) & 2) == 2, -second, second)
    return first, second


def as_column(row, size):
    across = lax.broadcasted_iota(jnp.int32, (size, size), 1)
    down = lax.broadcasted_iota(jnp.int32, (size, size), 0)
    return jnp.sum(jnp.where(across == down, row, 0.0), axis=1, keepdims=True)


def ranks_of(keep_row, size):
    across = lax.broadcasted_iota(jnp.int32, (size, size), 1)
    down = lax.broadcasted_iota(jnp.int32, (size, size), 0)
    column = as_column(keep_row, size)
    return jnp.sum(jnp.where(down < across, column, 0.0), axis=0, keepdims=True)


class Layout:
    def __init__(self, counts, place, level, seq_count, ctx_count):
        lanes = counts.shape[1:]
        cores = (seq_count // 2, 2, ctx_count) + lanes
        extra = jnp.maximum(counts - BASE, 0.0).reshape(cores)
        first = jnp.minimum(extra[:, 0], 1.0 * GROUP)
        second = jnp.minimum(extra[:, 1], GROUP - first)
        of_chip = first + second
        tail_of = jnp.stack([first, second], axis=1).reshape(counts.shape)
        over = extra.reshape(counts.shape) - tail_of
        index = lax.broadcasted_iota(jnp.int32, counts.shape, 0)
        self.over_start = jnp.sum(jnp.where(index < place, over, 0.0), axis=0)
        self.own_tail = jnp.sum(jnp.where(index == place, tail_of, 0.0), axis=0)
        before = jnp.sum(jnp.where(index == place - ctx_count, tail_of, 0.0), axis=0)
        self.own_start = jnp.where(lax.rem(place // ctx_count, 2) == 1, before, 0.0)
        total = jnp.sum(over, axis=0)
        tails, free, starts = [], [], []
        running = jnp.zeros(lanes, jnp.float32)
        for z in range(ctx_count):
            tail = jnp.sum(of_chip[:, z], axis=0)
            room = jnp.clip(TAIL - tail, 0.0, 1.0 * SHARED)
            tails.append(tail)
            free.append(room)
            starts.append(running)
            running = running + room
        self.fits = jnp.where(total > running, 0.0, 1.0)
        self.tails, self.free, self.starts = tails, free, starts
        self.used = [jnp.clip(total - starts[z], 0.0, free[z]) for z in range(ctx_count)]
        by_plane = counts.reshape((seq_count, ctx_count) + lanes)
        seat = lax.broadcasted_iota(jnp.int32, by_plane.shape, 0)
        lane = lax.broadcasted_iota(jnp.int32, by_plane.shape, 3)
        self.lane_counts = jnp.sum(jnp.where(lane // GROUP == seat, by_plane, 0.0), axis=0)
        seat = lax.broadcasted_iota(jnp.int32, of_chip.shape, 0)
        lane = lax.broadcasted_iota(jnp.int32, of_chip.shape, 3)
        self.lane_tails = jnp.sum(jnp.where(lane // GROUP == seat, of_chip, 0.0), axis=0)
        self.lane_tail_start = jnp.sum(jnp.where(seat < lane // GROUP, of_chip, 0.0), axis=0)

    def of_level(self, values, level):
        out = values[0]
        for z in range(1, len(values)):
            out = jnp.where(level == z, values[z], out)
        return out

    def shared_slots(self, keep_row, rank_row):
        beyond = rank_row - BASE - self.own_tail[0:1]
        ordinal = self.over_start[0:1] + beyond
        slot = jnp.full(ordinal.shape, -1.0, jnp.float32)
        for z in range(len(self.free)):
            here = (ordinal >= self.starts[z][0:1]) & (ordinal < self.starts[z][0:1] + self.free[z][0:1])
            slot = jnp.where(here, ordinal - self.starts[z][0:1] + SHARED * z, slot)
        return jnp.where((keep_row > 0.0) & (beyond >= 0.0), slot, -1.0)

    def tail_slots(self, keep_row, rank_row):
        ordinal = rank_row - BASE
        valid = (keep_row > 0.0) & (ordinal >= 0.0) & (ordinal < self.own_tail[0:1])
        return jnp.where(valid, ordinal + self.own_start[0:1], -1.0)

    def tail_choice(self, level):
        counts = self.of_level([self.lane_tails[z] for z in range(len(self.free))], level)[0:1]
        start = self.of_level([self.lane_tail_start[z] for z in range(len(self.free))], level)[0:1]
        tail = self.of_level(self.tails, level)[0:1]
        used = self.of_level(self.used, level)[0:1]
        size = (TAIL, counts.shape[1])
        target = f32(lax.broadcasted_iota(jnp.int32, size, 0))
        lane = lax.broadcasted_iota(jnp.int32, size, 1)
        within = f32(lane % GROUP)
        valid = counts > within
        grouped = bf16(jnp.where(valid & (start + within == target), 1.0, 0.0))
        where = f32(lane)
        shared = bf16(jnp.where((where < used) & (tail + where == target), 1.0, 0.0))
        return grouped, shared[:, :SHARED]

    def key_bias(self):
        width = self.lane_counts.shape[2]
        within = f32(lax.broadcasted_iota(jnp.int32, (1, width), 1) % GROUP)
        parts = []
        for group in range(GROUPS):
            for z in range(len(self.free)):
                parts.append(jnp.where(self.lane_counts[z][0:1] > within + group * GROUP, 0.0, NEGATIVE))
        slot = f32(lax.broadcasted_iota(jnp.int32, (1, width), 1))
        for z in range(0, len(self.free), 2):
            low = self.tails[z][0:1] + self.used[z][0:1]
            high = self.tails[z + 1][0:1] + self.used[z + 1][0:1]
            limit = jnp.where(slot < TAIL, low, high + TAIL)
            parts.append(jnp.where(slot < limit, 0.0, NEGATIVE))
        return jnp.concatenate(parts, axis=1)


class Plane:
    def __init__(self):
        self.me = lax.axis_index("seq")
        self.level = lax.axis_index("ctx")
        self.sibling, self.left, self.down = flip(self.me, 1), flip(self.me, 2), flip(self.me, 4)
        self.across = flip(self.left, 4)

    def order(self, seat):
        core, x, y = lax.rem(seat, 2), lax.rem(seat // 2, 2), seat // 4
        return core * 4 + y * 2 + x


class Gather:
    def __init__(self, plane, halves, sems, at):
        self.plane, self.halves, self.sems, self.at = plane, halves, sems, at

    def moves(self):
        p = self.plane
        out = []
        for origin, half, place in (
            (p.me, None, p.left),
            (p.me, None, p.down),
            (p.me, None, p.sibling),
            (p.left, 0, p.down),
            (p.down, 1, p.left),
            (p.left, None, p.sibling),
            (p.down, None, p.sibling),
            (p.across, 0, p.sibling),
            (p.across, 1, p.sibling),
        ):
            out.append((self.halves(origin, half), place))
        return out

    def copy(self, move):
        ref, place = self.moves()[move]
        return remote(ref, ref, self.sems, (self.at, move), {"seq": place})

    def begin(self):
        for move in (0, 1, 2):
            self.copy(move).start()

    def forward(self):
        self.copy(0).wait_recv()
        self.copy(3).start()
        self.copy(5).start()
        self.copy(1).wait_recv()
        self.copy(4).start()
        self.copy(6).start()

    def finish(self):
        self.copy(3).wait_recv()
        self.copy(7).start()
        self.copy(4).wait_recv()
        self.copy(8).start()

    def arrive(self):
        for move in (2, 5, 6, 7, 8):
            self.copy(move).wait_recv()

    def drain(self):
        for move in range(9):
            self.copy(move).wait_send()


class BlockSum:
    def __init__(self, plane, source, first, second, third, result, sems):
        self.plane, self.sems = plane, sems
        self.source, self.first, self.second, self.third, self.result = source, first, second, third, result

    def block(self, seat, half):
        return 2 * (lax.rem(seat // 2, 2) + 2 * (seat // 4)) + half

    def copies(self):
        p = self.plane
        core = lax.rem(p.me, 2)
        out = [(self.source.at[pl.ds(8 * (1 - core), 8)], self.first, p.sibling)]
        mine = 8 * core
        out.append((self.source.at[mine + self.block(p.across, 0)], self.second.at[0], p.left))
        out.append((self.source.at[mine + self.block(p.left, 0)], self.second.at[1], p.left))
        out.append((self.source.at[mine + self.block(p.across, 1)], self.second.at[2], p.down))
        out.append((self.source.at[mine + self.block(p.down, 1)], self.second.at[3], p.down))
        out.append((self.source.at[mine + self.block(p.down, 0)], self.third.at[0], p.down))
        out.append((self.source.at[mine + self.block(p.left, 1)], self.third.at[1], p.left))
        return out

    def copy(self, at):
        src, dst, place = self.copies()[at]
        return remote(src, dst, self.sems, (at,), {"seq": place})

    def level_one(self):
        self.copy(0).start()

    def level_two(self):
        core = lax.rem(self.plane.me, 2)
        self.copy(0).wait_recv()
        for block in range(8):
            at = 8 * core + block
            self.source[at] = self.source[at] + self.first[block]
        for at in (1, 2, 3, 4):
            self.copy(at).start()

    def level_three(self):
        p = self.plane
        mine = 8 * lax.rem(p.me, 2)
        self.copy(1).wait_recv()
        at = mine + self.block(p.down, 0)
        self.source[at] = self.source[at] + self.second[0]
        self.copy(5).start()
        self.copy(3).wait_recv()
        at = mine + self.block(p.left, 1)
        self.source[at] = self.source[at] + self.second[2]
        self.copy(6).start()

    def total(self):
        p = self.plane
        mine = 8 * lax.rem(p.me, 2)
        self.copy(2).wait_recv()
        self.copy(5).wait_recv()
        first = self.source[mine + self.block(p.me, 0)]
        self.result[0] = first + self.second[1] + self.third[0]
        self.copy(4).wait_recv()
        self.copy(6).wait_recv()
        second = self.source[mine + self.block(p.me, 1)]
        self.result[1] = second + self.second[3] + self.third[1]

    def drain(self):
        for at in range(7):
            self.copy(at).wait_send()


class RowSum:
    def __init__(self, plane, given, mine, near, sums, from_left, from_down, last, passed, store, sems, at):
        self.plane, self.given, self.mine, self.near, self.sums = plane, given, mine, near, sums
        self.from_left, self.from_down, self.last, self.passed = from_left, from_down, last, passed
        self.store, self.sems, self.at = store, sems, at
        self.half = passed.shape[-1]

    def over(self, q):
        return remote(self.given(q), self.near.at[q], self.sems, (self.at, q), {"seq": self.plane.sibling})

    def far(self, which):
        low, high = pl.ds(0, self.half), pl.ds(self.half, self.half)
        left, down = self.plane.left, self.plane.down
        src, dst, to = (
            (self.sums.at[3, :, low], self.from_left.at[1], left),
            (self.sums.at[3, :, high], self.from_down.at[1], down),
            (self.sums.at[1, :, low], self.from_left.at[0], left),
            (self.sums.at[2, :, high], self.from_down.at[0], down),
            (self.passed.at[0], self.last.at[0], down),
            (self.passed.at[1], self.last.at[1], left),
        )[which]
        return remote(src, dst, self.sems, (self.at, 4 + which), {"seq": to})

    def begin(self):
        for q in (3, 1, 2, 0):
            self.over(q).start()

    def chip(self):
        for q in (3, 1, 2, 0):
            self.over(q).wait_recv()
            self.sums[q] = self.mine(q) + self.near[q]
            if q == 3:
                self.far(0).start()
                self.far(1).start()
            if q == 1:
                self.far(2).start()
            if q == 2:
                self.far(3).start()

    def relay(self):
        self.far(0).wait_recv()
        self.passed[0] = bf16(f32(self.sums[2, :, : self.half]) + f32(self.from_left[1]))
        self.far(4).start()
        self.far(1).wait_recv()
        self.passed[1] = bf16(f32(self.sums[1, :, self.half :]) + f32(self.from_down[1]))
        self.far(5).start()

    def end(self):
        self.far(2).wait_recv()
        self.far(4).wait_recv()
        self.store(0, bf16(f32(self.sums[0, :, : self.half]) + f32(self.from_left[0]) + f32(self.last[0])))
        self.far(3).wait_recv()
        self.far(5).wait_recv()
        self.store(1, bf16(f32(self.sums[0, :, self.half :]) + f32(self.from_down[0]) + f32(self.last[1])))

    def drain(self):
        for q in range(4):
            self.over(q).wait_send()
        for which in range(6):
            self.far(which).wait_send()


def counts_of(ref, seq_count, ctx_count):
    return f32(ref[...].reshape((seq_count * ctx_count,) + ref.shape[2:]))


def embedded_rows(tokens, waves, taxel, table):
    return bf16(tokens + waves + jnp.where(taxel, table[1:2], table[0:1]))


def encode(tokens, modality, keep, positions, frequency, modal_table, gain, bias, qkv_weight, out_weight, collective_id):
    seq_count, ctx_count = lax.axis_size("seq"), lax.axis_size("ctx")
    tok_rows, width = tokens.shape
    kinds, _, local_width = qkv_weight.shape
    head_width = local_width // ctx_count
    blocks = 16
    block_width = width // blocks
    plane_rows = seq_count * GROUP
    slots = ctx_count * (2 * plane_rows + TAIL)
    half_width = width // 2
    shared_rows = ctx_count * SHARED
    score_scale = 1.0 / math.sqrt(HEAD_DIM)
    early = 4
    early_width = width // early

    quarter = width // 4
    chips = seq_count // 2
    sets = GROUPS + 1

    def kernel(
        mod_ref, keep_ref, pos_ref, freq_ref, table_ref, gain_ref, bias_ref, tok_hbm, w_hbm, proj_hbm,
        out_hbm, emb_hbm, fits_ref,
        tok_ref, w_ref, proj_ref, emb_ref, cnt_ref, normed, opening, gathered, tail_own, tail_in, tail,
        shared_in, first, second, third, summed, crossed, shared, staged, qk_ref, v_ref, peak, running,
        attended, inward, shares, near, sums, from_left, from_down, last, passed, returned,
        tail_shares, tail_near, tail_sums, tail_left, tail_down, tail_last, tail_passed,
        ret_in, ret_first, ret_second, ret_third, final, out_ref,
        w_sems, cs, cr, gs, gr, bs, br, xs, xr, ds, dr,
        fs, fr, back_sems, ss, sr, rs, rr, ys, yr, ts, tr, out_sems,
    ):
        plane = Plane()
        me, level = plane.me, plane.level
        sibling, left, down = plane.sibling, plane.left, plane.down
        unpack = (((0,), (0,)), ((), ()))

        def fetch(kind):
            return pltpu.make_async_copy(w_hbm.at[kind], w_ref.at[kind], w_sems.at[kind])

        save_embedded = pltpu.make_async_copy(emb_ref, emb_hbm, w_sems.at[kinds + 2])
        fetch_tokens = pltpu.make_async_copy(tok_hbm, tok_ref, w_sems.at[kinds])
        fetch_projection = pltpu.make_async_copy(proj_hbm, proj_ref, w_sems.at[kinds + 1])

        def count_line(step):
            peer = lax.rem(level + step, ctx_count)
            ref = cnt_ref.at[me, level]
            return remote(ref, ref, (cs, cr), (step - 1,), {"ctx": peer})

        def count_plane(step):
            peer = lax.rem(me + step, seq_count)
            ref = cnt_ref.at[me]
            return remote(ref, ref, (cs, cr), (ctx_count - 2 + step,), {"seq": peer})

        def piece(group):
            def halves(origin, half):
                ref = gathered.at[group, origin]
                if half is None:
                    return ref
                return ref.at[:, pl.ds(half * half_width, half_width)]

            return halves

        def blocks_of(ref):
            def halves(origin, half):
                start = 2 * plane.order(origin)
                if half is None:
                    return ref.at[pl.ds(start, 2)]
                return ref.at[start + half]

            return halves

        def tail_piece(origin, half):
            start = lax.rem(origin, 2) * half_width + (half or 0) * quarter
            cols = pl.ds(pl.multiple_of(start, quarter), half_width if half is None else quarter)
            return tail.at[origin // 2, :, cols]

        groups = [Gather(plane, piece(g), (gs, gr), g) for g in range(GROUPS)]
        groups.append(Gather(plane, tail_piece, (gs, gr), GROUPS))
        spread = Gather(plane, blocks_of(shared), (gs, gr), GROUPS + 1)
        back_spread = Gather(plane, blocks_of(final), (gs, gr), GROUPS + 2)
        core = lax.rem(me, 2)
        my_half, other_half = aligned(core, half_width), aligned(1 - core, half_width)
        tail_swap = remote(tail_own.at[:, other_half], tail_in, (ts, tr), (0,), {"seq": sibling})
        tail_rows = pl.ds(BASE, GROUP)
        tail_result = returned.at[tail_rows, my_half]
        tail_back = remote(tail_result, tail_result, (ts, tr), (1,), {"seq": sibling})
        reduce_in = BlockSum(plane, shared_in, first, second, third, summed, (bs, br))

        def cross(step):
            peer = lax.rem(level + step, ctx_count)
            src = summed.at[:, aligned(peer, SHARED), :]
            return remote(src, crossed.at[step - 1], (xs, xr), (step - 1,), {"ctx": peer})

        def rows_of(group):
            return plane_rows if group < 2 else TAIL

        def slot_start(group, z):
            return pl.multiple_of(group * ctx_count * plane_rows + z * rows_of(group), GROUP)

        def dealt(kind, start, rows):
            here = pl.ds(pl.multiple_of(start, GROUP), rows)
            if kind == 2:
                return v_ref.at[here, pl.ds(0, head_width)]
            return qk_ref.at[kind, here]

        def deal(group, kind, step):
            peer = lax.rem(level + step, ctx_count)
            src = staged.at[group * kinds + kind, peer, pl.ds(0, rows_of(group))]
            at = (group * kinds + kind) * (ctx_count - 1) + step - 1
            return remote(src, dealt(kind, slot_start(group, level), rows_of(group)), (ds, dr), (at,), {"ctx": peer})

        def place(which_seat, which):
            seat = flip(which_seat, 2) if which % 2 else which_seat
            return flip(seat, 4) if which // 2 else seat

        def row_sum(g):
            def store(side, value):
                returned[g * GROUP : (g + 1) * GROUP, side * half_width : (side + 1) * half_width] = value

            return RowSum(
                plane, lambda q: shares.at[g, place(sibling, q)], lambda q: shares[g, place(me, q)], near.at[g],
                sums.at[g], from_left.at[g], from_down.at[g], last.at[g], passed.at[g], store, (ss, sr), g,
            )

        def store_tail(side, value):
            start = pl.multiple_of(core * half_width + side * quarter, quarter)
            returned[tail_rows, pl.ds(start, quarter)] = value

        row_sums = [row_sum(g) for g in range(GROUPS)]
        row_sums.append(
            RowSum(
                plane, lambda q: tail_shares.at[place(me, q) // 2, :, other_half],
                lambda q: tail_shares[place(me, q) // 2, :, my_half], tail_near,
                tail_sums, tail_left, tail_down, tail_last, tail_passed, store_tail, (ss, sr), GROUPS,
            )
        )

        def back(group, step):
            peer = lax.rem(level + step, ctx_count)
            src = attended.at[pl.ds(slot_start(group, peer), rows_of(group))]
            dst = inward.at[group, pl.ds(0, rows_of(group)), aligned(level, head_width)]
            return remote(src, dst, (fs, fr), (group * (ctx_count - 1) + step - 1,), {"ctx": peer})

        def back_own(group):
            src = attended.at[pl.ds(slot_start(group, level), rows_of(group))]
            dst = inward.at[group, pl.ds(0, rows_of(group)), aligned(level, head_width)]
            return pltpu.make_async_copy(src, dst, back_sems.at[group])

        own_start = 2 * plane.order(me)

        def cross_back(step):
            peer = lax.rem(level + step, ctx_count)
            ref = final.at[pl.ds(own_start, 2), aligned(level, SHARED), :]
            return remote(ref, ref, (ys, yr), (step - 1,), {"ctx": peer})

        class Result:
            def __setitem__(self, half, value):
                final[own_start + half, aligned(level, SHARED), :] = value

        reduce_back = BlockSum(plane, ret_in, ret_first, ret_second, ret_third, Result(), (rs, rr))

        fetch_tokens.start()
        barrier = pltpu.get_barrier_semaphore()
        for step in range(1, seq_count):
            peer = {"seq": lax.rem(me + step, seq_count)}
            pl.semaphore_signal(barrier, inc=1, device_id=peer, device_id_type=MESH)
        for step in range(1, ctx_count):
            peer = {"ctx": lax.rem(level + step, ctx_count)}
            pl.semaphore_signal(barrier, inc=1, device_id=peer, device_id_type=MESH)
        keep_row = f32(keep_ref[...])
        place_row, taxel_row = f32(pos_ref[...]), f32(mod_ref[...])
        own_count = jnp.sum(keep_row, axis=1, keepdims=True).astype(jnp.int32)
        cnt_ref[me, level] = jnp.broadcast_to(own_count, cnt_ref.shape[2:])
        rank_row = ranks_of(keep_row, tok_rows)
        slot = f32(lax.broadcasted_iota(jnp.int32, (BASE, tok_rows), 0))
        base_pick = jnp.where((keep_row > 0.0) & (rank_row == slot), 1.0, 0.0)
        base_choice = bf16(base_pick)

        opening_pick = base_pick[:GROUP]
        opening_place = jnp.sum(opening_pick * place_row, axis=1, keepdims=True)
        opening_taxel = jnp.sum(opening_pick * taxel_row, axis=1, keepdims=True) > 0.5
        total = jnp.zeros((GROUP, 1), jnp.float32)
        fetch_tokens.wait()
        for part in range(early // 2):
            waves = sine_and_cosine(opening_place * freq_ref[:, part * early_width : (part + 1) * early_width])
            for side in range(2):
                start = side * half_width + part * early_width
                cols = slice(start, start + early_width)
                rows = jnp.dot(base_choice[:GROUP], tok_ref[:, cols], preferred_element_type=jnp.float32)
                rounded = embedded_rows(rows, waves[side], opening_taxel, table_ref[:, cols])
                opening[:, cols] = rounded
                total = total + jnp.sum(f32(rounded), axis=1, keepdims=True)
        mean = total * (1.0 / width)
        total = jnp.zeros((GROUP, 1), jnp.float32)
        for part in range(early):
            centered = f32(opening[:, part * early_width : (part + 1) * early_width]) - mean
            total = total + jnp.sum(centered * centered, axis=1, keepdims=True)
        scale = lax.rsqrt(total * (1.0 / width) + EPSILON)
        for part in range(early):
            cols = slice(part * early_width, (part + 1) * early_width)
            gathered[0, me, :, cols] = bf16((f32(opening[:, cols]) - mean) * scale * gain_ref[:, cols] + bias_ref[:, cols])
        pl.semaphore_wait(barrier, seq_count + ctx_count - 2)
        groups[0].begin()
        for step in range(1, ctx_count):
            count_line(step).start()

        def project(rows, kind):
            return bf16(jnp.dot(rows, w_ref[kind], preferred_element_type=jnp.float32))

        def send(group, kind, values):
            rows = rows_of(group)
            for z in range(ctx_count):
                staged[group * kinds + kind, z, :rows] = values[:, z * head_width : (z + 1) * head_width]
            dealt(kind, slot_start(group, level), rows)[...] = staged[group * kinds + kind, level, :rows]
            for step in (2, 3, 1):
                deal(group, kind, step).start()

        for kind in (1, 2, 0):
            fetch(kind).start()
        fetch_projection.start()
        v_ref[:, head_width:] = jnp.ones((slots, head_width), jnp.bfloat16)

        place_column = as_column(place_row, tok_rows)
        taxel = as_column(taxel_row, tok_rows) > 0.5

        def embed_block(at, total):
            waves = sine_and_cosine(place_column * freq_ref[:, aligned(at, block_width)])
            for side in range(2):
                start = side * half_width + at * block_width
                cols = pl.ds(pl.multiple_of(start, block_width), block_width)
                rounded = embedded_rows(f32(tok_ref[:, cols]), waves[side], taxel, table_ref[:, cols])
                emb_ref[:, cols] = rounded
                values = f32(rounded)
                for lane in range(0, block_width, 128):
                    total = total + values[:, lane : lane + 128]
            return total

        nothing = jnp.zeros((tok_rows, 128), jnp.float32)
        total = lax.fori_loop(0, blocks // 2, embed_block, nothing)
        mean = jnp.sum(total, axis=1, keepdims=True) * (1.0 / width)
        for step in range(1, ctx_count):
            count_line(step).wait_recv()
        for step in range(1, seq_count):
            count_plane(step).start()
        groups[0].forward()

        def var_block(at, total):
            centered = f32(emb_ref[:, aligned(at, block_width)]) - mean
            centered = centered * centered
            for lane in range(0, block_width, 128):
                total = total + centered[:, lane : lane + 128]
            return total

        total = lax.fori_loop(0, blocks, var_block, nothing)
        scale = lax.rsqrt(jnp.sum(total, axis=1, keepdims=True) * (1.0 / width) + EPSILON)

        def norm_block(at, carry):
            cols = aligned(at, block_width)
            values = (f32(emb_ref[:, cols]) - mean) * scale * gain_ref[:, cols] + bias_ref[:, cols]
            rows = bf16(values)
            normed[:, cols] = rows
            gathered[1, me, :, cols] = moved(base_choice[GROUP:], rows)
            return carry

        lax.fori_loop(0, blocks, norm_block, 0)
        groups[1].begin()
        groups[0].finish()
        save_embedded.start()
        groups[0].arrive()
        opening_rows = gathered[0].reshape(plane_rows, width)
        fetch(1).wait()
        send(0, 1, project(opening_rows, 1))
        for step in range(1, seq_count):
            count_plane(step).wait_recv()
        layout = Layout(counts_of(cnt_ref, seq_count, ctx_count), me * ctx_count + level, level, seq_count, ctx_count)
        fits_ref[0] = jnp.max(layout.fits).astype(jnp.int32)
        slot = f32(lax.broadcasted_iota(jnp.int32, (shared_rows, tok_rows), 0))
        shared_choice = bf16(jnp.where(layout.shared_slots(keep_row, rank_row) == slot, 1.0, 0.0))
        slot = f32(lax.broadcasted_iota(jnp.int32, (GROUP, tok_rows), 0))
        tail_choice = bf16(jnp.where(layout.tail_slots(keep_row, rank_row) == slot, 1.0, 0.0))
        both_choice = jnp.concatenate([shared_choice, tail_choice], axis=0)
        for block in range(blocks):
            cols = slice(block * block_width, (block + 1) * block_width)
            rows = moved(both_choice, normed[:, cols])
            shared_in[block] = rows[:shared_rows]
            tail_own[:, cols] = rows[shared_rows:]
        reduce_in.level_one()
        tail_swap.start()

        reduce_in.level_two()
        groups[1].forward()
        fetch(2).wait()
        send(0, 2, project(opening_rows, 2))
        fetch(0).wait()
        send(0, 0, project(opening_rows, 0))
        tail_swap.wait_recv()
        tail[me // 2, :, my_half] = tail_own[:, my_half] + tail_in[...]
        groups[1].finish()
        reduce_in.level_three()
        groups[2].begin()
        groups[1].arrive()
        group_rows = gathered[1].reshape(plane_rows, width)
        send(1, 1, project(group_rows, 1))
        reduce_in.total()
        for step in range(1, ctx_count):
            cross(step).start()
        groups[2].forward()
        value_rows = project(group_rows, 2)
        groups[2].finish()
        for step in range(1, ctx_count):
            cross(step).wait_recv()
        own = summed[:, aligned(level, SHARED), :]
        shared[pl.ds(own_start, 2)] = own + crossed[0] + crossed[1] + crossed[2]
        spread.begin()
        send(1, 2, value_rows)
        send(1, 0, project(group_rows, 0))
        grouped_choice, shared_choice = layout.tail_choice(level)
        key_bias = layout.key_bias()
        spread.forward()
        groups[2].arrive()
        spread.finish()
        spread.arrive()
        tail_count = chips * GROUP
        held_tail = tail[...].reshape(tail_count, width)
        for kind in (0, 1, 2):
            total = jnp.zeros((tail_count + SHARED, local_width), jnp.float32)
            for block in range(blocks):
                cols = slice(block * block_width, (block + 1) * block_width)
                rows = jnp.concatenate([held_tail[:, cols], shared[block]], axis=0)
                total = total + jnp.dot(rows, w_ref[kind, cols, :], preferred_element_type=jnp.float32)
            rows = bf16(total)
            packed = jnp.dot(grouped_choice[:, :tail_count], rows[:tail_count], preferred_element_type=jnp.float32)
            packed = packed + jnp.dot(shared_choice, rows[tail_count:], preferred_element_type=jnp.float32)
            send(2, kind, bf16(packed))

        def dealt_in(group, kind):
            for step in range(1, ctx_count):
                deal(group, kind, step).wait_recv()

        first_keys = GROUPS * ctx_count * plane_rows
        factor = score_scale * math.log2(math.e)

        def scores_of(begin, rows, low, high):
            scores = lax.dot_general(
                qk_ref[0, pl.ds(begin, rows)], qk_ref[1, low:high], (((1,), (1,)), ((), ())),
                preferred_element_type=jnp.float32,
            )
            return scores * factor + key_bias[:, low:high]

        def weigh(scores, top, low, high):
            weights = bf16(jnp.exp2(scores - top))
            return jnp.dot(weights, v_ref[low:high], preferred_element_type=jnp.float32)

        def finish_rows(begin, rows, both):
            attended[pl.ds(begin, rows)] = bf16(both[:, :head_width] / both[:, head_width:])

        def attend_early(begin, rows):
            scores = scores_of(begin, rows, 0, first_keys)
            top = jnp.max(scores, axis=1, keepdims=True)
            peak[pl.ds(begin, rows)] = jnp.broadcast_to(top, (rows, 128))
            running[pl.ds(begin, rows)] = weigh(scores, top, 0, first_keys)

        def attend_late(begin, rows):
            scores = scores_of(begin, rows, first_keys, slots)
            before = peak[pl.ds(begin, rows)][:, :1]
            top = jnp.maximum(before, jnp.max(scores, axis=1, keepdims=True))
            both = running[pl.ds(begin, rows)] * jnp.exp2(before - top)
            finish_rows(begin, rows, both + weigh(scores, top, first_keys, slots))

        def send_back(group):
            for step in (2, 3, 1):
                back(group, step).start()
            back_own(group).start()

        def collect(group):
            back_own(group).wait()
            for step in range(1, ctx_count):
                back(group, step).wait_recv()

        span = ctx_count * plane_rows // 2
        for group in range(GROUPS):
            dealt_in(group, 1)
            dealt_in(group, 2)
        for group in range(GROUPS):
            dealt_in(group, 0)
            attend_early(2 * group * span, span)
            attend_early((2 * group + 1) * span, span)
        dealt_in(GROUPS, 0)
        attend_early(first_keys, ctx_count * TAIL)
        dealt_in(GROUPS, 1)
        dealt_in(GROUPS, 2)
        attend_late(first_keys, ctx_count * TAIL)
        send_back(2)
        for group in range(GROUPS):
            attend_late(2 * group * span, span)
            attend_late((2 * group + 1) * span, span)
            if group == 0:
                send_back(group)
        fetch_projection.wait()
        collect(2)
        packed = inward[2, :TAIL]
        grouped = bf16(lax.dot_general(grouped_choice, packed, unpack, preferred_element_type=jnp.float32))
        extra = bf16(lax.dot_general(shared_choice, packed, unpack, preferred_element_type=jnp.float32))
        rows = jnp.concatenate([grouped[:tail_count], extra], axis=0)
        for block in range(blocks):
            cols = slice(block * block_width, (block + 1) * block_width)
            values = bf16(jnp.dot(rows, proj_ref[:, cols], preferred_element_type=jnp.float32))
            tail_shares[:, :, cols] = values[:tail_count].reshape(chips, GROUP, block_width)
            ret_in[block] = values[tail_count:]
        reduce_back.level_one()
        row_sums[2].begin()
        reduce_back.level_two()
        row_sums[2].chip()
        reduce_back.level_three()

        def project_back(g):
            for block in range(blocks):
                cols = slice(block * block_width, (block + 1) * block_width)
                values = moved(inward[g], proj_ref[:, cols])
                shares[g, :, :, cols] = values.reshape(seq_count, GROUP, block_width)

        collect(0)
        send_back(1)
        project_back(0)
        row_sums[0].begin()
        reduce_back.total()
        for step in range(1, ctx_count):
            cross_back(step).start()
        row_sums[2].relay()
        row_sums[0].chip()
        collect(1)
        project_back(1)
        row_sums[1].begin()
        for step in range(1, ctx_count):
            cross_back(step).wait_recv()
        back_spread.begin()
        row_sums[0].relay()
        row_sums[1].chip()
        row_sums[2].end()
        tail_back.start()
        back_spread.forward()
        row_sums[1].relay()
        row_sums[0].end()
        back_spread.finish()
        slot = f32(lax.broadcasted_iota(jnp.int32, (shared_rows, tok_rows), 0))
        from_shared = bf16(jnp.where(layout.shared_slots(keep_row, rank_row) == slot, 1.0, 0.0))
        from_rows = jnp.concatenate([base_choice, tail_choice], axis=0)
        tail_back.wait_recv()
        back_spread.arrive()
        row_sums[1].end()

        def deliver(part):
            cols = pl.ds(part * early_width, early_width)
            return pltpu.make_async_copy(out_ref.at[:, cols], out_hbm.at[:, cols], out_sems.at[part])

        for block in range(blocks):
            cols = slice(block * block_width, (block + 1) * block_width)
            placed = lax.dot_general(from_shared, final[block], unpack, preferred_element_type=jnp.float32)
            placed = placed + lax.dot_general(
                from_rows, returned[:, cols], unpack, preferred_element_type=jnp.float32
            )
            out_ref[:, cols] = bf16(placed)
            if (block + 1) % (blocks // early) == 0:
                deliver(block // (blocks // early)).start()
        save_embedded.wait()
        for part in range(early):
            deliver(part).wait()
        for g in range(sets):
            for kind in range(kinds):
                for step in range(1, ctx_count):
                    deal(g, kind, step).wait_send()
            row_sums[g].drain()
            for step in range(1, ctx_count):
                back(g, step).wait_send()
        tail_swap.wait_send()
        tail_back.wait_send()
        for step in range(1, ctx_count):
            count_line(step).wait_send()
            cross(step).wait_send()
            cross_back(step).wait_send()
        for step in range(1, seq_count):
            count_plane(step).wait_send()
        for gather in groups + [spread, back_spread]:
            gather.drain()
        reduce_in.drain()
        reduce_back.drain()

    dma = pltpu.SemaphoreType.DMA
    b16 = jnp.bfloat16
    vmem = pl.BlockSpec(memory_space=pltpu.VMEM)
    anywhere = pl.BlockSpec(memory_space=pl.ANY)

    def held(*shape):
        return pltpu.VMEM(shape, b16)

    def pair(*shape):
        return [dma(shape)] * 2

    return pl.pallas_call(
        kernel,
        out_shape=[jax.ShapeDtypeStruct((tok_rows, width), b16)] * 2 + [jax.ShapeDtypeStruct((1,), jnp.int32)],
        in_specs=[vmem] * 7 + [anywhere] * 3,
        out_specs=[anywhere, anywhere, pl.BlockSpec(memory_space=pltpu.SMEM)],
        scratch_shapes=[
            held(tok_rows, width),
            held(*qkv_weight.shape),
            held(*out_weight.shape),
            held(tok_rows, width),
            pltpu.VMEM((seq_count, ctx_count, 8, 128), jnp.int32),
            held(tok_rows, width),
            held(GROUP, width),
            held(GROUPS, seq_count, GROUP, width),
            held(GROUP, width),
            held(GROUP, half_width),
            held(chips, GROUP, width),
            held(blocks, shared_rows, block_width),
            held(8, shared_rows, block_width),
            held(4, shared_rows, block_width),
            held(2, shared_rows, block_width),
            held(2, shared_rows, block_width),
            held(ctx_count - 1, 2, SHARED, block_width),
            held(blocks, SHARED, block_width),
            held(sets * kinds, ctx_count, plane_rows, head_width),
            held(2, slots, head_width),
            held(slots, 2 * head_width),
            pltpu.VMEM((slots, 128), jnp.float32),
            pltpu.VMEM((slots, 2 * head_width), jnp.float32),
            held(slots, head_width),
            held(sets, plane_rows, local_width),
            held(GROUPS, seq_count, GROUP, width),
            held(GROUPS, 4, GROUP, width),
            held(GROUPS, 4, GROUP, width),
        ]
        + [held(GROUPS, 2, GROUP, half_width)] * 4
        + [
            held(BASE + GROUP, width),
            held(chips, GROUP, width),
            held(4, GROUP, half_width),
            held(4, GROUP, half_width),
        ]
        + [held(2, GROUP, quarter)] * 4
        + [
            held(blocks, SHARED, block_width),
            held(8, SHARED, block_width),
            held(4, SHARED, block_width),
            held(2, SHARED, block_width),
            held(blocks, shared_rows, block_width),
            held(tok_rows, width),
        ]
        + [dma((kinds + 3,))]
        + pair(seq_count + ctx_count - 2)
        + pair(sets + 2, 9)
        + pair(7)
        + pair(ctx_count - 1)
        + pair(sets * kinds * (ctx_count - 1))
        + pair(sets * (ctx_count - 1))
        + [dma((sets,))]
        + pair(sets, 10)
        + pair(7)
        + pair(ctx_count - 1)
        + pair(2)
        + [dma((early,))],
        compiler_params=pltpu.CompilerParams(
            collective_id=collective_id, has_side_effects=True, vmem_limit_bytes=60 * 2**20
        ),
    )(modality, keep, positions, frequency, modal_table, gain, bias, tokens, qkv_weight, out_weight)


def local(
    tokens,
    modality,
    keep_mask,
    positions,
    modal_table,
    norm_gain,
    norm_bias,
    qkv_weight,
    out_weight,
    mask_token,
):
    arguments = (
        tokens, modality, keep_mask, positions, modal_table, norm_gain, norm_bias, qkv_weight, out_weight, mask_token,
    )
    seq_count, ctx_count = lax.axis_size("seq"), lax.axis_size("ctx")
    tok_rows, width = tokens.shape
    local_width = qkv_weight.shape[2]
    shaped = seq_count == 8 and ctx_count == 4 and tok_rows == 128 and width % 4096 == 0
    shaped = shaped and local_width == ctx_count * HEAD_DIM
    if shaped:
        half_width = width // 2
        exponents = np.arange(half_width, dtype=np.float64) / half_width
        frequency = jnp.asarray(np.exp(-math.log(10000.0) * exponents).astype(np.float32))[None]
        *done, fits = encode(
            tokens, modality[None], keep_mask[None], positions[None], frequency, modal_table,
            norm_gain[None], norm_bias[None], qkv_weight, out_weight, 11,
        )
        restored, embedded = lax.cond(fits[0] == 1, lambda done, *given: done, lambda done, *given: general(*given), done, *arguments)
        restored, embedded = lax.optimization_barrier((restored, embedded))
    else:
        restored, embedded = general(*arguments)
    return jnp.where((keep_mask == 1)[:, None], f32(embedded) + f32(restored), mask_token[None, :])


def solution(mesh):
    in_specs = (
        P(("seq", "ctx"), None),
        P(("seq", "ctx")),
        P(("seq", "ctx")),
        P(("seq", "ctx")),
        P(),
        P(),
        P(),
        P(None, None, "seq"),
        P("seq", None),
        P(),
    )
    out_specs = P(("seq", "ctx"), None)
    return jax.shard_map(local, mesh=mesh, in_specs=in_specs, out_specs=out_specs, check_vma=False)
```

```python
import math

import jax
import jax.numpy as jnp
import numpy as np
from jax import lax
from jax.experimental import pallas as pl
from jax.experimental.pallas import tpu as pltpu
from jax.sharding import PartitionSpec as P

HEAD_DIM = 128


EPSILON = 1e-06
MESH = pl.DeviceIdType.MESH


def position_table(positions, feature_width):
    half_width = feature_width // 2
    frequency = jnp.exp(-math.log(10000.0) * jnp.arange(half_width, dtype=jnp.float32) / half_width)
    angles = positions.astype(jnp.float32)[:, None] * frequency[None, :]
    return jnp.concatenate([jnp.sin(angles), jnp.cos(angles)], axis=1)


def embed(tokens, modality, positions, modal_table):
    table_rows = jnp.where(modality[:, None] == 1, modal_table[1][None, :], modal_table[0][None, :])
    summed = tokens.astype(jnp.float32) + position_table(positions, tokens.shape[1]) + table_rows
    return summed.astype(jnp.bfloat16)


def layer_norm(embedded, norm_gain, norm_bias):
    values = embedded.astype(jnp.float32)
    row_mean = jnp.mean(values, axis=1, keepdims=True)
    centered = values - row_mean
    row_var = jnp.mean(centered * centered, axis=1, keepdims=True)
    return (centered * lax.rsqrt(row_var + EPSILON) * norm_gain + norm_bias).astype(jnp.bfloat16)


def everyone():
    seq_count, ctx_count = lax.axis_size("seq"), lax.axis_size("ctx")

    def place():
        return lax.axis_index("seq") * ctx_count + lax.axis_index("ctx")

    return seq_count * ctx_count, place, lambda j: {"seq": j // ctx_count, "ctx": lax.rem(j, ctx_count)}


def along(axis):
    return lax.axis_size(axis), lambda: lax.axis_index(axis), lambda j: {axis: j}


def exchange(x, group, source, target, out_shape, collective_id):
    count, place, device_of = group

    def kernel(x_ref, out_ref, send_sem, recv_sem, own_sem):
        me = place()
        barrier = pltpu.get_barrier_semaphore()

        def greet(step, carry):
            peer = lax.rem(me + step, count)
            pl.semaphore_signal(barrier, inc=1, device_id=device_of(peer), device_id_type=MESH)
            return carry

        def push(step):
            peer = lax.rem(me + step, count)
            return pltpu.make_async_remote_copy(
                src_ref=source(x_ref, peer),
                dst_ref=target(out_ref, me),
                send_sem=send_sem.at[step],
                recv_sem=recv_sem.at[step],
                device_id=device_of(peer),
                device_id_type=MESH,
            )

        def start(step, carry):
            push(step).start()
            return carry

        def finish(step, carry):
            push(step).wait()
            return carry

        lax.fori_loop(1, count, greet, 0)
        own = pltpu.make_async_copy(source(x_ref, me), target(out_ref, me), own_sem)
        own.start()
        pl.semaphore_wait(barrier, count - 1)
        lax.fori_loop(1, count, start, 0)
        lax.fori_loop(1, count, finish, 0)
        own.wait()

    return pl.pallas_call(
        kernel,
        out_shape=jax.ShapeDtypeStruct(out_shape, x.dtype),
        in_specs=[pl.BlockSpec(memory_space=pltpu.VMEM)],
        out_specs=pl.BlockSpec(memory_space=pltpu.VMEM),
        scratch_shapes=[
            pltpu.SemaphoreType.DMA((count,)),
            pltpu.SemaphoreType.DMA((count,)),
            pltpu.SemaphoreType.DMA,
        ],
        compiler_params=pltpu.CompilerParams(collective_id=collective_id, has_side_effects=True),
    )(x)


CHUNKS = 4


def remote(src, dst, sems, at, device):
    send_sem, recv_sem = sems
    return pltpu.make_async_remote_copy(
        src_ref=src,
        dst_ref=dst,
        send_sem=send_sem.at[at],
        recv_sem=recv_sem.at[at],
        device_id=device,
        device_id_type=MESH,
    )


def aligned(start, size):
    return pl.ds(pl.multiple_of(start * size, size), size)


def greet_line_and_plane(seq_count, ctx_count):
    me, level = lax.axis_index("seq"), lax.axis_index("ctx")
    barrier = pltpu.get_barrier_semaphore()
    for step in range(1, seq_count):
        peer = {"seq": lax.rem(me + step, seq_count)}
        pl.semaphore_signal(barrier, inc=1, device_id=peer, device_id_type=MESH)
    for step in range(1, ctx_count):
        peer = {"ctx": lax.rem(level + step, ctx_count)}
        pl.semaphore_signal(barrier, inc=1, device_id=peer, device_id_type=MESH)
    pl.semaphore_wait(barrier, seq_count + ctx_count - 2)


def regrouping(capacity, outer, inner, slot_count):
    row = lax.broadcasted_iota(jnp.int32, (capacity, capacity), 0)
    column = lax.broadcasted_iota(jnp.int32, (capacity, capacity), 1)
    first = row // (inner * slot_count)
    second = row // slot_count % inner
    wanted = (second * outer + first) * slot_count + row % slot_count
    return (column == wanted).astype(jnp.bfloat16)


def moved(choice, rows):
    return jnp.dot(choice, rows, preferred_element_type=jnp.float32).astype(jnp.bfloat16)


def spread_rows(outgoing, choice, qkv_weight, slot_count, collective_id):
    capacity, width = outgoing.shape
    rows = choice.shape[0]
    half = rows // 2
    seq_count, ctx_count = lax.axis_size("seq"), lax.axis_size("ctx")
    line_rows, plane_rows = capacity // ctx_count, capacity // seq_count
    part_width = width // CHUNKS

    kinds, _, local_width = qkv_weight.shape

    def kernel(
        x_ref, choice_ref, w_hbm, triple_ref, mid, ordered, arrived, out_ref, w_ref, total,
        zs, zr, ps, pr, gs, gr, own_sem, own_sems, w_sems,
    ):
        me, level = lax.axis_index("seq"), lax.axis_index("ctx")
        sibling, left, down = flip(me, 1), flip(me, 2), flip(me, 4)
        across = flip(left, 4)
        all_rows, first, second = pl.ds(0, rows), pl.ds(0, half), pl.ds(half, half)
        along_line, over_plane, gathering = (zs, zr), (ps, pr), (gs, gr)

        def cols(k):
            return pl.ds(k * part_width, part_width)

        def line(k, step):
            peer = lax.rem(level + step, ctx_count)
            src = x_ref.at[aligned(peer, line_rows), cols(k)]
            dst = mid.at[aligned(level, line_rows), cols(k)]
            return remote(src, dst, along_line, (k, step), {"ctx": peer})

        def plane(k, step):
            peer = lax.rem(me + step, seq_count)
            src = ordered.at[aligned(peer, plane_rows), cols(k)]
            dst = arrived.at[aligned(me, plane_rows), cols(k)]
            return remote(src, dst, over_plane, (k, step), {"seq": peer})

        def plane_own(k):
            here = aligned(me, plane_rows)
            return pltpu.make_async_copy(ordered.at[here, cols(k)], arrived.at[here, cols(k)], own_sems.at[k])

        moves = (
            (me, all_rows, sibling),
            (me, all_rows, left),
            (me, all_rows, down),
            (left, first, down),
            (down, second, left),
            (left, all_rows, sibling),
            (down, all_rows, sibling),
            (across, first, sibling),
            (across, second, sibling),
        )

        def hand(k, at):
            origin, which, place = moves[at]
            ref = out_ref.at[origin, which, cols(k)]
            return remote(ref, ref, gathering, (k, at), {"seq": place})

        def fetch(k):
            return pltpu.make_async_copy(w_hbm.at[:, cols(k), :], w_ref.at[:, cols(k), :], w_sems.at[k])

        greet_line_and_plane(seq_count, ctx_count)
        for k in range(CHUNKS):
            for step in range(1, ctx_count):
                line(k, step).start()
        for k in range(CHUNKS):
            fetch(k).start()
        here = aligned(level, line_rows)
        own = pltpu.make_async_copy(x_ref.at[here], mid.at[here], own_sem)
        own.start()
        regroup = regrouping(capacity, seq_count, ctx_count, slot_count)
        own.wait()
        for turn in range(CHUNKS + 4):
            k = turn - 4
            if 0 <= k < CHUNKS:
                for at in (0, 5, 6, 7, 8):
                    hand(k, at).wait_recv()
                fetch(k).wait()
                gathered = out_ref[:, :, cols(k)].reshape(seq_count * rows, part_width)
                for kind in range(kinds):
                    term = jnp.dot(gathered, w_ref[kind, cols(k), :], preferred_element_type=jnp.float32)
                    if k == 0:
                        total[kind] = term
                    elif k < CHUNKS - 1:
                        total[kind] += term
                    else:
                        triple_ref[kind] = (total[kind] + term).astype(jnp.bfloat16)
            k = turn - 3
            if 0 <= k < CHUNKS:
                hand(k, 3).wait_recv()
                hand(k, 7).start()
                hand(k, 4).wait_recv()
                hand(k, 8).start()
            k = turn - 2
            if 0 <= k < CHUNKS:
                hand(k, 1).wait_recv()
                hand(k, 3).start()
                hand(k, 5).start()
                hand(k, 2).wait_recv()
                hand(k, 4).start()
                hand(k, 6).start()
            k = turn - 1
            if 0 <= k < CHUNKS:
                for step in range(1, seq_count):
                    plane(k, step).wait_recv()
                plane_own(k).wait()
                out_ref[me, :, cols(k)] = moved(choice_ref[...], arrived[:, cols(k)])
                for at in (1, 2, 0):
                    hand(k, at).start()
            k = turn
            if k < CHUNKS:
                for step in range(1, ctx_count):
                    line(k, step).wait_recv()
                ordered[:, cols(k)] = moved(regroup, mid[:, cols(k)])
                for step in range(1, seq_count):
                    plane(k, step).start()
                plane_own(k).start()
        for k in range(CHUNKS):
            for at in range(9):
                hand(k, at).wait_send()
            for step in range(1, seq_count):
                plane(k, step).wait_send()
            for step in range(1, ctx_count):
                line(k, step).wait_send()

    dma = pltpu.SemaphoreType.DMA
    return pl.pallas_call(
        kernel,
        out_shape=jax.ShapeDtypeStruct((kinds, seq_count * rows, local_width), jnp.bfloat16),
        in_specs=[pl.BlockSpec(memory_space=pltpu.VMEM)] * 2 + [pl.BlockSpec(memory_space=pl.ANY)],
        out_specs=pl.BlockSpec(memory_space=pltpu.VMEM),
        scratch_shapes=[pltpu.VMEM((capacity, width), jnp.bfloat16)] * 3
        + [
            pltpu.VMEM((seq_count, rows, width), jnp.bfloat16),
            pltpu.VMEM(qkv_weight.shape, jnp.bfloat16),
            pltpu.VMEM((kinds, seq_count * rows, local_width), jnp.float32),
        ]
        + [dma((CHUNKS, ctx_count))] * 2
        + [dma((CHUNKS, seq_count))] * 2
        + [dma((CHUNKS, 9))] * 2
        + [dma, dma((CHUNKS,)), dma((CHUNKS,))],
        compiler_params=pltpu.CompilerParams(collective_id=collective_id, has_side_effects=True),
    )(outgoing, choice, qkv_weight)


def flip(position, bit):
    return position + bit * (1 - 2 * lax.rem(position // bit, 2))


def return_rows(attended, out_weight, choice, slot_count, collective_id):
    width = out_weight.shape[1]
    capacity, rows = choice.shape
    half = rows // 2
    seq_count, ctx_count = lax.axis_size("seq"), lax.axis_size("ctx")
    line_rows, plane_rows = capacity // ctx_count, capacity // seq_count
    part_width = width // CHUNKS

    def kernel(
        x_ref, w_ref, choice_ref, out_ref, shares, near, sums, from_left, from_down, last, passed, total,
        sorted_rows, arrived, ordered, ss, sr, ps, pr, zs, zr, own_sems, line_sems,
    ):
        me, level = lax.axis_index("seq"), lax.axis_index("ctx")
        sibling, left, down = flip(me, 1), flip(me, 2), flip(me, 4)
        first, second = pl.ds(0, half), pl.ds(half, half)
        summing, over_plane, along_line = (ss, sr), (ps, pr), (zs, zr)

        def cols(k):
            return pl.ds(k * part_width, part_width)

        def at(place, which):
            place = flip(place, 2) if which % 2 else place
            return flip(place, 4) if which // 2 else place

        def over(k, q):
            src = shares.at[aligned(at(sibling, q), rows), cols(k)]
            return remote(src, near.at[q, :, cols(k)], summing, (k, q), {"seq": sibling})

        def far(k, which):
            if which == 0:
                return remote(sums.at[3, first, cols(k)], from_left.at[1, :, cols(k)], summing, (k, 4), {"seq": left})
            if which == 1:
                return remote(sums.at[3, second, cols(k)], from_down.at[1, :, cols(k)], summing, (k, 5), {"seq": down})
            if which == 2:
                return remote(sums.at[1, first, cols(k)], from_left.at[0, :, cols(k)], summing, (k, 6), {"seq": left})
            if which == 3:
                return remote(sums.at[2, second, cols(k)], from_down.at[0, :, cols(k)], summing, (k, 7), {"seq": down})
            if which == 4:
                return remote(passed.at[0, :, cols(k)], last.at[0, :, cols(k)], summing, (k, 8), {"seq": down})
            return remote(passed.at[1, :, cols(k)], last.at[1, :, cols(k)], summing, (k, 9), {"seq": left})

        def plane(k, step):
            peer = lax.rem(me + step, seq_count)
            src = sorted_rows.at[aligned(peer, plane_rows), cols(k)]
            dst = arrived.at[aligned(me, plane_rows), cols(k)]
            return remote(src, dst, over_plane, (k, step), {"seq": peer})

        def plane_own(k):
            here = aligned(me, plane_rows)
            return pltpu.make_async_copy(sorted_rows.at[here, cols(k)], arrived.at[here, cols(k)], own_sems.at[k])

        def line(k, step):
            peer = lax.rem(level + step, ctx_count)
            src = ordered.at[aligned(peer, line_rows), cols(k)]
            dst = out_ref.at[aligned(level, line_rows), cols(k)]
            return remote(src, dst, along_line, (k, step), {"ctx": peer})

        def line_own(k):
            here = aligned(level, line_rows)
            return pltpu.make_async_copy(ordered.at[here, cols(k)], out_ref.at[here, cols(k)], line_sems.at[k])

        def wide(value):
            return value.astype(jnp.float32)

        def narrow(value):
            return value.astype(jnp.bfloat16)

        greet_line_and_plane(seq_count, ctx_count)
        regroup = regrouping(capacity, ctx_count, seq_count, slot_count)
        order = (3, 1, 2, 0)
        for turn in range(CHUNKS + 4):
            k = turn - 4
            if 0 <= k < CHUNKS:
                for step in range(1, seq_count):
                    plane(k, step).wait_recv()
                plane_own(k).wait()
                ordered[:, cols(k)] = moved(regroup, arrived[:, cols(k)])
                for step in range(1, ctx_count):
                    line(k, step).start()
                line_own(k).start()
            k = turn - 3
            if 0 <= k < CHUNKS:
                c = cols(k)
                far(k, 2).wait_recv()
                far(k, 4).wait_recv()
                total[:half, c] = narrow(wide(sums[0, :half, c]) + wide(from_left[0, :, c]) + wide(last[0, :, c]))
                far(k, 3).wait_recv()
                far(k, 5).wait_recv()
                total[half:, c] = narrow(wide(sums[0, half:, c]) + wide(from_down[0, :, c]) + wide(last[1, :, c]))
                sorted_rows[:, c] = moved(choice_ref[...], total[:, c])
                for step in range(1, seq_count):
                    plane(k, step).start()
                plane_own(k).start()
            k = turn - 2
            if 0 <= k < CHUNKS:
                c = cols(k)
                far(k, 0).wait_recv()
                passed[0, :, c] = narrow(wide(sums[2, :half, c]) + wide(from_left[1, :, c]))
                far(k, 4).start()
                far(k, 1).wait_recv()
                passed[1, :, c] = narrow(wide(sums[1, half:, c]) + wide(from_down[1, :, c]))
                far(k, 5).start()
            k = turn - 1
            if 0 <= k < CHUNKS:
                c = cols(k)
                for q in order:
                    over(k, q).wait_recv()
                    mine = shares[aligned(at(me, q), rows), c]
                    sums[q, :, c] = narrow(wide(mine) + wide(near[q, :, c]))
                    if q == 3:
                        far(k, 0).start()
                        far(k, 1).start()
                    if q == 1:
                        far(k, 2).start()
                    if q == 2:
                        far(k, 3).start()
            k = turn
            if k < CHUNKS:
                shares[:, cols(k)] = moved(x_ref[...], w_ref[:, cols(k)])
                for q in order:
                    over(k, q).start()
        for k in range(CHUNKS):
            for step in range(1, ctx_count):
                line(k, step).wait()
            line_own(k).wait()
            for step in range(1, seq_count):
                plane(k, step).wait_send()
            for q in order:
                over(k, q).wait_send()
            for which in range(6):
                far(k, which).wait_send()

    dma = pltpu.SemaphoreType.DMA
    bf16 = jnp.bfloat16
    return pl.pallas_call(
        kernel,
        out_shape=jax.ShapeDtypeStruct((capacity, width), bf16),
        in_specs=[pl.BlockSpec(memory_space=pltpu.VMEM)] * 3,
        out_specs=pl.BlockSpec(memory_space=pltpu.VMEM),
        scratch_shapes=[pltpu.VMEM((seq_count * rows, width), bf16)]
        + [pltpu.VMEM((4, rows, width), bf16)] * 2
        + [pltpu.VMEM((2, half, width), bf16)] * 4
        + [pltpu.VMEM((rows, width), bf16)]
        + [pltpu.VMEM((capacity, width), bf16)] * 3
        + [dma((CHUNKS, 10))] * 2
        + [dma((CHUNKS, seq_count))] * 2
        + [dma((CHUNKS, ctx_count))] * 2
        + [dma((CHUNKS,))] * 2,
        compiler_params=pltpu.CompilerParams(collective_id=collective_id, has_side_effects=True),
    )(attended, out_weight, choice)


def part(ref, j):
    return ref.at[j]


def whole(ref, j):
    return ref


def attend(triple):
    _, heads, rows, _ = triple.shape
    block = min(rows, 256)
    score_scale = 1.0 / math.sqrt(HEAD_DIM)

    def kernel(q_ref, k_ref, v_ref, out_ref):
        scores = (
            lax.dot_general(
                q_ref[...], k_ref[...], (((1,), (1,)), ((), ())), preferred_element_type=jnp.float32
            )
            * score_scale
        )
        expanded = jnp.exp(scores - jnp.max(scores, axis=1, keepdims=True))
        total = jnp.sum(expanded, axis=1, keepdims=True)
        summed = jnp.dot(expanded.astype(jnp.bfloat16), v_ref[...], preferred_element_type=jnp.float32)
        out_ref[...] = (summed / total).astype(jnp.bfloat16)

    return pl.pallas_call(
        kernel,
        grid=(heads, rows // block),
        out_shape=jax.ShapeDtypeStruct((heads, rows, HEAD_DIM), jnp.bfloat16),
        in_specs=[
            pl.BlockSpec((None, None, block, HEAD_DIM), lambda h, i: (0, h, i, 0)),
            pl.BlockSpec((None, None, rows, HEAD_DIM), lambda h, i: (1, h, 0, 0)),
            pl.BlockSpec((None, None, rows, HEAD_DIM), lambda h, i: (2, h, 0, 0)),
        ],
        out_specs=pl.BlockSpec((None, block, HEAD_DIM), lambda h, i: (h, i, 0)),
    )(triple, triple, triple)


def attend_by_head(triple):
    _, group_rows, local_width = triple.shape
    ctx = along("ctx")
    count = ctx[0]
    width = local_width // count
    heads = width // HEAD_DIM
    gathered = exchange(
        triple,
        ctx,
        lambda ref, j: ref.at[:, :, pl.ds(pl.multiple_of(j * width, HEAD_DIM), width)],
        lambda ref, j: ref.at[:, pl.ds(pl.multiple_of(j * group_rows, group_rows), group_rows), :],
        (3, count * group_rows, width),
        3,
    )
    if heads == 1:
        split = gathered[:, None]
    else:
        split = jnp.transpose(
            gathered.reshape(3, count * group_rows, heads, HEAD_DIM), (0, 2, 1, 3)
        )
    done = attend(split)
    if heads == 1:
        done = done[0]
    else:
        done = jnp.transpose(done, (1, 0, 2)).reshape(count * group_rows, width)
    return exchange(
        done,
        ctx,
        lambda ref, j: ref.at[pl.ds(pl.multiple_of(j * group_rows, group_rows), group_rows), :],
        lambda ref, j: ref.at[:, pl.ds(pl.multiple_of(j * width, HEAD_DIM), width)],
        (group_rows, local_width),
        4,
    )


def attend_by_row(triple):
    queries, key_rows, values = (triple[0], triple[1], triple[2])
    group_rows, local_width = queries.shape
    heads_here = local_width // HEAD_DIM
    score_scale = 1.0 / math.sqrt(HEAD_DIM)
    both = lax.all_gather(jnp.stack([key_rows, values]), "ctx", axis=1, tiled=True)
    length = both.shape[1]
    query_heads = queries.reshape(group_rows, heads_here, HEAD_DIM)
    key_heads = both[0].reshape(length, heads_here, HEAD_DIM)
    value_heads = both[1].reshape(length, heads_here, HEAD_DIM)
    scores = (
        jnp.einsum("ghd,khd->hgk", query_heads, key_heads, preferred_element_type=jnp.float32)
        * score_scale
    )
    expanded = jnp.exp(scores - jnp.max(scores, axis=2, keepdims=True))
    total = jnp.sum(expanded, axis=2, keepdims=True)
    summed = jnp.einsum(
        "hgk,khd->hgd",
        expanded.astype(jnp.bfloat16),
        value_heads,
        preferred_element_type=jnp.float32,
    )
    attended = (summed / total).astype(jnp.bfloat16)
    return jnp.transpose(attended, (1, 0, 2)).reshape(group_rows, local_width)


def general(
    tokens,
    modality,
    keep_mask,
    positions,
    modal_table,
    norm_gain,
    norm_bias,
    qkv_weight,
    out_weight,
    mask_token,
):
    tok_rows, feature_width = tokens.shape
    seq_count = lax.axis_size("seq")
    ctx_count = lax.axis_size("ctx")
    devices = seq_count * ctx_count
    slot_count = (tok_rows + devices - 1) // devices
    capacity = devices * slot_count
    own_rows = tok_rows // 4
    my_index = lax.axis_index("seq") * ctx_count + lax.axis_index("ctx")
    visible = keep_mask == 1
    own_count = jnp.sum(keep_mask)
    counts = exchange(
        jnp.full((1, 128), own_count, jnp.int32), everyone(), whole, part, (devices, 1, 128), 0
    )[:, 0, 0]
    index = jnp.arange(devices, dtype=jnp.int32)
    starts = jnp.sum(jnp.where(index[None, :] < index[:, None], counts[None, :], 0), axis=1)
    my_start = jnp.sum(jnp.where(index < my_index, counts, 0))
    token_index = jnp.arange(tok_rows, dtype=jnp.int32)
    local_rank = (
        jnp.sum(jnp.where(token_index[None, :] <= token_index[:, None], keep_mask[None, :], 0), axis=1) - 1
    )
    global_rank = my_start + local_rank
    owner = global_rank % devices
    piped = seq_count == 8 and slot_count * ctx_count % 16 == 0
    if piped:
        owner = owner % ctx_count * seq_count + owner // ctx_count
    token_slot = jnp.where(visible, owner * slot_count + local_rank // devices, capacity)
    slot_index = jnp.arange(capacity, dtype=jnp.int32)
    slot_of_token = (token_slot[:, None] == slot_index[None, :]).astype(jnp.bfloat16)
    slot_place = slot_index % slot_count
    source_start = jnp.repeat(starts, slot_count)
    source_count = jnp.repeat(counts, slot_count)
    offset = (my_index - source_start) % devices + devices * slot_place
    usable = offset < source_count
    slot_row = jnp.where(usable, (source_start + offset) // devices, own_rows)
    row_of_slot = (
        slot_row[:, None] == jnp.arange(own_rows, dtype=jnp.int32)[None, :]
    ).astype(jnp.bfloat16)

    embedded = embed(tokens, modality, positions, modal_table)

    def pick(choice, rows, side):
        return lax.dot_general(
            choice, rows, (((side,), (0,)), ((), ())), preferred_element_type=jnp.float32
        )

    normed = layer_norm(embedded, norm_gain, norm_bias)
    outgoing = pick(slot_of_token, normed, 0).astype(jnp.bfloat16)
    slots = (devices, slot_count, feature_width)
    if piped:
        triple = spread_rows(outgoing, row_of_slot.T, qkv_weight, slot_count, 1)
    else:
        arriving = exchange(outgoing.reshape(slots), everyone(), part, part, slots, 1)
        own_normed = pick(row_of_slot, arriving.reshape(capacity, feature_width), 0).astype(jnp.bfloat16)
        group = exchange(own_normed, along("seq"), whole, part, (seq_count,) + own_normed.shape, 2)
        triple = jnp.einsum(
            "rd,tdc->trc",
            group.reshape(seq_count * own_rows, feature_width),
            qkv_weight,
            preferred_element_type=jnp.float32,
        ).astype(jnp.bfloat16)
    if triple.shape[2] % (ctx_count * HEAD_DIM) == 0:
        attended = attend_by_head(triple)
    else:
        attended = attend_by_row(triple)
    if piped:
        returned = return_rows(attended, out_weight, row_of_slot, slot_count, 5)
    else:
        shares = jnp.dot(attended, out_weight, preferred_element_type=jnp.float32).astype(jnp.bfloat16)
        shares = shares.reshape(seq_count, own_rows, feature_width)
        shares = exchange(shares, along("seq"), part, part, shares.shape, 5)
        projected = jnp.sum(shares.astype(jnp.float32), axis=0).astype(jnp.bfloat16)
        returning = pick(row_of_slot, projected, 1).astype(jnp.bfloat16)
        returned = exchange(returning.reshape(slots), everyone(), part, part, slots, 6)
        returned = returned.reshape(capacity, feature_width)
    restored = pick(slot_of_token, returned, 1)
    return [bf16(restored), embedded]


GROUP = 16
GROUPS = 2
BASE = GROUP * GROUPS
SHARED = 32
TAIL = 64
NEGATIVE = -1e30


def bf16(value):
    return value.astype(jnp.bfloat16)


def f32(value):
    return value.astype(jnp.float32)


def sine_and_cosine(angle):
    turns = jnp.floor(angle * (2.0 / math.pi) + 0.5)
    quarter = turns.astype(jnp.int32)
    r = ((angle - turns * 1.5703125) - turns * 4.837512969970703125e-4) - turns * 7.54978995489188216e-8
    square = r * r
    sine = r + r * square * (-1.6666654611e-1 + square * (8.3321608736e-3 - square * 1.9515295891e-4))
    cosine = (
        1.0
        - 0.5 * square
        + square * square * (4.166664568298827e-2 + square * (-1.388731625493765e-3 + square * 2.443315711809948e-5))
    )
    odd = (quarter & 1) == 1
    first = jnp.where(odd, cosine, sine)
    second = jnp.where(odd, sine, cosine)
    first = jnp.where((quarter & 2) == 2, -first, first)
    second = jnp.where(((quarter + 1) & 2) == 2, -second, second)
    return first, second


def as_column(row, size):
    across = lax.broadcasted_iota(jnp.int32, (size, size), 1)
    down = lax.broadcasted_iota(jnp.int32, (size, size), 0)
    return jnp.sum(jnp.where(across == down, row, 0.0), axis=1, keepdims=True)


def ranks_of(keep_row, size):
    across = lax.broadcasted_iota(jnp.int32, (size, size), 1)
    down = lax.broadcasted_iota(jnp.int32, (size, size), 0)
    column = as_column(keep_row, size)
    return jnp.sum(jnp.where(down < across, column, 0.0), axis=0, keepdims=True)


class Layout:
    def __init__(self, counts, place, level, seq_count, ctx_count):
        lanes = counts.shape[1:]
        cores = (seq_count // 2, 2, ctx_count) + lanes
        extra = jnp.maximum(counts - BASE, 0.0).reshape(cores)
        first = jnp.minimum(extra[:, 0], 1.0 * GROUP)
        second = jnp.minimum(extra[:, 1], GROUP - first)
        of_chip = first + second
        tail_of = jnp.stack([first, second], axis=1).reshape(counts.shape)
        over = extra.reshape(counts.shape) - tail_of
        index = lax.broadcasted_iota(jnp.int32, counts.shape, 0)
        self.over_start = jnp.sum(jnp.where(index < place, over, 0.0), axis=0)
        self.own_tail = jnp.sum(jnp.where(index == place, tail_of, 0.0), axis=0)
        before = jnp.sum(jnp.where(index == place - ctx_count, tail_of, 0.0), axis=0)
        self.own_start = jnp.where(lax.rem(place // ctx_count, 2) == 1, before, 0.0)
        total = jnp.sum(over, axis=0)
        tails, free, starts = [], [], []
        running = jnp.zeros(lanes, jnp.float32)
        for z in range(ctx_count):
            tail = jnp.sum(of_chip[:, z], axis=0)
            room = jnp.clip(TAIL - tail, 0.0, 1.0 * SHARED)
            tails.append(tail)
            free.append(room)
            starts.append(running)
            running = running + room
        self.fits = jnp.where(total > running, 0.0, 1.0)
        self.tails, self.free, self.starts = tails, free, starts
        self.used = [jnp.clip(total - starts[z], 0.0, free[z]) for z in range(ctx_count)]
        by_plane = counts.reshape((seq_count, ctx_count) + lanes)
        seat = lax.broadcasted_iota(jnp.int32, by_plane.shape, 0)
        lane = lax.broadcasted_iota(jnp.int32, by_plane.shape, 3)
        self.lane_counts = jnp.sum(jnp.where(lane // GROUP == seat, by_plane, 0.0), axis=0)
        seat = lax.broadcasted_iota(jnp.int32, of_chip.shape, 0)
        lane = lax.broadcasted_iota(jnp.int32, of_chip.shape, 3)
        self.lane_tails = jnp.sum(jnp.where(lane // GROUP == seat, of_chip, 0.0), axis=0)
        self.lane_tail_start = jnp.sum(jnp.where(seat < lane // GROUP, of_chip, 0.0), axis=0)

    def of_level(self, values, level):
        out = values[0]
        for z in range(1, len(values)):
            out = jnp.where(level == z, values[z], out)
        return out

    def shared_slots(self, keep_row, rank_row):
        beyond = rank_row - BASE - self.own_tail[0:1]
        ordinal = self.over_start[0:1] + beyond
        slot = jnp.full(ordinal.shape, -1.0, jnp.float32)
        for z in range(len(self.free)):
            here = (ordinal >= self.starts[z][0:1]) & (ordinal < self.starts[z][0:1] + self.free[z][0:1])
            slot = jnp.where(here, ordinal - self.starts[z][0:1] + SHARED * z, slot)
        return jnp.where((keep_row > 0.0) & (beyond >= 0.0), slot, -1.0)

    def tail_slots(self, keep_row, rank_row):
        ordinal = rank_row - BASE
        valid = (keep_row > 0.0) & (ordinal >= 0.0) & (ordinal < self.own_tail[0:1])
        return jnp.where(valid, ordinal + self.own_start[0:1], -1.0)

    def tail_choice(self, level):
        counts = self.of_level([self.lane_tails[z] for z in range(len(self.free))], level)[0:1]
        start = self.of_level([self.lane_tail_start[z] for z in range(len(self.free))], level)[0:1]
        tail = self.of_level(self.tails, level)[0:1]
        used = self.of_level(self.used, level)[0:1]
        size = (TAIL, counts.shape[1])
        target = f32(lax.broadcasted_iota(jnp.int32, size, 0))
        lane = lax.broadcasted_iota(jnp.int32, size, 1)
        within = f32(lane % GROUP)
        valid = counts > within
        grouped = bf16(jnp.where(valid & (start + within == target), 1.0, 0.0))
        where = f32(lane)
        shared = bf16(jnp.where((where < used) & (tail + where == target), 1.0, 0.0))
        return grouped, shared[:, :SHARED]

    def key_bias(self):
        width = self.lane_counts.shape[2]
        within = f32(lax.broadcasted_iota(jnp.int32, (1, width), 1) % GROUP)
        parts = []
        for group in range(GROUPS):
            for z in range(len(self.free)):
                parts.append(jnp.where(self.lane_counts[z][0:1] > within + group * GROUP, 0.0, NEGATIVE))
        slot = f32(lax.broadcasted_iota(jnp.int32, (1, width), 1))
        for z in range(0, len(self.free), 2):
            low = self.tails[z][0:1] + self.used[z][0:1]
            high = self.tails[z + 1][0:1] + self.used[z + 1][0:1]
            limit = jnp.where(slot < TAIL, low, high + TAIL)
            parts.append(jnp.where(slot < limit, 0.0, NEGATIVE))
        return jnp.concatenate(parts, axis=1)


class Plane:
    def __init__(self):
        self.me = lax.axis_index("seq")
        self.level = lax.axis_index("ctx")
        self.sibling, self.left, self.down = flip(self.me, 1), flip(self.me, 2), flip(self.me, 4)
        self.across = flip(self.left, 4)

    def order(self, seat):
        core, x, y = lax.rem(seat, 2), lax.rem(seat // 2, 2), seat // 4
        return core * 4 + y * 2 + x


class Gather:
    def __init__(self, plane, halves, sems, at):
        self.plane, self.halves, self.sems, self.at = plane, halves, sems, at

    def moves(self):
        p = self.plane
        out = []
        for origin, half, place in (
            (p.me, None, p.left),
            (p.me, None, p.down),
            (p.me, None, p.sibling),
            (p.left, 0, p.down),
            (p.down, 1, p.left),
            (p.left, None, p.sibling),
            (p.down, None, p.sibling),
            (p.across, 0, p.sibling),
            (p.across, 1, p.sibling),
        ):
            out.append((self.halves(origin, half), place))
        return out

    def copy(self, move):
        ref, place = self.moves()[move]
        return remote(ref, ref, self.sems, (self.at, move), {"seq": place})

    def begin(self):
        for move in (0, 1, 2):
            self.copy(move).start()

    def forward(self):
        self.copy(0).wait_recv()
        self.copy(3).start()
        self.copy(5).start()
        self.copy(1).wait_recv()
        self.copy(4).start()
        self.copy(6).start()

    def finish(self):
        self.copy(3).wait_recv()
        self.copy(7).start()
        self.copy(4).wait_recv()
        self.copy(8).start()

    def arrive(self):
        for move in (2, 5, 6, 7, 8):
            self.copy(move).wait_recv()

    def drain(self):
        for move in range(9):
            self.copy(move).wait_send()


class BlockSum:
    def __init__(self, plane, source, first, second, third, result, sems):
        self.plane, self.sems = plane, sems
        self.source, self.first, self.second, self.third, self.result = source, first, second, third, result

    def block(self, seat, half):
        return 2 * (lax.rem(seat // 2, 2) + 2 * (seat // 4)) + half

    def copies(self):
        p = self.plane
        core = lax.rem(p.me, 2)
        out = [(self.source.at[pl.ds(8 * (1 - core), 8)], self.first, p.sibling)]
        mine = 8 * core
        out.append((self.source.at[mine + self.block(p.across, 0)], self.second.at[0], p.left))
        out.append((self.source.at[mine + self.block(p.left, 0)], self.second.at[1], p.left))
        out.append((self.source.at[mine + self.block(p.across, 1)], self.second.at[2], p.down))
        out.append((self.source.at[mine + self.block(p.down, 1)], self.second.at[3], p.down))
        out.append((self.source.at[mine + self.block(p.down, 0)], self.third.at[0], p.down))
        out.append((self.source.at[mine + self.block(p.left, 1)], self.third.at[1], p.left))
        return out

    def copy(self, at):
        src, dst, place = self.copies()[at]
        return remote(src, dst, self.sems, (at,), {"seq": place})

    def level_one(self):
        self.copy(0).start()

    def level_two(self):
        core = lax.rem(self.plane.me, 2)
        self.copy(0).wait_recv()
        for block in range(8):
            at = 8 * core + block
            self.source[at] = self.source[at] + self.first[block]
        for at in (1, 2, 3, 4):
            self.copy(at).start()

    def level_three(self):
        p = self.plane
        mine = 8 * lax.rem(p.me, 2)
        self.copy(1).wait_recv()
        at = mine + self.block(p.down, 0)
        self.source[at] = self.source[at] + self.second[0]
        self.copy(5).start()
        self.copy(3).wait_recv()
        at = mine + self.block(p.left, 1)
        self.source[at] = self.source[at] + self.second[2]
        self.copy(6).start()

    def total(self):
        p = self.plane
        mine = 8 * lax.rem(p.me, 2)
        self.copy(2).wait_recv()
        self.copy(5).wait_recv()
        first = self.source[mine + self.block(p.me, 0)]
        self.result[0] = first + self.second[1] + self.third[0]
        self.copy(4).wait_recv()
        self.copy(6).wait_recv()
        second = self.source[mine + self.block(p.me, 1)]
        self.result[1] = second + self.second[3] + self.third[1]

    def drain(self):
        for at in range(7):
            self.copy(at).wait_send()


class RowSum:
    def __init__(self, plane, given, mine, near, sums, from_left, from_down, last, passed, store, sems, at):
        self.plane, self.given, self.mine, self.near, self.sums = plane, given, mine, near, sums
        self.from_left, self.from_down, self.last, self.passed = from_left, from_down, last, passed
        self.store, self.sems, self.at = store, sems, at
        self.half = passed.shape[-1]

    def over(self, q):
        return remote(self.given(q), self.near.at[q], self.sems, (self.at, q), {"seq": self.plane.sibling})

    def far(self, which):
        low, high = pl.ds(0, self.half), pl.ds(self.half, self.half)
        left, down = self.plane.left, self.plane.down
        src, dst, to = (
            (self.sums.at[3, :, low], self.from_left.at[1], left),
            (self.sums.at[3, :, high], self.from_down.at[1], down),
            (self.sums.at[1, :, low], self.from_left.at[0], left),
            (self.sums.at[2, :, high], self.from_down.at[0], down),
            (self.passed.at[0], self.last.at[0], down),
            (self.passed.at[1], self.last.at[1], left),
        )[which]
        return remote(src, dst, self.sems, (self.at, 4 + which), {"seq": to})

    def begin(self):
        for q in (3, 1, 2, 0):
            self.over(q).start()

    def chip(self):
        for q in (3, 1, 2, 0):
            self.over(q).wait_recv()
            self.sums[q] = self.mine(q) + self.near[q]
            if q == 3:
                self.far(0).start()
                self.far(1).start()
            if q == 1:
                self.far(2).start()
            if q == 2:
                self.far(3).start()

    def relay(self):
        self.far(0).wait_recv()
        self.passed[0] = bf16(f32(self.sums[2, :, : self.half]) + f32(self.from_left[1]))
        self.far(4).start()
        self.far(1).wait_recv()
        self.passed[1] = bf16(f32(self.sums[1, :, self.half :]) + f32(self.from_down[1]))
        self.far(5).start()

    def end(self):
        self.far(2).wait_recv()
        self.far(4).wait_recv()
        self.store(0, bf16(f32(self.sums[0, :, : self.half]) + f32(self.from_left[0]) + f32(self.last[0])))
        self.far(3).wait_recv()
        self.far(5).wait_recv()
        self.store(1, bf16(f32(self.sums[0, :, self.half :]) + f32(self.from_down[0]) + f32(self.last[1])))

    def drain(self):
        for q in range(4):
            self.over(q).wait_send()
        for which in range(6):
            self.far(which).wait_send()


def counts_of(ref, seq_count, ctx_count):
    return f32(ref[...].reshape((seq_count * ctx_count,) + ref.shape[2:]))


def embedded_rows(tokens, waves, taxel, table):
    return bf16(tokens + waves + jnp.where(taxel, table[1:2], table[0:1]))


def encode(tokens, modality, keep, positions, frequency, modal_table, gain, bias, qkv_weight, out_weight, collective_id):
    seq_count, ctx_count = lax.axis_size("seq"), lax.axis_size("ctx")
    tok_rows, width = tokens.shape
    kinds, _, local_width = qkv_weight.shape
    head_width = local_width // ctx_count
    blocks = 16
    block_width = width // blocks
    plane_rows = seq_count * GROUP
    slots = ctx_count * (2 * plane_rows + TAIL)
    half_width = width // 2
    shared_rows = ctx_count * SHARED
    score_scale = 1.0 / math.sqrt(HEAD_DIM)
    early = 4
    early_width = width // early

    quarter = width // 4
    chips = seq_count // 2
    sets = GROUPS + 1

    def kernel(
        mod_ref, keep_ref, pos_ref, freq_ref, table_ref, gain_ref, bias_ref, tok_hbm, w_hbm, proj_hbm,
        out_hbm, emb_hbm, fits_ref,
        tok_ref, w_ref, proj_ref, emb_ref, cnt_ref, normed, opening, gathered, tail_own, tail_in, tail,
        shared_in, first, second, third, summed, crossed, shared, staged, qk_ref, v_ref, peak, running,
        attended, inward, shares, near, sums, from_left, from_down, last, passed, returned,
        tail_shares, tail_near, tail_sums, tail_left, tail_down, tail_last, tail_passed,
        ret_in, ret_first, ret_second, ret_third, final, out_ref,
        w_sems, cs, cr, gs, gr, bs, br, xs, xr, ds, dr,
        fs, fr, back_sems, ss, sr, rs, rr, ys, yr, ts, tr, out_sems,
    ):
        plane = Plane()
        me, level = plane.me, plane.level
        sibling, left, down = plane.sibling, plane.left, plane.down
        unpack = (((0,), (0,)), ((), ()))

        def fetch(kind):
            return pltpu.make_async_copy(w_hbm.at[kind], w_ref.at[kind], w_sems.at[kind])

        save_embedded = pltpu.make_async_copy(emb_ref, emb_hbm, w_sems.at[kinds + 2])
        fetch_tokens = pltpu.make_async_copy(tok_hbm, tok_ref, w_sems.at[kinds])
        fetch_projection = pltpu.make_async_copy(proj_hbm, proj_ref, w_sems.at[kinds + 1])

        def count_line(step):
            peer = lax.rem(level + step, ctx_count)
            ref = cnt_ref.at[me, level]
            return remote(ref, ref, (cs, cr), (step - 1,), {"ctx": peer})

        def count_plane(step):
            peer = lax.rem(me + step, seq_count)
            ref = cnt_ref.at[me]
            return remote(ref, ref, (cs, cr), (ctx_count - 2 + step,), {"seq": peer})

        def piece(group):
            def halves(origin, half):
                ref = gathered.at[group, origin]
                if half is None:
                    return ref
                return ref.at[:, pl.ds(half * half_width, half_width)]

            return halves

        def blocks_of(ref):
            def halves(origin, half):
                start = 2 * plane.order(origin)
                if half is None:
                    return ref.at[pl.ds(start, 2)]
                return ref.at[start + half]

            return halves

        def tail_piece(origin, half):
            start = lax.rem(origin, 2) * half_width + (half or 0) * quarter
            cols = pl.ds(pl.multiple_of(start, quarter), half_width if half is None else quarter)
            return tail.at[origin // 2, :, cols]

        groups = [Gather(plane, piece(g), (gs, gr), g) for g in range(GROUPS)]
        groups.append(Gather(plane, tail_piece, (gs, gr), GROUPS))
        spread = Gather(plane, blocks_of(shared), (gs, gr), GROUPS + 1)
        back_spread = Gather(plane, blocks_of(final), (gs, gr), GROUPS + 2)
        core = lax.rem(me, 2)
        my_half, other_half = aligned(core, half_width), aligned(1 - core, half_width)
        tail_swap = remote(tail_own.at[:, other_half], tail_in, (ts, tr), (0,), {"seq": sibling})
        tail_rows = pl.ds(BASE, GROUP)
        tail_result = returned.at[tail_rows, my_half]
        tail_back = remote(tail_result, tail_result, (ts, tr), (1,), {"seq": sibling})
        reduce_in = BlockSum(plane, shared_in, first, second, third, summed, (bs, br))

        def cross(step):
            peer = lax.rem(level + step, ctx_count)
            src = summed.at[:, aligned(peer, SHARED), :]
            return remote(src, crossed.at[step - 1], (xs, xr), (step - 1,), {"ctx": peer})

        def rows_of(group):
            return plane_rows if group < 2 else TAIL

        def slot_start(group, z):
            return pl.multiple_of(group * ctx_count * plane_rows + z * rows_of(group), GROUP)

        def dealt(kind, start, rows):
            here = pl.ds(pl.multiple_of(start, GROUP), rows)
            if kind == 2:
                return v_ref.at[here, pl.ds(0, head_width)]
            return qk_ref.at[kind, here]

        def deal(group, kind, step):
            peer = lax.rem(level + step, ctx_count)
            src = staged.at[group * kinds + kind, peer, pl.ds(0, rows_of(group))]
            at = (group * kinds + kind) * (ctx_count - 1) + step - 1
            return remote(src, dealt(kind, slot_start(group, level), rows_of(group)), (ds, dr), (at,), {"ctx": peer})

        def place(which_seat, which):
            seat = flip(which_seat, 2) if which % 2 else which_seat
            return flip(seat, 4) if which // 2 else seat

        def row_sum(g):
            def store(side, value):
                returned[g * GROUP : (g + 1) * GROUP, side * half_width : (side + 1) * half_width] = value

            return RowSum(
                plane, lambda q: shares.at[g, place(sibling, q)], lambda q: shares[g, place(me, q)], near.at[g],
                sums.at[g], from_left.at[g], from_down.at[g], last.at[g], passed.at[g], store, (ss, sr), g,
            )

        def store_tail(side, value):
            start = pl.multiple_of(core * half_width + side * quarter, quarter)
            returned[tail_rows, pl.ds(start, quarter)] = value

        row_sums = [row_sum(g) for g in range(GROUPS)]
        row_sums.append(
            RowSum(
                plane, lambda q: tail_shares.at[place(me, q) // 2, :, other_half],
                lambda q: tail_shares[place(me, q) // 2, :, my_half], tail_near,
                tail_sums, tail_left, tail_down, tail_last, tail_passed, store_tail, (ss, sr), GROUPS,
            )
        )

        def back(group, step):
            peer = lax.rem(level + step, ctx_count)
            src = attended.at[pl.ds(slot_start(group, peer), rows_of(group))]
            dst = inward.at[group, pl.ds(0, rows_of(group)), aligned(level, head_width)]
            return remote(src, dst, (fs, fr), (group * (ctx_count - 1) + step - 1,), {"ctx": peer})

        def back_own(group):
            src = attended.at[pl.ds(slot_start(group, level), rows_of(group))]
            dst = inward.at[group, pl.ds(0, rows_of(group)), aligned(level, head_width)]
            return pltpu.make_async_copy(src, dst, back_sems.at[group])

        own_start = 2 * plane.order(me)

        def cross_back(step):
            peer = lax.rem(level + step, ctx_count)
            ref = final.at[pl.ds(own_start, 2), aligned(level, SHARED), :]
            return remote(ref, ref, (ys, yr), (step - 1,), {"ctx": peer})

        class Result:
            def __setitem__(self, half, value):
                final[own_start + half, aligned(level, SHARED), :] = value

        reduce_back = BlockSum(plane, ret_in, ret_first, ret_second, ret_third, Result(), (rs, rr))

        fetch_tokens.start()
        barrier = pltpu.get_barrier_semaphore()
        for step in range(1, seq_count):
            peer = {"seq": lax.rem(me + step, seq_count)}
            pl.semaphore_signal(barrier, inc=1, device_id=peer, device_id_type=MESH)
        for step in range(1, ctx_count):
            peer = {"ctx": lax.rem(level + step, ctx_count)}
            pl.semaphore_signal(barrier, inc=1, device_id=peer, device_id_type=MESH)
        keep_row = f32(keep_ref[...])
        place_row, taxel_row = f32(pos_ref[...]), f32(mod_ref[...])
        own_count = jnp.sum(keep_row, axis=1, keepdims=True).astype(jnp.int32)
        cnt_ref[me, level] = jnp.broadcast_to(own_count, cnt_ref.shape[2:])
        rank_row = ranks_of(keep_row, tok_rows)
        slot = f32(lax.broadcasted_iota(jnp.int32, (BASE, tok_rows), 0))
        base_pick = jnp.where((keep_row > 0.0) & (rank_row == slot), 1.0, 0.0)
        base_choice = bf16(base_pick)

        opening_pick = base_pick[:GROUP]
        opening_place = jnp.sum(opening_pick * place_row, axis=1, keepdims=True)
        opening_taxel = jnp.sum(opening_pick * taxel_row, axis=1, keepdims=True) > 0.5
        total = jnp.zeros((GROUP, 1), jnp.float32)
        fetch_tokens.wait()
        for part in range(early // 2):
            waves = sine_and_cosine(opening_place * freq_ref[:, part * early_width : (part + 1) * early_width])
            for side in range(2):
                start = side * half_width + part * early_width
                cols = slice(start, start + early_width)
                rows = jnp.dot(base_choice[:GROUP], tok_ref[:, cols], preferred_element_type=jnp.float32)
                rounded = embedded_rows(rows, waves[side], opening_taxel, table_ref[:, cols])
                opening[:, cols] = rounded
                total = total + jnp.sum(f32(rounded), axis=1, keepdims=True)
        mean = total * (1.0 / width)
        total = jnp.zeros((GROUP, 1), jnp.float32)
        for part in range(early):
            centered = f32(opening[:, part * early_width : (part + 1) * early_width]) - mean
            total = total + jnp.sum(centered * centered, axis=1, keepdims=True)
        scale = lax.rsqrt(total * (1.0 / width) + EPSILON)
        for part in range(early):
            cols = slice(part * early_width, (part + 1) * early_width)
            gathered[0, me, :, cols] = bf16((f32(opening[:, cols]) - mean) * scale * gain_ref[:, cols] + bias_ref[:, cols])
        pl.semaphore_wait(barrier, seq_count + ctx_count - 2)
        groups[0].begin()
        for step in range(1, ctx_count):
            count_line(step).start()

        def project(rows, kind):
            return bf16(jnp.dot(rows, w_ref[kind], preferred_element_type=jnp.float32))

        def send(group, kind, values):
            rows = rows_of(group)
            for z in range(ctx_count):
                staged[group * kinds + kind, z, :rows] = values[:, z * head_width : (z + 1) * head_width]
            dealt(kind, slot_start(group, level), rows)[...] = staged[group * kinds + kind, level, :rows]
            for step in (2, 3, 1):
                deal(group, kind, step).start()

        for kind in (1, 2, 0):
            fetch(kind).start()
        fetch_projection.start()
        v_ref[:, head_width:] = jnp.ones((slots, head_width), jnp.bfloat16)

        place_column = as_column(place_row, tok_rows)
        taxel = as_column(taxel_row, tok_rows) > 0.5

        def embed_block(at, total):
            waves = sine_and_cosine(place_column * freq_ref[:, aligned(at, block_width)])
            for side in range(2):
                start = side * half_width + at * block_width
                cols = pl.ds(pl.multiple_of(start, block_width), block_width)
                rounded = embedded_rows(f32(tok_ref[:, cols]), waves[side], taxel, table_ref[:, cols])
                emb_ref[:, cols] = rounded
                values = f32(rounded)
                for lane in range(0, block_width, 128):
                    total = total + values[:, lane : lane + 128]
            return total

        nothing = jnp.zeros((tok_rows, 128), jnp.float32)
        total = lax.fori_loop(0, blocks // 2, embed_block, nothing)
        mean = jnp.sum(total, axis=1, keepdims=True) * (1.0 / width)
        for step in range(1, ctx_count):
            count_line(step).wait_recv()
        for step in range(1, seq_count):
            count_plane(step).start()
        groups[0].forward()

        def var_block(at, total):
            centered = f32(emb_ref[:, aligned(at, block_width)]) - mean
            centered = centered * centered
            for lane in range(0, block_width, 128):
                total = total + centered[:, lane : lane + 128]
            return total

        total = lax.fori_loop(0, blocks, var_block, nothing)
        scale = lax.rsqrt(jnp.sum(total, axis=1, keepdims=True) * (1.0 / width) + EPSILON)

        def norm_block(at, carry):
            cols = aligned(at, block_width)
            values = (f32(emb_ref[:, cols]) - mean) * scale * gain_ref[:, cols] + bias_ref[:, cols]
            rows = bf16(values)
            normed[:, cols] = rows
            gathered[1, me, :, cols] = moved(base_choice[GROUP:], rows)
            return carry

        lax.fori_loop(0, blocks, norm_block, 0)
        groups[1].begin()
        groups[0].finish()
        save_embedded.start()
        groups[0].arrive()
        opening_rows = gathered[0].reshape(plane_rows, width)
        fetch(1).wait()
        send(0, 1, project(opening_rows, 1))
        for step in range(1, seq_count):
            count_plane(step).wait_recv()
        layout = Layout(counts_of(cnt_ref, seq_count, ctx_count), me * ctx_count + level, level, seq_count, ctx_count)
        fits_ref[0] = jnp.max(layout.fits).astype(jnp.int32)
        slot = f32(lax.broadcasted_iota(jnp.int32, (shared_rows, tok_rows), 0))
        shared_choice = bf16(jnp.where(layout.shared_slots(keep_row, rank_row) == slot, 1.0, 0.0))
        slot = f32(lax.broadcasted_iota(jnp.int32, (GROUP, tok_rows), 0))
        tail_choice = bf16(jnp.where(layout.tail_slots(keep_row, rank_row) == slot, 1.0, 0.0))
        both_choice = jnp.concatenate([shared_choice, tail_choice], axis=0)
        for block in range(blocks):
            cols = slice(block * block_width, (block + 1) * block_width)
            rows = moved(both_choice, normed[:, cols])
            shared_in[block] = rows[:shared_rows]
            tail_own[:, cols] = rows[shared_rows:]
        reduce_in.level_one()
        tail_swap.start()

        reduce_in.level_two()
        groups[1].forward()
        fetch(2).wait()
        send(0, 2, project(opening_rows, 2))
        fetch(0).wait()
        send(0, 0, project(opening_rows, 0))
        tail_swap.wait_recv()
        tail[me // 2, :, my_half] = tail_own[:, my_half] + tail_in[...]
        groups[1].finish()
        reduce_in.level_three()
        groups[2].begin()
        groups[1].arrive()
        group_rows = gathered[1].reshape(plane_rows, width)
        send(1, 1, project(group_rows, 1))
        reduce_in.total()
        for step in range(1, ctx_count):
            cross(step).start()
        groups[2].forward()
        value_rows = project(group_rows, 2)
        groups[2].finish()
        for step in range(1, ctx_count):
            cross(step).wait_recv()
        own = summed[:, aligned(level, SHARED), :]
        shared[pl.ds(own_start, 2)] = own + crossed[0] + crossed[1] + crossed[2]
        spread.begin()
        send(1, 2, value_rows)
        send(1, 0, project(group_rows, 0))
        grouped_choice, shared_choice = layout.tail_choice(level)
        key_bias = layout.key_bias()
        spread.forward()
        groups[2].arrive()
        spread.finish()
        spread.arrive()
        tail_count = chips * GROUP
        held_tail = tail[...].reshape(tail_count, width)
        for kind in (0, 1, 2):
            total = jnp.zeros((tail_count + SHARED, local_width), jnp.float32)
            for block in range(blocks):
                cols = slice(block * block_width, (block + 1) * block_width)
                rows = jnp.concatenate([held_tail[:, cols], shared[block]], axis=0)
                total = total + jnp.dot(rows, w_ref[kind, cols, :], preferred_element_type=jnp.float32)
            rows = bf16(total)
            packed = jnp.dot(grouped_choice[:, :tail_count], rows[:tail_count], preferred_element_type=jnp.float32)
            packed = packed + jnp.dot(shared_choice, rows[tail_count:], preferred_element_type=jnp.float32)
            send(2, kind, bf16(packed))

        def dealt_in(group, kind):
            for step in range(1, ctx_count):
                deal(group, kind, step).wait_recv()

        first_keys = GROUPS * ctx_count * plane_rows
        factor = score_scale * math.log2(math.e)

        def scores_of(begin, rows, low, high):
            scores = lax.dot_general(
                qk_ref[0, pl.ds(begin, rows)], qk_ref[1, low:high], (((1,), (1,)), ((), ())),
                preferred_element_type=jnp.float32,
            )
            return scores * factor + key_bias[:, low:high]

        def weigh(scores, top, low, high):
            weights = bf16(jnp.exp2(scores - top))
            return jnp.dot(weights, v_ref[low:high], preferred_element_type=jnp.float32)

        def finish_rows(begin, rows, both):
            attended[pl.ds(begin, rows)] = bf16(both[:, :head_width] / both[:, head_width:])

        def attend_early(begin, rows):
            scores = scores_of(begin, rows, 0, first_keys)
            top = jnp.max(scores, axis=1, keepdims=True)
            peak[pl.ds(begin, rows)] = jnp.broadcast_to(top, (rows, 128))
            running[pl.ds(begin, rows)] = weigh(scores, top, 0, first_keys)

        def attend_late(begin, rows):
            scores = scores_of(begin, rows, first_keys, slots)
            before = peak[pl.ds(begin, rows)][:, :1]
            top = jnp.maximum(before, jnp.max(scores, axis=1, keepdims=True))
            both = running[pl.ds(begin, rows)] * jnp.exp2(before - top)
            finish_rows(begin, rows, both + weigh(scores, top, first_keys, slots))

        def send_back(group):
            for step in (2, 3, 1):
                back(group, step).start()
            back_own(group).start()

        def collect(group):
            back_own(group).wait()
            for step in range(1, ctx_count):
                back(group, step).wait_recv()

        span = ctx_count * plane_rows // 2
        for group in range(GROUPS):
            dealt_in(group, 1)
            dealt_in(group, 2)
        for group in range(GROUPS):
            dealt_in(group, 0)
            attend_early(2 * group * span, span)
            attend_early((2 * group + 1) * span, span)
        dealt_in(GROUPS, 0)
        attend_early(first_keys, ctx_count * TAIL)
        dealt_in(GROUPS, 1)
        dealt_in(GROUPS, 2)
        attend_late(first_keys, ctx_count * TAIL)
        send_back(2)
        for group in range(GROUPS):
            attend_late(2 * group * span, span)
            attend_late((2 * group + 1) * span, span)
            if group == 0:
                send_back(group)
        fetch_projection.wait()
        collect(2)
        packed = inward[2, :TAIL]
        grouped = bf16(lax.dot_general(grouped_choice, packed, unpack, preferred_element_type=jnp.float32))
        extra = bf16(lax.dot_general(shared_choice, packed, unpack, preferred_element_type=jnp.float32))
        rows = jnp.concatenate([grouped[:tail_count], extra], axis=0)
        for block in range(blocks):
            cols = slice(block * block_width, (block + 1) * block_width)
            values = bf16(jnp.dot(rows, proj_ref[:, cols], preferred_element_type=jnp.float32))
            tail_shares[:, :, cols] = values[:tail_count].reshape(chips, GROUP, block_width)
            ret_in[block] = values[tail_count:]
        reduce_back.level_one()
        row_sums[2].begin()
        reduce_back.level_two()
        row_sums[2].chip()
        reduce_back.level_three()

        def project_back(g):
            for block in range(blocks):
                cols = slice(block * block_width, (block + 1) * block_width)
                values = moved(inward[g], proj_ref[:, cols])
                shares[g, :, :, cols] = values.reshape(seq_count, GROUP, block_width)

        collect(0)
        send_back(1)
        project_back(0)
        row_sums[0].begin()
        reduce_back.total()
        for step in range(1, ctx_count):
            cross_back(step).start()
        row_sums[2].relay()
        row_sums[0].chip()
        collect(1)
        for step in range(1, ctx_count):
            cross_back(step).wait_recv()
        back_spread.begin()
        project_back(1)
        row_sums[1].begin()
        row_sums[0].relay()
        row_sums[1].chip()
        row_sums[2].end()
        tail_back.start()
        back_spread.forward()
        row_sums[1].relay()
        row_sums[0].end()
        back_spread.finish()
        slot = f32(lax.broadcasted_iota(jnp.int32, (shared_rows, tok_rows), 0))
        from_shared = bf16(jnp.where(layout.shared_slots(keep_row, rank_row) == slot, 1.0, 0.0))
        from_rows = jnp.concatenate([base_choice, tail_choice], axis=0)
        tail_back.wait_recv()
        back_spread.arrive()
        row_sums[1].end()

        def deliver(part):
            cols = pl.ds(part * early_width, early_width)
            return pltpu.make_async_copy(out_ref.at[:, cols], out_hbm.at[:, cols], out_sems.at[part])

        for block in range(blocks):
            cols = slice(block * block_width, (block + 1) * block_width)
            placed = lax.dot_general(from_shared, final[block], unpack, preferred_element_type=jnp.float32)
            placed = placed + lax.dot_general(
                from_rows, returned[:, cols], unpack, preferred_element_type=jnp.float32
            )
            out_ref[:, cols] = bf16(placed)
            if (block + 1) % (blocks // early) == 0:
                deliver(block // (blocks // early)).start()
        save_embedded.wait()
        for part in range(early):
            deliver(part).wait()
        for g in range(sets):
            for kind in range(kinds):
                for step in range(1, ctx_count):
                    deal(g, kind, step).wait_send()
            row_sums[g].drain()
            for step in range(1, ctx_count):
                back(g, step).wait_send()
        tail_swap.wait_send()
        tail_back.wait_send()
        for step in range(1, ctx_count):
            count_line(step).wait_send()
            cross(step).wait_send()
            cross_back(step).wait_send()
        for step in range(1, seq_count):
            count_plane(step).wait_send()
        for gather in groups + [spread, back_spread]:
            gather.drain()
        reduce_in.drain()
        reduce_back.drain()

    dma = pltpu.SemaphoreType.DMA
    b16 = jnp.bfloat16
    vmem = pl.BlockSpec(memory_space=pltpu.VMEM)
    anywhere = pl.BlockSpec(memory_space=pl.ANY)

    def held(*shape):
        return pltpu.VMEM(shape, b16)

    def pair(*shape):
        return [dma(shape)] * 2

    return pl.pallas_call(
        kernel,
        out_shape=[jax.ShapeDtypeStruct((tok_rows, width), b16)] * 2 + [jax.ShapeDtypeStruct((1,), jnp.int32)],
        in_specs=[vmem] * 7 + [anywhere] * 3,
        out_specs=[anywhere, anywhere, pl.BlockSpec(memory_space=pltpu.SMEM)],
        scratch_shapes=[
            held(tok_rows, width),
            held(*qkv_weight.shape),
            held(*out_weight.shape),
            held(tok_rows, width),
            pltpu.VMEM((seq_count, ctx_count, 8, 128), jnp.int32),
            held(tok_rows, width),
            held(GROUP, width),
            held(GROUPS, seq_count, GROUP, width),
            held(GROUP, width),
            held(GROUP, half_width),
            held(chips, GROUP, width),
            held(blocks, shared_rows, block_width),
            held(8, shared_rows, block_width),
            held(4, shared_rows, block_width),
            held(2, shared_rows, block_width),
            held(2, shared_rows, block_width),
            held(ctx_count - 1, 2, SHARED, block_width),
            held(blocks, SHARED, block_width),
            held(sets * kinds, ctx_count, plane_rows, head_width),
            held(2, slots, head_width),
            held(slots, 2 * head_width),
            pltpu.VMEM((slots, 128), jnp.float32),
            pltpu.VMEM((slots, 2 * head_width), jnp.float32),
            held(slots, head_width),
            held(sets, plane_rows, local_width),
            held(GROUPS, seq_count, GROUP, width),
            held(GROUPS, 4, GROUP, width),
            held(GROUPS, 4, GROUP, width),
        ]
        + [held(GROUPS, 2, GROUP, half_width)] * 4
        + [
            held(BASE + GROUP, width),
            held(chips, GROUP, width),
            held(4, GROUP, half_width),
            held(4, GROUP, half_width),
        ]
        + [held(2, GROUP, quarter)] * 4
        + [
            held(blocks, SHARED, block_width),
            held(8, SHARED, block_width),
            held(4, SHARED, block_width),
            held(2, SHARED, block_width),
            held(blocks, shared_rows, block_width),
            held(tok_rows, width),
        ]
        + [dma((kinds + 3,))]
        + pair(seq_count + ctx_count - 2)
        + pair(sets + 2, 9)
        + pair(7)
        + pair(ctx_count - 1)
        + pair(sets * kinds * (ctx_count - 1))
        + pair(sets * (ctx_count - 1))
        + [dma((sets,))]
        + pair(sets, 10)
        + pair(7)
        + pair(ctx_count - 1)
        + pair(2)
        + [dma((early,))],
        compiler_params=pltpu.CompilerParams(
            collective_id=collective_id, has_side_effects=True, vmem_limit_bytes=60 * 2**20
        ),
    )(modality, keep, positions, frequency, modal_table, gain, bias, tokens, qkv_weight, out_weight)


def local(
    tokens,
    modality,
    keep_mask,
    positions,
    modal_table,
    norm_gain,
    norm_bias,
    qkv_weight,
    out_weight,
    mask_token,
):
    arguments = (
        tokens, modality, keep_mask, positions, modal_table, norm_gain, norm_bias, qkv_weight, out_weight, mask_token,
    )
    seq_count, ctx_count = lax.axis_size("seq"), lax.axis_size("ctx")
    tok_rows, width = tokens.shape
    local_width = qkv_weight.shape[2]
    shaped = seq_count == 8 and ctx_count == 4 and tok_rows == 128 and width % 4096 == 0
    shaped = shaped and local_width == ctx_count * HEAD_DIM
    if shaped:
        half_width = width // 2
        exponents = np.arange(half_width, dtype=np.float64) / half_width
        frequency = jnp.asarray(np.exp(-math.log(10000.0) * exponents).astype(np.float32))[None]
        *done, fits = encode(
            tokens, modality[None], keep_mask[None], positions[None], frequency, modal_table,
            norm_gain[None], norm_bias[None], qkv_weight, out_weight, 11,
        )
        restored, embedded = lax.cond(fits[0] == 1, lambda done, *given: done, lambda done, *given: general(*given), done, *arguments)
        restored, embedded = lax.optimization_barrier((restored, embedded))
    else:
        restored, embedded = general(*arguments)
    return jnp.where((keep_mask == 1)[:, None], f32(embedded) + f32(restored), mask_token[None, :])


def solution(mesh):
    in_specs = (
        P(("seq", "ctx"), None),
        P(("seq", "ctx")),
        P(("seq", "ctx")),
        P(("seq", "ctx")),
        P(),
        P(),
        P(),
        P(None, None, "seq"),
        P("seq", None),
        P(),
    )
    out_specs = P(("seq", "ctx"), None)
    return jax.shard_map(local, mesh=mesh, in_specs=in_specs, out_specs=out_specs, check_vma=False)
```
